32 devices in a mesh: ep: 8 (over z, x), tp: 4 (over y, core).
Axes of the slice: x: 2, y: 2, z: 4, core: 2. Of those that a mesh axis runs over, the one named last changes fastest.
Arguments:
- tokens: bfloat16 [16384, 768], P(('ep', 'tp')), may hold values from -6 to 6
- d_out: bfloat16 [16384, 768], P(('ep', 'tp')), may hold values from -6 to 6
- segment: int32 [16384], P(('ep', 'tp')), may hold values from -1 to 15, as said below
- route: int32 [16384, 1], P(('ep', 'tp')), may hold values from 0 to 15; in each aligned block of 512 rows (0 to 511, 512 to 1023, ...) at most 48 rows name the same one
- gain_one: bfloat16 [768], replicated, may hold values from 0.5 to 1.5
- w_in: bfloat16 [768, 3072], replicated, may hold values from -0.21875 to 0.21875
- conv_w: bfloat16 [4, 1536], replicated, may hold values from -3 to 3
- conv_b: bfloat16 [1536], replicated, may hold values from -3 to 3
- w_x: bfloat16 [1536, 80], replicated, may hold values from -0.15625 to 0.15625
- w_dt: bfloat16 [48, 1536], replicated, may hold values from -0.875 to 0.875
- b_dt: bfloat16 [1536], replicated, may hold values from -6 to -2
- a_log: bfloat16 [16, 1536], replicated, may hold values from 0 to 2.765625
- d_skip: bfloat16 [1536], replicated, may hold values from 0.5 to 1.5
- w_out: bfloat16 [1536, 768], replicated, may hold values from -0.15625 to 0.15625
- gain_two: bfloat16 [768], replicated, may hold values from 0.5 to 1.5
- w_router: bfloat16 [768, 16], replicated, may hold values from -0.15625 to 0.15625
- w_up: bfloat16 [16, 768, 3072], P('ep', None, 'tp'), may hold values from -0.21875 to 0.21875
- w_down: bfloat16 [16, 3072, 768], P('ep', 'tp'), may hold values from -1.75 to 1.75
Outputs:
- block_out: bfloat16 [16384, 768], P(('ep', 'tp'))
- d_tokens: float32 [16384, 768], P(('ep', 'tp'))
- counts: int32 [2, 16], replicated
- g_gain_one: float32 [768], replicated
- g_w_in: float32 [768, 3072], replicated
- g_conv_w: float32 [4, 1536], replicated
- g_conv_b: float32 [1536], replicated
- g_w_x: float32 [1536, 80], replicated
- g_w_dt: float32 [48, 1536], replicated
- g_b_dt: float32 [1536], replicated
- g_a_log: float32 [16, 1536], replicated
- g_d_skip: float32 [1536], replicated
- g_w_out: float32 [1536, 768], replicated
- g_gain_two: float32 [768], replicated
- g_w_router: float32 [768, 16], replicated
- g_w_up: float32 [16, 768, 3072], P('ep', None, 'tp')
- g_w_down: float32 [16, 3072, 768], P('ep', 'tp')
The draws below stay inside these ranges and needn't reach their ends.
Inputs may be any that keep to these rules, and one draw needn't show every extreme that they name: `segment`: in each device's block of 512 tokens the samples are numbered 0, 1, 2 in order up to at most 15, each a run of consecutive positions beginning with the block's first position; padding tokens (-1) follow the last sample. No sample crosses a block. In every draw some block holds one sample of all 512 tokens, and some block reaches the largest number. `route`: within the tokens of one device, no expert is named by more than 48 tokens, padding included; some device reaches 48 for some expert.
All inputs are finite; a program needn't handle non-finite values.
Results may differ from the reference program's by a relative error of at most 0.0092.
Values may be sent and summed in bfloat16 or wider, within the bound.
A program may use at most 576 MiB of HBM per device.

```python
import math
from functools import partial
import jax
import jax.numpy as jnp
import numpy as np
from jax import lax

D = 768
DI = 1536
STATE = 16
DT_RANK = 48
CONV = 4
FF = 3072
TOK_DEV = 512
EXPERTS = 16
TOKENS = 16384
SLOT = 48
CAPACITY = 1280


def draw_segment(key, part):
    blocks = TOKENS // TOK_DEV
    key_start, key_kind, key_pad = jax.random.split(jax.random.fold_in(key, 11), 3)
    places = jnp.arange(TOK_DEV, dtype=jnp.int32)[None, :]
    kind = jax.random.randint(key_kind, (blocks, 1), 0, 2)
    spacing = jnp.where(kind == 1, 24, 160).astype(jnp.int32)
    starts = jax.random.randint(key_start, (blocks, TOK_DEV), 0, 1 << 20) % spacing == 0
    first_row = (jnp.arange(blocks, dtype=jnp.int32) == 0)[:, None]
    last_row = (jnp.arange(blocks, dtype=jnp.int32) == blocks - 1)[:, None]
    starts = starts | last_row & (places % 16 == 0)
    starts = jnp.where(first_row, places == 0, starts | (places == 0))
    numbers = jnp.cumsum(starts.astype(jnp.int32), axis=1) - 1
    numbers = jnp.minimum(numbers, TOK_DEV // 32 - 1)
    pads = jax.random.randint(key_pad, (blocks, 1), 0, TOK_DEV // 16 + 1)
    pads = jnp.where(first_row | last_row, 0, pads)
    numbers = jnp.where(places >= TOK_DEV - pads, -1, numbers)
    return numbers.reshape(TOKENS).astype(jnp.int32)


def block_levels(key, shape, cuts, smallest, largest):
    def one(position, shards_of):
        draws = jax.random.uniform(jax.random.fold_in(jax.random.fold_in(key, 6), position), (shards_of,), jnp.float32, smallest / len(cuts), largest / len(cuts))
        return jnp.repeat(jnp.exp(draws), shape[position] // shards_of).reshape((-1,) + (1,) * (len(shape) - position - 1))

    loudness = one(*cuts[0])
    for cut in cuts[1:]:
        loudness = loudness * one(*cut)
    return loudness


def deal_out(stream_key, own, number, rows, amount, top, bound, skew):
    sequence = jax.random.permutation(stream_key, amount)
    packed, usual = load_shares(amount, rows * top, bound, skew, True), load_shares(amount, rows * top, bound, skew, False)
    places = jnp.arange(amount)

    def named(tallies, offset_by):
        used = int((tallies > 0).sum())
        fixed = max(1, used // 4)
        passed = fixed + (places - fixed + offset_by * (used - fixed)) % max(1, amount - fixed)
        return jnp.zeros((amount,), jnp.int32).at[sequence[jnp.where(places < fixed, places, passed)]].set(jnp.asarray(tallies, jnp.int32))

    tallies = jnp.where(number % 4 == 0, named(packed, number // 4), named(usual, number - number // 4 - 1))
    mixed = jax.random.permutation(jax.random.fold_in(own, 3), amount)
    donor, taker = mixed[0:amount // 2 * 2:2], mixed[1:amount // 2 * 2:2]
    slack = jnp.minimum(tallies[donor] - 1, bound - tallies[taker]) // 2
    slack = jnp.where((donor == sequence[0]) | (taker == sequence[0]) | (tallies[taker] == 0), 0, jnp.maximum(slack, 0))
    passed = jax.random.randint(jax.random.fold_in(own, 4), (amount // 2,), 0, 1 << 20) % (slack + 1)
    tallies = tallies.at[donor].add(-passed).at[taker].add(passed)
    labels = jnp.searchsorted(jnp.cumsum(tallies), jnp.arange(rows * top), side="right").astype(jnp.int32)
    grid = labels.reshape(top, rows).T
    grid = grid[jax.random.permutation(jax.random.fold_in(own, 1), rows)]
    offset_by = jax.random.randint(jax.random.fold_in(own, 2), (rows, 1), 0, top)
    return jnp.take_along_axis(grid, (jnp.arange(top)[None, :] + offset_by) % top, axis=1)


def load_shares(count, total, bound, slope, full):
    portions = [(1 << 20) // math.isqrt(standing ** slope) + 1 for standing in range(1, count + 1)]
    largest = bound if full else min(bound, max(-(-total // count), total * portions[0] // sum(portions)))
    least = 1 if total - largest >= count - 1 else 0
    given, spare = [largest] + [least] * (count - 1), total - largest - least * (count - 1)
    while spare > 0:
        candidates = [i for i in range(1, count) if given[i] < largest] or [i for i in range(1, count) if given[i] < bound]
        mass, remaining = sum([portions[i] for i in candidates]), spare
        for i in candidates:
            extra = min(bound - given[i], max(1, remaining * portions[i] // mass), spare)
            given[i] = given[i] + extra
            spare = spare - extra
    return np.array(given)


def gaussian(own_key, dims, deviation, limit, cuts=(), held_as=jnp.bfloat16):
    values = jax.random.normal(own_key, dims, jnp.float32) * deviation
    if len(cuts) > 0:
        values = block_levels(own_key, dims, cuts, -0.22, 0.18) * values
    return jnp.clip(values, min=-limit, max=limit).astype(held_as)


def setup_inputs(seed: int = 0) -> dict:
    key_list = jax.random.split(jax.random.key(seed), 19)
    tokens = gaussian(key_list[0], (TOKENS, D), 1.0, 6.0, ((0, 32),))
    d_out = gaussian(key_list[1], (TOKENS, D), 1.0, 6.0, ((0, 32),))
    segment = draw_segment(jax.random.fold_in(key_list[18], 71), 0)
    route_keys = jax.random.split(jax.random.fold_in(key_list[3], 1), TOKENS // TOK_DEV)
    route_turns = jax.random.permutation(jax.random.fold_in(key_list[3], 3), TOKENS // TOK_DEV)
    route = jax.vmap(lambda own, number: deal_out(jax.random.fold_in(key_list[3], 2), own, number, TOK_DEV, EXPERTS, 1, SLOT, 2))(route_keys, route_turns).reshape((TOKENS, 1))
    gain_one = jnp.clip(1.0 + 0.1 * jax.random.normal(key_list[4], (D,), jnp.float32), 0.5, 1.5).astype(jnp.bfloat16)
    w_in = gaussian(key_list[5], (D, 2 * DI), D ** -0.5, 0.21875)
    conv_w = gaussian(key_list[6], (CONV, DI), 0.5, 3.0)
    conv_b = gaussian(key_list[7], (DI,), 0.5, 3.0)
    w_x = gaussian(key_list[8], (DI, DT_RANK + 2 * STATE), DI ** -0.5, 0.15625)
    w_dt = gaussian(key_list[9], (DT_RANK, DI), DT_RANK ** -0.5, 0.875)
    b_dt = jnp.clip(jax.random.uniform(key_list[10], (DI,), jnp.float32, -6.0, -2.0), -6.0, -2.0).astype(jnp.bfloat16)
    a_log = jnp.clip(jax.random.uniform(key_list[11], (STATE, DI), jnp.float32, 0.0, 2.765625), 0.0, 2.765625).astype(jnp.bfloat16)
    d_skip = jnp.clip(jax.random.uniform(key_list[12], (DI,), jnp.float32, 0.5, 1.5), 0.5, 1.5).astype(jnp.bfloat16)
    w_out = gaussian(key_list[13], (DI, D), DI ** -0.5, 0.15625)
    gain_two = jnp.clip(1.0 + 0.1 * jax.random.normal(key_list[14], (D,), jnp.float32), 0.5, 1.5).astype(jnp.bfloat16)
    w_router = gaussian(key_list[15], (D, EXPERTS), (2 * D) ** -0.5, 0.15625)
    w_up = gaussian(key_list[16], (EXPERTS, D, FF), D ** -0.5, 0.21875, ((0, 8), (2, 4)))
    w_down = gaussian(key_list[17], (EXPERTS, FF, D), (max(1, FF // (EXPERTS * EXPERTS))) ** -0.5, 1.75, ((0, 8), (1, 4)))
    return {"tokens": tokens, "d_out": d_out, "segment": segment, "route": route, "gain_one": gain_one, "w_in": w_in, "conv_w": conv_w, "conv_b": conv_b, "w_x": w_x, "w_dt": w_dt, "b_dt": b_dt, "a_log": a_log, "d_skip": d_skip, "w_out": w_out, "gain_two": gain_two, "w_router": w_router, "w_up": w_up, "w_down": w_down}


EPS = 1e-06
HIGH = lax.Precision.HIGHEST

@jax.custom_vjp
def low(v):
    return lax.optimization_barrier(v.astype(jnp.bfloat16)).astype(jnp.float32)

@jax.custom_vjp
def low_back(v):
    return v

def low_keep(v):
    return (low(v), None)

def low_pass(kept, grad):
    return (grad,)

def back_keep(v):
    return (v, None)

def back_low(kept, grad):
    return (low(grad),)
low.defvjp(low_keep, low_pass)
low_back.defvjp(back_keep, back_low)

def rms_scale(values, gain):
    return values * lax.rsqrt(lax.optimization_barrier(jnp.mean(values * values, axis=-1, keepdims=True)) + EPS) * gain

def sample_masks(segment):
    length = segment.shape[0]
    masks = []
    for shift in range(CONV):
        earlier = jnp.concatenate([jnp.full((shift,), -2, jnp.int32), segment[:length - shift]])
        masks.append((earlier == segment).astype(jnp.float32)[:, None])
    return masks

def causal_conv(inner, conv_w, conv_b, masks):
    length = inner.shape[0]
    total = conv_b[None, :] + conv_w[CONV - 1][None, :] * inner
    for shift in range(1, CONV):
        moved = jnp.concatenate([jnp.zeros((shift, inner.shape[1]), jnp.float32), inner[:length - shift]], axis=0)
        total = total + conv_w[CONV - 1 - shift][None, :] * moved * masks[shift]
    return total

def mixer(block_tokens, segment, gain_one, w_in, conv_w, conv_b, w_x, w_dt, b_dt, a_log, d_skip, w_out):
    normed = low(rms_scale(block_tokens, gain_one))
    both = low_back(jnp.dot(normed, w_in, precision=HIGH))
    inner = both[:, :DI]
    gate_z = both[:, DI:]
    masks = sample_masks(segment)
    conv = jax.nn.silu(causal_conv(inner, conv_w, conv_b, masks))
    proj = jnp.dot(conv, w_x, precision=HIGH)
    step = jax.nn.softplus(jnp.dot(proj[:, :DT_RANK], w_dt, precision=HIGH) + b_dt)
    in_b = proj[:, DT_RANK:DT_RANK + STATE]
    out_c = proj[:, DT_RANK + STATE:]
    rates = -jnp.exp(a_log)
    keep = masks[1][:, 0]

    def advance(state, item):
        step_t, inb_t, outc_t, conv_t, keep_t = item
        state = keep_t * jnp.exp(step_t[None, :] * rates) * state + inb_t[:, None] * (step_t * conv_t)[None, :]
        return (state, lax.optimization_barrier(jnp.sum(outc_t[:, None] * state, axis=0)))
    _, ssm_out = lax.scan(advance, jnp.zeros((STATE, DI), jnp.float32), (step, in_b, out_c, conv, keep))
    result = ssm_out + d_skip * conv
    gated = low(result * jax.nn.silu(gate_z))
    return low_back(jnp.dot(gated, w_out, precision=HIGH))

def expert_apply(item):
    slot_rows, up_weight, down_weight = item
    hidden_pre = low_back(jnp.dot(slot_rows, up_weight, precision=HIGH))
    hidden = low(jax.nn.gelu(hidden_pre, approximate=False))
    return jnp.dot(hidden, down_weight, precision=HIGH)

def routing(segment, route):
    choice_one = route[:, 0]
    picks = ((choice_one[:, None] == jnp.arange(EXPERTS, dtype=jnp.int32)[None, :]) & (segment >= 0)[:, None]).astype(jnp.int32)
    rank = lax.optimization_barrier(jnp.sum(jnp.cumsum(picks, axis=0) * picks, axis=1)) - 1
    kept = (segment >= 0) & (rank < CAPACITY)
    place = jnp.where(kept, rank, CAPACITY).astype(jnp.int32)
    return (choice_one, picks, kept, place)

def forward(tokens, gain_one, w_in, conv_w, conv_b, w_x, w_dt, b_dt, a_log, d_skip, w_out, gain_two, w_router, w_up, w_down, segment=None, route=None):
    blocks = TOKENS // TOK_DEV

    def one_block(item):
        return mixer(item[0], item[1], gain_one, w_in, conv_w, conv_b, w_x, w_dt, b_dt, a_log, d_skip, w_out)
    mixed = lax.map(jax.checkpoint(one_block), (tokens.reshape(blocks, TOK_DEV, D), segment.reshape(blocks, TOK_DEV)))
    valid = (segment >= 0).astype(jnp.float32)[:, None]
    after_mix = tokens + mixed.reshape(TOKENS, D) * valid
    normed = rms_scale(after_mix, gain_two)
    probs = jax.nn.softmax(jnp.dot(normed, w_router, precision=HIGH), axis=-1)
    choice_one, picks, kept, place = routing(segment, route)
    gate = lax.optimization_barrier(jnp.sum(probs * picks.astype(jnp.float32), axis=-1))
    table = jnp.zeros((EXPERTS, CAPACITY), jnp.int32).at[choice_one, place].set(jnp.arange(TOKENS, dtype=jnp.int32), mode='drop')
    filled = jnp.zeros((EXPERTS, CAPACITY), jnp.float32).at[choice_one, place].set(1.0, mode='drop')
    expert_in = low_back(low(normed))
    slot_rows = expert_in[table] * filled[:, :, None]
    outputs = lax.map(jax.checkpoint(expert_apply), (slot_rows, w_up, w_down))
    returned = low_back(low(outputs))
    picked = returned[choice_one, jnp.minimum(place, CAPACITY - 1)]
    keep_f = kept.astype(jnp.float32)[:, None]
    return after_mix + gate[:, None] * keep_f * picked

def reference(tokens, d_out, segment, route, gain_one, w_in, conv_w, conv_b, w_x, w_dt, b_dt, a_log, d_skip, w_out, gain_two, w_router, w_up, w_down):
    floats = tuple((item.astype(jnp.float32) for item in (tokens, gain_one, w_in, conv_w, conv_b, w_x, w_dt, b_dt, a_log, d_skip, w_out, gain_two, w_router, w_up, w_down)))
    result, pull = jax.vjp(partial(forward, segment=segment, route=route), *floats)
    grads = pull(d_out.astype(jnp.float32))
    choice_one, picks, kept, place = routing(segment, route)
    routed = lax.optimization_barrier(jnp.sum(picks, axis=0))
    held = lax.optimization_barrier(jnp.sum(picks * kept.astype(jnp.int32)[:, None], axis=0))
    counts = jnp.stack([routed, routed - held]).astype(jnp.int32)
    return (result.astype(jnp.bfloat16), grads[0], counts, grads[1], grads[2], grads[3], grads[4], grads[5], grads[6], grads[7], grads[8], grads[9], grads[10], grads[11], grads[12], grads[13], grads[14])
```

```python
import functools
from functools import partial

import jax
import jax.numpy as jnp
from jax import lax
from jax.experimental import pallas as pl
from jax.experimental.pallas import tpu as pltpu
from jax.sharding import PartitionSpec as P

EPS = 1e-06
HIGH = lax.Precision.HIGHEST

TB = 128
CH = 16
LB = 512
LOG2E = 1.4426950408889634
LN2 = 0.6931471805599453
F32 = jnp.float32
BF16 = jnp.bfloat16
NN = (((1,), (0,)), ((), ()))
NT = (((1,), (1,)), ((), ()))
TN = (((0,), (0,)), ((), ()))


def mxu(left, right, dims):
    return lax.dot_general(left, right, dims, preferred_element_type=F32)


def split(x):
    high = x.astype(BF16)
    return high, (x - high.astype(F32)).astype(BF16)


def dot2(x, w, dims):
    high, rest = split(x)
    return mxu(high, w, dims) + mxu(rest, w, dims)


def dot3(x, w, dims):
    high, rest = split(x)
    high_w, rest_w = split(w)
    return mxu(high, high_w, dims) + mxu(high, rest_w, dims) + mxu(rest, high_w, dims)


def sigmoid(x):
    return 1.0 / (1.0 + jnp.exp(-x))


def softplus(x):
    return jnp.maximum(x, 0.0) + jnp.log1p(jnp.exp(-jnp.abs(x)))


def mid_fwd_kernel(rank, both_ref, mask_ref, vec_ref, wx_ref, wdt_ref, rates_ref,
                   gated_ref, pre_ref, pdt_ref, y_ref, proj_ref, hs_ref,
                   ext_ref, conv_ref, h_ref, turned_ref):
    states, width = rates_ref.shape

    @pl.when(pl.program_id(0) == 0)
    def _():
        ext_ref[:8, :] = jnp.zeros((8, width), F32)
        h_ref[...] = jnp.zeros_like(h_ref)

    @pl.when(pl.program_id(0) > 0)
    def _():
        ext_ref[:8, :] = ext_ref[TB:, :]

    def conv_chunk(c, _):
        rows = pl.ds(pl.multiple_of(c * CH, CH), CH)
        masks = mask_ref[rows, :]
        for b in range(width // LB):
            lanes = slice(b * LB, (b + 1) * LB)
            ext_ref[pl.ds(pl.multiple_of(c * CH + 8, 8), CH), lanes] = both_ref[rows, lanes]
            window = ext_ref[pl.ds(pl.multiple_of(c * CH, 8), CH + 8), lanes]
            total = vec_ref[4:5, lanes] + vec_ref[3:4, lanes] * window[8:]
            for k in range(1, 4):
                total = total + vec_ref[3 - k:4 - k, lanes] * window[8 - k:8 - k + CH] * masks[:, k - 1:k]
            pre_ref[rows, lanes] = total
            conv_ref[rows, lanes] = total * sigmoid(total)
        return 0

    lax.fori_loop(0, TB // CH, conv_chunk, 0)
    proj = dot2(conv_ref[...], wx_ref[...], NN)
    proj_ref[...] = proj
    turned_ref[...] = proj.T
    pdt_ref[...] = dot2(proj, wdt_ref[...], NN) + vec_ref[5:6, :]

    def scan_chunk(c, _):
        rows = pl.ds(pl.multiple_of(c * CH, CH), CH)
        tile = pltpu.roll(turned_ref[rank:rank + 2 * states, :], TB - c * CH, 1)
        keep = mask_ref[rows, 0:1]
        for b in range(width // LB):
            lanes = slice(b * LB, (b + 1) * LB)
            rates = rates_ref[:, lanes]
            h = h_ref[:, lanes]
            hs_ref[c, :, lanes] = h
            conv = conv_ref[rows, lanes]
            step = softplus(pdt_ref[rows, lanes])
            source = step * conv
            step = jnp.where(keep > 0.0, step, 1e4)
            outs = []
            for k in range(CH):
                h = jnp.exp2(step[k:k + 1, :] * rates) * h + tile[:states, k:k + 1] * source[k:k + 1, :]
                outs.append(jnp.sum(tile[states:, k:k + 1] * h, axis=0, keepdims=True))
            h_ref[:, lanes] = h
            y = jnp.concatenate(outs, axis=0)
            y_ref[rows, lanes] = y
            gate = both_ref[rows, width + b * LB:width + (b + 1) * LB]
            gated_ref[rows, lanes] = ((y + vec_ref[6:7, lanes] * conv) * (gate * sigmoid(gate))).astype(BF16)
        return 0

    lax.fori_loop(0, TB // CH, scan_chunk, 0)


def mid_fwd(both, masks, vec, wx, wdt, rates, rank):
    length = both.shape[0]
    states, width = rates.shape
    row = lambda i: (i, 0)
    fix = lambda i: (0, 0)
    tall = pl.BlockSpec((TB, width), row)
    like = jax.ShapeDtypeStruct((length, width), F32)
    return pl.pallas_call(
        functools.partial(mid_fwd_kernel, rank),
        grid=(length // TB,),
        out_shape=(jax.ShapeDtypeStruct((length, width), BF16), like, like, like,
                   jax.ShapeDtypeStruct((length, 128), F32),
                   jax.ShapeDtypeStruct((length // CH, states, width), F32)),
        in_specs=[pl.BlockSpec((TB, 2 * width), row), pl.BlockSpec((TB, 8), row), pl.BlockSpec(vec.shape, fix),
                  pl.BlockSpec(wx.shape, fix), pl.BlockSpec(wdt.shape, fix), pl.BlockSpec(rates.shape, fix)],
        out_specs=(tall, tall, tall, tall, pl.BlockSpec((TB, 128), row),
                   pl.BlockSpec((TB // CH, states, width), lambda i: (i, 0, 0))),
        scratch_shapes=[pltpu.VMEM((TB + 8, width), F32), pltpu.VMEM((TB, width), F32),
                        pltpu.VMEM((states, width), F32), pltpu.VMEM((128, TB), F32)],
        compiler_params=pltpu.CompilerParams(vmem_limit_bytes=40 << 20),
        name="mid_fwd",
    )(both, masks, vec, wx, wdt, rates)


def mid_bwd_kernel(rank, both_ref, dg_ref, pre_ref, pdt_ref, y_ref, proj_ref, hs_ref, mask_ref, vec_ref, wxt_ref,
                   wdt_ref, rates_ref,
                   dboth_ref, gvec_ref, gwx_ref, gwdt_ref, gr_ref,
                   ext_ref, g_ref, dec_ref, p_ref, part_ref, dproj_ref, dconv_ref, dpdt_ref, conv_ref, turned_ref,
                   acc_ref):
    states, width = rates_ref.shape
    steps = TB // CH

    @pl.when(pl.program_id(0) == 0)
    def _():
        ext_ref[TB:, :] = jnp.zeros((8, width), F32)
        g_ref[...] = jnp.zeros_like(g_ref)
        acc_ref[...] = jnp.zeros_like(acc_ref)
        gwx_ref[...] = jnp.zeros_like(gwx_ref)
        gwdt_ref[...] = jnp.zeros_like(gwdt_ref)
        gr_ref[...] = jnp.zeros_like(gr_ref)

    @pl.when(pl.program_id(0) > 0)
    def _():
        ext_ref[TB:, :] = ext_ref[:8, :]

    turned_ref[...] = proj_ref[...].T
    ones = jnp.ones((128, 128), BF16)
    lane = lax.broadcasted_iota(jnp.int32, (2 * states, 128), 1)
    place = lax.broadcasted_iota(jnp.int32, (2 * states, 128), 0) + rank

    def fold(x):
        out = x[:, :128]
        for i in range(1, LB // 128):
            out = out + x[:, i * 128:(i + 1) * 128]
        return out

    def halves(x):
        out = x[:8]
        for i in range(1, CH // 8):
            out = out + x[i * 8:(i + 1) * 8]
        return out

    def scan_chunk(i, _):
        c = steps - 1 - i
        rows = pl.ds(pl.multiple_of(c * CH, CH), CH)
        tile = pltpu.roll(turned_ref[rank:rank + 2 * states, :], TB - c * CH, 1)
        keep = mask_ref[rows, 0:1]
        for b in range(width // LB):
            lanes = slice(b * LB, (b + 1) * LB)
            rates = rates_ref[:, lanes]
            h = hs_ref[c, :, lanes]
            pre = pre_ref[rows, lanes]
            conv = pre * sigmoid(pre)
            conv_ref[rows, lanes] = conv
            pdt = pdt_ref[rows, lanes]
            step = softplus(pdt)
            source = step * conv
            decay_step = jnp.where(keep > 0.0, step, 1e4)
            skip = vec_ref[6:7, lanes]
            gate = both_ref[rows, width + b * LB:width + (b + 1) * LB]
            sig = sigmoid(gate)
            dg = dg_ref[rows, lanes]
            dboth_ref[rows, width + b * LB:width + (b + 1) * LB] = (
                dg * (y_ref[rows, lanes] + skip * conv) * (sig * (1.0 + gate * (1.0 - sig)))).astype(BF16)
            dy = dg * (gate * sig)
            for k in range(CH):
                dec = jnp.exp2(decay_step[k:k + 1, :] * rates)
                p = dec * h
                dec_ref[k] = dec
                p_ref[k] = p
                h = p + tile[:states, k:k + 1] * source[k:k + 1, :]
                out = fold(dy[k:k + 1, :] * h)
                part_ref[k, states:, :] = out if b == 0 else part_ref[k, states:, :] + out
            g = g_ref[:, lanes]
            dr = gr_ref[:, lanes]
            dus, dss = [None] * CH, [None] * CH
            for k in reversed(range(CH)):
                dh = g + tile[states:, k:k + 1] * dy[k:k + 1, :]
                out = fold(dh * source[k:k + 1, :])
                part_ref[k, :states, :] = out if b == 0 else part_ref[k, :states, :] + out
                dus[k] = jnp.sum(dh * tile[:states, k:k + 1], axis=0, keepdims=True)
                da = dh * p_ref[k]
                dss[k] = jnp.sum(da * rates, axis=0, keepdims=True)
                dr = dr + da * decay_step[k:k + 1, :]
                g = dec_ref[k] * dh
            g_ref[:, lanes] = g
            gr_ref[:, lanes] = dr
            du = jnp.concatenate(dus, axis=0)
            dpdt = (jnp.concatenate(dss, axis=0) * LN2 + du * conv) * sigmoid(pdt)
            dpdt_ref[rows, lanes] = dpdt
            dconv_ref[rows, lanes] = dy * skip + du * step
            acc_ref[5, :, lanes] += halves(dpdt)
            acc_ref[6, :, lanes] += halves(dy * conv)
        high, rest = split(part_ref[...].reshape(CH * 2 * states, 128))
        sums = (mxu(high, ones, NN) + mxu(rest, ones, NN)).reshape(CH, 2 * states, 128)
        picked = jnp.where((lane == place)[None], sums, 0.0)
        dproj_ref[rows, :] = jnp.sum(picked, axis=1)
        return 0

    lax.fori_loop(0, steps, scan_chunk, 0)
    dpdt = dpdt_ref[...]
    dproj = dproj_ref[...] + dot2(dpdt, wdt_ref[...], NT)
    gwdt_ref[...] += dot3(turned_ref[...], dpdt, NN)
    gwx_ref[...] += dot3(dproj.T, conv_ref[...], NN)
    dconv_ref[...] += dot2(dproj, wxt_ref[...], NN)

    def act_chunk(c, _):
        rows = pl.ds(pl.multiple_of(c * CH, CH), CH)
        for b in range(width // LB):
            lanes = slice(b * LB, (b + 1) * LB)
            pre = pre_ref[rows, lanes]
            sig = sigmoid(pre)
            ext_ref[rows, lanes] = dconv_ref[rows, lanes] * (sig * (1.0 + pre * (1.0 - sig)))
        return 0

    lax.fori_loop(0, steps, act_chunk, 0)

    def conv_chunk(c, _):
        rows = pl.ds(pl.multiple_of(c * CH, CH), CH)
        masks = mask_ref[rows, :]
        for b in range(width // LB):
            lanes = slice(b * LB, (b + 1) * LB)
            inner = both_ref[rows, lanes]
            window = ext_ref[pl.ds(pl.multiple_of(c * CH, 8), CH + 8), lanes]
            here = window[:CH]
            total = vec_ref[3:4, lanes] * here
            acc_ref[4, :, lanes] += halves(here)
            acc_ref[3, :, lanes] += halves(here * inner)
            for k in range(1, 4):
                later = window[k:k + CH] * masks[:, 2 + k:3 + k]
                total = total + vec_ref[3 - k:4 - k, lanes] * later
                acc_ref[3 - k, :, lanes] += halves(later * inner)
            dboth_ref[rows, lanes] = total.astype(BF16)
        return 0

    lax.fori_loop(0, steps, conv_chunk, 0)

    @pl.when(pl.program_id(0) == pl.num_programs(0) - 1)
    def _():
        gvec_ref[...] = jnp.concatenate(
            [jnp.sum(acc_ref[k], axis=0, keepdims=True) for k in range(8)], axis=0)


def mid_bwd(both, dg, pre, pdt, y, proj, hs, masks, vec, wxt, wdt, rates, rank):
    length = both.shape[0]
    states, width = rates.shape
    blocks = length // TB
    row = lambda i: (blocks - 1 - i, 0)
    fix = lambda i: (0, 0)
    tall = pl.BlockSpec((TB, width), row)
    return pl.pallas_call(
        functools.partial(mid_bwd_kernel, rank),
        grid=(blocks,),
        out_shape=(jax.ShapeDtypeStruct((length, 2 * width), BF16), jax.ShapeDtypeStruct((8, width), F32),
                   jax.ShapeDtypeStruct((128, width), F32), jax.ShapeDtypeStruct((128, width), F32),
                   jax.ShapeDtypeStruct((states, width), F32)),
        in_specs=[pl.BlockSpec((TB, 2 * width), row), tall, tall, tall, tall, pl.BlockSpec((TB, 128), row),
                  pl.BlockSpec((TB // CH, states, width), lambda i: (blocks - 1 - i, 0, 0)),
                  pl.BlockSpec((TB, 8), row), pl.BlockSpec(vec.shape, fix), pl.BlockSpec(wxt.shape, fix),
                  pl.BlockSpec(wdt.shape, fix), pl.BlockSpec(rates.shape, fix)],
        out_specs=(pl.BlockSpec((TB, 2 * width), row), pl.BlockSpec((8, width), fix),
                   pl.BlockSpec((128, width), fix), pl.BlockSpec((128, width), fix), pl.BlockSpec((states, width), fix)),
        scratch_shapes=[pltpu.VMEM((TB + 8, width), F32), pltpu.VMEM((states, width), F32),
                        pltpu.VMEM((CH, states, LB), F32), pltpu.VMEM((CH, states, LB), F32),
                        pltpu.VMEM((CH, 2 * states, 128), F32), pltpu.VMEM((TB, 128), F32),
                        pltpu.VMEM((TB, width), F32), pltpu.VMEM((TB, width), F32), pltpu.VMEM((TB, width), F32),
                        pltpu.VMEM((128, TB), F32), pltpu.VMEM((8, 8, width), F32)],
        compiler_params=pltpu.CompilerParams(vmem_limit_bytes=56 << 20),
        name="mid_bwd",
    )(both, dg, pre, pdt, y, proj, hs, masks, vec, wxt, wdt, rates)


def flags(segment):
    length = segment.shape[0]
    cols = []
    for k in range(1, 4):
        moved = jnp.concatenate([jnp.full((k,), -2, jnp.int32), segment[:length - k]])
        cols.append(moved == segment)
    for k in range(1, 4):
        moved = jnp.concatenate([segment[k:], jnp.full((k,), -2, jnp.int32)])
        cols.append(moved == segment)
    cols.append(segment >= 0)
    cols.append(segment >= 0)
    return jnp.stack(cols, axis=1).astype(F32)


def prefix(part, axis, combine, identity):
    place = lax.axis_index(axis)
    gathered = lax.all_gather(part, axis)
    state = jnp.zeros_like(part) + jnp.asarray(identity, part.dtype)

    def one(lap, state):
        return combine(state, lax.dynamic_index_in_dim(gathered, lap, 0, False))

    return lax.fori_loop(0, place, one, state)


def rms_scale(values, gain):
    return values * lax.rsqrt(jnp.mean(values * values, axis=-1, keepdims=True) + EPS) * gain


def add_counts(earlier, later):
    return earlier + later


def contract_rows(left, right):
    return lax.dot_general(
        left, right, (((0,), (0,)), ((), ())), preferred_element_type=jnp.float32
    )


def local(
    tokens,
    d_out,
    segment,
    route,
    gain_one,
    w_in,
    conv_w,
    conv_b,
    w_x,
    w_dt,
    b_dt,
    a_log,
    d_skip,
    w_out,
    gain_two,
    w_router,
    w_up,
    w_down,
):
    length, width = tokens.shape
    inner_w = w_in.shape[1] // 2
    experts = w_router.shape[1]
    local_experts = w_up.shape[0]
    groups = lax.axis_size("ep")
    slots = 3 * length // (2 * experts)
    capacity = 5 * length * lax.axis_size("ep") * lax.axis_size("tp") // (4 * experts)
    token_f = tokens.astype(jnp.float32)
    valid = (segment >= 0).astype(jnp.float32)[:, None]
    rank_dt, states = w_dt.shape[0], a_log.shape[0]
    masks = flags(segment)
    vec = jnp.concatenate([conv_w, conv_b[None], b_dt[None], d_skip[None], d_skip[None]], axis=0).astype(F32)
    wx_pad = jnp.pad(w_x, ((0, 0), (0, 128 - rank_dt - 2 * states)))
    wdt_pad = jnp.pad(w_dt, ((0, 128 - rank_dt), (0, 0)))
    rates = -jnp.exp(a_log.astype(F32))
    normed_one, norm_one_pull = jax.vjp(rms_scale, token_f, gain_one.astype(jnp.float32))
    normed_low = normed_one.astype(jnp.bfloat16)
    both = jnp.dot(normed_low, w_in, preferred_element_type=jnp.float32)

    gated_low, pre, pre_dt, scanned, proj, starts = mid_fwd(
        both, masks, vec, wx_pad, wdt_pad, rates * LOG2E, rank_dt
    )
    mixed = jnp.dot(gated_low, w_out, preferred_element_type=jnp.float32)
    after_mix = token_f + mixed * valid
    normed_two, norm_two_pull = jax.vjp(rms_scale, after_mix, gain_two.astype(jnp.float32))
    pick_int = (
        (route == jnp.arange(experts, dtype=jnp.int32)[None, :]) & (segment >= 0)[:, None]
    ).astype(jnp.int32)
    picks = pick_int.astype(jnp.float32)

    def router(normed_in, router_w):
        probs = jax.nn.softmax(jnp.dot(normed_in, router_w, precision=HIGH), axis=-1)
        return jnp.sum(probs * picks, axis=-1)

    gate, router_pull = jax.vjp(router, normed_two, w_router.astype(jnp.float32))
    local_count = jnp.sum(pick_int, axis=0)
    prior = prefix(local_count, ("ep", "tp"), add_counts, jnp.zeros_like(local_count))
    local_rank = jnp.sum(jnp.cumsum(pick_int, axis=0) * pick_int, axis=1) - 1
    global_rank = jnp.sum(pick_int * prior[None, :], axis=1) + local_rank
    kept = (segment >= 0) & (global_rank < capacity)
    slot_id = jnp.where(kept, route[:, 0] * slots + local_rank, -1)
    dispatch = (jnp.arange(experts * slots, dtype=jnp.int32)[:, None] == slot_id[None, :]).astype(
        jnp.bfloat16
    )
    expert_in = normed_two.astype(jnp.bfloat16)
    outgoing = jnp.dot(dispatch, expert_in, preferred_element_type=jnp.float32).astype(jnp.bfloat16)
    outgoing = outgoing.reshape(groups, local_experts, slots, width)
    received = lax.all_to_all(outgoing, "ep", split_axis=0, concat_axis=2, tiled=True)
    full_up, full_down = (w_up, w_down)
    expert_rows = lax.all_gather(received, "tp", axis=2, tiled=True)
    hidden_pre = jnp.einsum(
        "axrd,xdf->axrf", expert_rows, full_up, preferred_element_type=jnp.float32
    )
    gelu_value, gelu_pull = jax.vjp(partial(jax.nn.gelu, approximate=False), hidden_pre)
    hidden_low = gelu_value.astype(jnp.bfloat16)
    terms = jnp.einsum("axrf,xfd->axrd", hidden_low, full_down, preferred_element_type=jnp.float32)
    expert_out = lax.psum_scatter(terms, "tp", scatter_dimension=2, tiled=True)
    returned = lax.all_to_all(
        expert_out.astype(jnp.bfloat16), "ep", split_axis=2, concat_axis=0, tiled=True
    )
    returned = returned.reshape(experts * slots, width)
    token_out = contract_rows(dispatch, returned)
    keep_f = kept.astype(jnp.float32)[:, None]
    weighting = gate[:, None] * keep_f
    final = after_mix + weighting * token_out
    upstream = d_out.astype(jnp.float32)
    d_token_out = (weighting * upstream).astype(jnp.bfloat16)
    d_slots = jnp.dot(dispatch, d_token_out, preferred_element_type=jnp.float32).astype(
        jnp.bfloat16
    )
    d_slots = d_slots.reshape(groups, local_experts, slots, width)
    d_gate = keep_f[:, 0] * jnp.sum(upstream * token_out, axis=1)
    d_received = lax.all_to_all(d_slots, "ep", split_axis=0, concat_axis=2, tiled=True)
    d_rows_all = lax.all_gather(d_received, "tp", axis=2, tiled=True)
    gelu_back, hidden_back = gelu_pull, hidden_low
    grad_down = jnp.einsum(
        "axrf,axrd->xfd", hidden_back, d_rows_all, preferred_element_type=jnp.float32
    )
    d_hidden = jnp.einsum(
        "axrd,xfd->axrf", d_rows_all, full_down, preferred_element_type=jnp.float32
    )
    d_pre = gelu_back(d_hidden)[0].astype(jnp.bfloat16)
    grad_up = jnp.einsum("axrd,axrf->xdf", expert_rows, d_pre, preferred_element_type=jnp.float32)
    row_terms = jnp.einsum("axrf,xdf->axrd", d_pre, full_up, preferred_element_type=jnp.float32)
    d_expert_in = lax.psum_scatter(row_terms, "tp", scatter_dimension=2, tiled=True)
    d_back = lax.all_to_all(
        d_expert_in.astype(jnp.bfloat16), "ep", split_axis=2, concat_axis=0, tiled=True
    )
    d_normed = contract_rows(dispatch, d_back.reshape(experts * slots, width))
    d_norm_router, grad_router = router_pull(d_gate)
    d_after, grad_gain_two = norm_two_pull(d_normed + d_norm_router)
    d_after = d_after + upstream
    d_mixed = (d_after * valid).astype(jnp.bfloat16)
    grad_out = contract_rows(gated_low, d_mixed)
    d_gated = lax.dot_general(
        d_mixed, w_out, (((1,), (1,)), ((), ())), preferred_element_type=jnp.float32
    )
    d_both, grad_vec, grad_x, grad_dt, grad_rates = mid_bwd(
        both, d_gated, pre, pre_dt, scanned, proj, starts, masks, vec, wx_pad.T, wdt_pad, rates * LOG2E, rank_dt
    )
    middle_grads = (
        grad_vec[: conv_w.shape[0]], grad_vec[4], grad_x[: rank_dt + 2 * states].T, grad_dt[:rank_dt], grad_vec[5],
        grad_rates * rates, grad_vec[6],
    )
    grad_in = contract_rows(normed_low, d_both)
    d_normed_one = lax.dot_general(
        d_both, w_in, (((1,), (1,)), ((), ())), preferred_element_type=jnp.float32
    )
    d_tokens_norm, grad_gain_one = norm_one_pull(d_normed_one)
    d_tokens = d_after + d_tokens_norm
    held = jnp.sum(pick_int * kept.astype(jnp.int32)[:, None], axis=0)
    count_f = jnp.stack([local_count, local_count - held]).astype(jnp.float32)
    summed = lax.psum(
        (
            grad_gain_one,
            grad_in,
            middle_grads[0],
            middle_grads[1],
            middle_grads[2],
            middle_grads[3],
            middle_grads[4],
            middle_grads[5],
            middle_grads[6],
            grad_out,
            grad_gain_two,
            grad_router,
            count_f,
        ),
        ("ep", "tp"),
    )
    return (
        final.astype(jnp.bfloat16),
        d_tokens,
        summed[12].astype(jnp.int32),
        summed[0],
        summed[1],
        summed[2],
        summed[3],
        summed[4],
        summed[5],
        summed[6],
        summed[7],
        summed[8],
        summed[9],
        summed[10],
        summed[11],
        grad_up,
        grad_down,
    )


def solution(mesh):
    in_specs = (
        P(("ep", "tp"), None),
        P(("ep", "tp"), None),
        P(("ep", "tp")),
        P(("ep", "tp"), None),
        P(),
        P(),
        P(),
        P(),
        P(),
        P(),
        P(),
        P(),
        P(),
        P(),
        P(),
        P(),
        P("ep", None, "tp"),
        P("ep", "tp", None),
    )
    out_specs = (
        P(("ep", "tp"), None),
        P(("ep", "tp"), None),
        P(),
        P(),
        P(),
        P(),
        P(),
        P(),
        P(),
        P(),
        P(),
        P(),
        P(),
        P(),
        P(),
        P("ep", None, "tp"),
        P("ep", "tp", None),
    )
    return jax.shard_map(local, mesh=mesh, in_specs=in_specs, out_specs=out_specs, check_vma=False)
```

```python
import functools
from functools import partial

import jax
import jax.numpy as jnp
from jax import lax
from jax.experimental import pallas as pl
from jax.experimental.pallas import tpu as pltpu
from jax.sharding import PartitionSpec as P

EPS = 1e-06
HIGH = lax.Precision.HIGHEST

MESH = pl.DeviceIdType.MESH
TB = 128
CH = 16
LB = 512
LOG2E = 1.4426950408889634
LN2 = 0.6931471805599453
F32 = jnp.float32
BF16 = jnp.bfloat16
NN = (((1,), (0,)), ((), ()))
NT = (((1,), (1,)), ((), ()))
TN = (((0,), (0,)), ((), ()))


def mxu(left, right, dims):
    return lax.dot_general(left, right, dims, preferred_element_type=F32)


def split(x):
    high = x.astype(BF16)
    return high, (x - high.astype(F32)).astype(BF16)


def dot2(x, w, dims):
    high, rest = split(x)
    return mxu(high, w, dims) + mxu(rest, w, dims)


def dot3(x, w, dims):
    high, rest = split(x)
    high_w, rest_w = split(w)
    return mxu(high, high_w, dims) + mxu(high, rest_w, dims) + mxu(rest, high_w, dims)


def sigmoid(x):
    return 1.0 / (1.0 + jnp.exp(-x))


def softplus(x):
    return jnp.maximum(x, 0.0) + jnp.log1p(jnp.exp(-jnp.abs(x)))


def mid_fwd_kernel(rank, both_ref, mask_ref, vec_ref, wx_ref, wdt_ref, rates_ref,
                   gated_ref, pre_ref, pdt_ref, y_ref, proj_ref, hs_ref,
                   ext_ref, conv_ref, h_ref, turned_ref):
    states, width = rates_ref.shape

    @pl.when(pl.program_id(0) == 0)
    def _():
        ext_ref[:8, :] = jnp.zeros((8, width), F32)
        h_ref[...] = jnp.zeros_like(h_ref)

    @pl.when(pl.program_id(0) > 0)
    def _():
        ext_ref[:8, :] = ext_ref[TB:, :]

    def conv_chunk(c, _):
        rows = pl.ds(pl.multiple_of(c * CH, CH), CH)
        masks = mask_ref[rows, :]
        for b in range(width // LB):
            lanes = slice(b * LB, (b + 1) * LB)
            ext_ref[pl.ds(pl.multiple_of(c * CH + 8, 8), CH), lanes] = both_ref[rows, lanes]
            window = ext_ref[pl.ds(pl.multiple_of(c * CH, 8), CH + 8), lanes]
            total = vec_ref[4:5, lanes] + vec_ref[3:4, lanes] * window[8:]
            for k in range(1, 4):
                total = total + vec_ref[3 - k:4 - k, lanes] * window[8 - k:8 - k + CH] * masks[:, k - 1:k]
            pre_ref[rows, lanes] = total
            conv_ref[rows, lanes] = total * sigmoid(total)
        return 0

    lax.fori_loop(0, TB // CH, conv_chunk, 0)
    proj = dot2(conv_ref[...], wx_ref[...], NN)
    proj_ref[...] = proj
    turned_ref[...] = proj.T
    pdt_ref[...] = dot2(proj, wdt_ref[...], NN) + vec_ref[5:6, :]

    def scan_chunk(c, _):
        rows = pl.ds(pl.multiple_of(c * CH, CH), CH)
        tile = pltpu.roll(turned_ref[rank:rank + 2 * states, :], TB - c * CH, 1)
        keep = mask_ref[rows, 0:1]
        for b in range(width // LB):
            lanes = slice(b * LB, (b + 1) * LB)
            rates = rates_ref[:, lanes]
            h = h_ref[:, lanes]
            hs_ref[c, :, lanes] = h
            conv = conv_ref[rows, lanes]
            step = softplus(pdt_ref[rows, lanes])
            source = step * conv
            step = jnp.where(keep > 0.0, step, 1e4)
            outs = []
            for k in range(CH):
                h = jnp.exp2(step[k:k + 1, :] * rates) * h + tile[:states, k:k + 1] * source[k:k + 1, :]
                outs.append(jnp.sum(tile[states:, k:k + 1] * h, axis=0, keepdims=True))
            h_ref[:, lanes] = h
            y = jnp.concatenate(outs, axis=0)
            y_ref[rows, lanes] = y
            gate = both_ref[rows, width + b * LB:width + (b + 1) * LB]
            gated_ref[rows, lanes] = ((y + vec_ref[6:7, lanes] * conv) * (gate * sigmoid(gate))).astype(BF16)
        return 0

    lax.fori_loop(0, TB // CH, scan_chunk, 0)


def mid_fwd(both, masks, vec, wx, wdt, rates, rank):
    length = both.shape[0]
    states, width = rates.shape
    row = lambda i: (i, 0)
    fix = lambda i: (0, 0)
    tall = pl.BlockSpec((TB, width), row)
    like = jax.ShapeDtypeStruct((length, width), F32)
    return pl.pallas_call(
        functools.partial(mid_fwd_kernel, rank),
        grid=(length // TB,),
        out_shape=(jax.ShapeDtypeStruct((length, width), BF16), like, like, like,
                   jax.ShapeDtypeStruct((length, 128), F32),
                   jax.ShapeDtypeStruct((length // CH, states, width), F32)),
        in_specs=[pl.BlockSpec((TB, 2 * width), row), pl.BlockSpec((TB, 8), row), pl.BlockSpec(vec.shape, fix),
                  pl.BlockSpec(wx.shape, fix), pl.BlockSpec(wdt.shape, fix), pl.BlockSpec(rates.shape, fix)],
        out_specs=(tall, tall, tall, tall, pl.BlockSpec((TB, 128), row),
                   pl.BlockSpec((TB // CH, states, width), lambda i: (i, 0, 0))),
        scratch_shapes=[pltpu.VMEM((TB + 8, width), F32), pltpu.VMEM((TB, width), F32),
                        pltpu.VMEM((states, width), F32), pltpu.VMEM((128, TB), F32)],
        compiler_params=pltpu.CompilerParams(vmem_limit_bytes=40 << 20),
        name="mid_fwd",
    )(both, masks, vec, wx, wdt, rates)


def mid_bwd_kernel(rank, both_ref, dg_ref, pre_ref, pdt_ref, y_ref, proj_ref, hs_ref, mask_ref, vec_ref, wxt_ref,
                   wdt_ref, rates_ref,
                   dboth_ref, gvec_ref, gwx_ref, gwdt_ref, gr_ref,
                   ext_ref, g_ref, dec_ref, p_ref, part_ref, dproj_ref, dconv_ref, dpdt_ref, conv_ref, turned_ref,
                   acc_ref):
    states, width = rates_ref.shape
    steps = TB // CH

    @pl.when(pl.program_id(0) == 0)
    def _():
        ext_ref[TB:, :] = jnp.zeros((8, width), F32)
        g_ref[...] = jnp.zeros_like(g_ref)
        acc_ref[...] = jnp.zeros_like(acc_ref)
        gwx_ref[...] = jnp.zeros_like(gwx_ref)
        gwdt_ref[...] = jnp.zeros_like(gwdt_ref)
        gr_ref[...] = jnp.zeros_like(gr_ref)

    @pl.when(pl.program_id(0) > 0)
    def _():
        ext_ref[TB:, :] = ext_ref[:8, :]

    turned_ref[...] = proj_ref[...].T
    ones = jnp.ones((128, 128), BF16)
    lane = lax.broadcasted_iota(jnp.int32, (2 * states, 128), 1)
    place = lax.broadcasted_iota(jnp.int32, (2 * states, 128), 0) + rank

    def fold(x):
        out = x[:, :128]
        for i in range(1, LB // 128):
            out = out + x[:, i * 128:(i + 1) * 128]
        return out

    def halves(x):
        out = x[:8]
        for i in range(1, CH // 8):
            out = out + x[i * 8:(i + 1) * 8]
        return out

    def scan_chunk(i, _):
        c = steps - 1 - i
        rows = pl.ds(pl.multiple_of(c * CH, CH), CH)
        tile = pltpu.roll(turned_ref[rank:rank + 2 * states, :], TB - c * CH, 1)
        keep = mask_ref[rows, 0:1]
        for b in range(width // LB):
            lanes = slice(b * LB, (b + 1) * LB)
            rates = rates_ref[:, lanes]
            h = hs_ref[c, :, lanes]
            pre = pre_ref[rows, lanes]
            conv = pre * sigmoid(pre)
            conv_ref[rows, lanes] = conv
            pdt = pdt_ref[rows, lanes]
            step = softplus(pdt)
            source = step * conv
            decay_step = jnp.where(keep > 0.0, step, 1e4)
            skip = vec_ref[6:7, lanes]
            gate = both_ref[rows, width + b * LB:width + (b + 1) * LB]
            sig = sigmoid(gate)
            dg = dg_ref[rows, lanes]
            dboth_ref[rows, width + b * LB:width + (b + 1) * LB] = (
                dg * (y_ref[rows, lanes] + skip * conv) * (sig * (1.0 + gate * (1.0 - sig)))).astype(BF16)
            dy = dg * (gate * sig)
            for k in range(CH):
                dec = jnp.exp2(decay_step[k:k + 1, :] * rates)
                p = dec * h
                dec_ref[k] = dec
                p_ref[k] = p
                h = p + tile[:states, k:k + 1] * source[k:k + 1, :]
                out = fold(dy[k:k + 1, :] * h)
                part_ref[k, states:, :] = out if b == 0 else part_ref[k, states:, :] + out
            g = g_ref[:, lanes]
            dr = gr_ref[:, lanes]
            dus, dss = [None] * CH, [None] * CH
            for k in reversed(range(CH)):
                dh = g + tile[states:, k:k + 1] * dy[k:k + 1, :]
                out = fold(dh * source[k:k + 1, :])
                part_ref[k, :states, :] = out if b == 0 else part_ref[k, :states, :] + out
                dus[k] = jnp.sum(dh * tile[:states, k:k + 1], axis=0, keepdims=True)
                da = dh * p_ref[k]
                dss[k] = jnp.sum(da * rates, axis=0, keepdims=True)
                dr = dr + da * decay_step[k:k + 1, :]
                g = dec_ref[k] * dh
            g_ref[:, lanes] = g
            gr_ref[:, lanes] = dr
            du = jnp.concatenate(dus, axis=0)
            dpdt = (jnp.concatenate(dss, axis=0) * LN2 + du * conv) * sigmoid(pdt)
            dpdt_ref[rows, lanes] = dpdt
            dconv_ref[rows, lanes] = dy * skip + du * step
            acc_ref[5, :, lanes] += halves(dpdt)
            acc_ref[6, :, lanes] += halves(dy * conv)
        high, rest = split(part_ref[...].reshape(CH * 2 * states, 128))
        sums = (mxu(high, ones, NN) + mxu(rest, ones, NN)).reshape(CH, 2 * states, 128)
        picked = jnp.where((lane == place)[None], sums, 0.0)
        dproj_ref[rows, :] = jnp.sum(picked, axis=1)
        return 0

    lax.fori_loop(0, steps, scan_chunk, 0)
    dpdt = dpdt_ref[...]
    dproj = dproj_ref[...] + dot2(dpdt, wdt_ref[...], NT)
    gwdt_ref[...] += dot3(turned_ref[...], dpdt, NN)
    gwx_ref[...] += dot3(dproj.T, conv_ref[...], NN)
    dconv_ref[...] += dot2(dproj, wxt_ref[...], NN)

    def act_chunk(c, _):
        rows = pl.ds(pl.multiple_of(c * CH, CH), CH)
        for b in range(width // LB):
            lanes = slice(b * LB, (b + 1) * LB)
            pre = pre_ref[rows, lanes]
            sig = sigmoid(pre)
            ext_ref[rows, lanes] = dconv_ref[rows, lanes] * (sig * (1.0 + pre * (1.0 - sig)))
        return 0

    lax.fori_loop(0, steps, act_chunk, 0)

    def conv_chunk(c, _):
        rows = pl.ds(pl.multiple_of(c * CH, CH), CH)
        masks = mask_ref[rows, :]
        for b in range(width // LB):
            lanes = slice(b * LB, (b + 1) * LB)
            inner = both_ref[rows, lanes]
            window = ext_ref[pl.ds(pl.multiple_of(c * CH, 8), CH + 8), lanes]
            here = window[:CH]
            total = vec_ref[3:4, lanes] * here
            acc_ref[4, :, lanes] += halves(here)
            acc_ref[3, :, lanes] += halves(here * inner)
            for k in range(1, 4):
                later = window[k:k + CH] * masks[:, 2 + k:3 + k]
                total = total + vec_ref[3 - k:4 - k, lanes] * later
                acc_ref[3 - k, :, lanes] += halves(later * inner)
            dboth_ref[rows, lanes] = total.astype(BF16)
        return 0

    lax.fori_loop(0, steps, conv_chunk, 0)

    @pl.when(pl.program_id(0) == pl.num_programs(0) - 1)
    def _():
        gvec_ref[...] = jnp.concatenate(
            [jnp.sum(acc_ref[k], axis=0, keepdims=True) for k in range(8)], axis=0)


def mid_bwd(both, dg, pre, pdt, y, proj, hs, masks, vec, wxt, wdt, rates, rank):
    length = both.shape[0]
    states, width = rates.shape
    blocks = length // TB
    row = lambda i: (blocks - 1 - i, 0)
    fix = lambda i: (0, 0)
    tall = pl.BlockSpec((TB, width), row)
    return pl.pallas_call(
        functools.partial(mid_bwd_kernel, rank),
        grid=(blocks,),
        out_shape=(jax.ShapeDtypeStruct((length, 2 * width), BF16), jax.ShapeDtypeStruct((8, width), F32),
                   jax.ShapeDtypeStruct((128, width), F32), jax.ShapeDtypeStruct((128, width), F32),
                   jax.ShapeDtypeStruct((states, width), F32)),
        in_specs=[pl.BlockSpec((TB, 2 * width), row), tall, tall, tall, tall, pl.BlockSpec((TB, 128), row),
                  pl.BlockSpec((TB // CH, states, width), lambda i: (blocks - 1 - i, 0, 0)),
                  pl.BlockSpec((TB, 8), row), pl.BlockSpec(vec.shape, fix), pl.BlockSpec(wxt.shape, fix),
                  pl.BlockSpec(wdt.shape, fix), pl.BlockSpec(rates.shape, fix)],
        out_specs=(pl.BlockSpec((TB, 2 * width), row), pl.BlockSpec((8, width), fix),
                   pl.BlockSpec((128, width), fix), pl.BlockSpec((128, width), fix), pl.BlockSpec((states, width), fix)),
        scratch_shapes=[pltpu.VMEM((TB + 8, width), F32), pltpu.VMEM((states, width), F32),
                        pltpu.VMEM((CH, states, LB), F32), pltpu.VMEM((CH, states, LB), F32),
                        pltpu.VMEM((CH, 2 * states, 128), F32), pltpu.VMEM((TB, 128), F32),
                        pltpu.VMEM((TB, width), F32), pltpu.VMEM((TB, width), F32), pltpu.VMEM((TB, width), F32),
                        pltpu.VMEM((128, TB), F32), pltpu.VMEM((8, 8, width), F32)],
        compiler_params=pltpu.CompilerParams(vmem_limit_bytes=56 << 20),
        name="mid_bwd",
    )(both, dg, pre, pdt, y, proj, hs, masks, vec, wxt, wdt, rates)


def flags(segment):
    length = segment.shape[0]
    cols = []
    for k in range(1, 4):
        moved = jnp.concatenate([jnp.full((k,), -2, jnp.int32), segment[:length - k]])
        cols.append(moved == segment)
    for k in range(1, 4):
        moved = jnp.concatenate([segment[k:], jnp.full((k,), -2, jnp.int32)])
        cols.append(moved == segment)
    cols.append(segment >= 0)
    cols.append(segment >= 0)
    return jnp.stack(cols, axis=1).astype(F32)


def bit_orders(groups, members):
    ep_bits, tp_bits = groups.bit_length() - 1, members.bit_length() - 1
    x = [("ep", b) for b in range(ep_bits - 2)]
    z = [("ep", b) for b in range(ep_bits - 2, ep_bits)]
    y = [("tp", b) for b in range(1, tp_bits)]
    core = [("tp", 0)]
    return [core + x + y + z, core + y + x + z]


def region_sizes(stages, rows, cols):
    sizes = []
    for _ in range(stages):
        if rows > 16:
            rows //= 2
            sizes.append((rows, cols, True))
        else:
            cols //= 2
            sizes.append((rows, cols, False))
    return sizes


def sum_kernel(orders, g_ref, out_ref, *rest):
    stages = len(orders[0])
    land = rest[:stages]
    work_ref, send_sem, recv_sem = rest[stages:]
    chunks, rows, cols = g_ref.shape
    sizes = region_sizes(stages, rows, cols)
    me = {"ep": lax.axis_index("ep"), "tp": lax.axis_index("tp")}

    def bit(stage):
        axis, b = stage
        return lax.rem(me[axis] // (1 << b), 2)

    def partner(stage):
        axis, b = stage
        there = dict(me)
        there[axis] = me[axis] + (1 << b) - 2 * (1 << b) * bit(stage)
        return (there["ep"], there["tp"])

    barrier = pltpu.get_barrier_semaphore()
    for stage in orders[0]:
        pl.semaphore_signal(barrier, inc=1, device_id=partner(stage), device_id_type=MESH)
    pl.semaphore_wait(barrier, stages)

    def place(order, upto, flip):
        r0, c0 = 0, 0
        for s in range(upto + 1):
            b = bit(order[s])
            if s == upto and flip:
                b = 1 - b
            if sizes[s][2]:
                r0 = r0 + b * sizes[s][0]
            else:
                c0 = c0 + b * sizes[s][1]
        return pl.multiple_of(r0, 16), (pl.multiple_of(c0, 128) if not isinstance(c0, int) else c0)

    def part(ref, c, order, upto, flip):
        r0, c0 = place(order, upto, flip)
        return ref.at[c, pl.ds(r0, sizes[upto][0]), pl.ds(c0, sizes[upto][1])]

    def scatter(s, p, c):
        order = orders[p]
        return pltpu.make_async_remote_copy(
            src_ref=part(g_ref if s == 0 else work_ref, c, order, s, True), dst_ref=land[s].at[c],
            send_sem=send_sem.at[s, c], recv_sem=recv_sem.at[s, c], device_id=partner(order[s]), device_id_type=MESH)

    def gather(s, p, c):
        order = orders[p]
        mine = part(out_ref, c, order, s, False)
        return pltpu.make_async_remote_copy(
            src_ref=mine, dst_ref=mine,
            send_sem=send_sem.at[stages + s, c], recv_sem=recv_sem.at[stages + s, c], device_id=partner(order[s]),
            device_id_type=MESH)

    def gathered(s, p, c):
        order = orders[p]
        other = part(out_ref, c, order, s, True)
        return pltpu.make_async_remote_copy(
            src_ref=other, dst_ref=other,
            send_sem=send_sem.at[stages + s, c], recv_sem=recv_sem.at[stages + s, c], device_id=partner(order[s]),
            device_id_type=MESH)

    def each(body):
        def pair(i, _):
            body(0, 2 * i)
            body(1, 2 * i + 1)
            return 0

        lax.fori_loop(0, chunks // 2, pair, 0)
        if chunks % 2:
            body(0, chunks - 1)

    each(lambda p, c: scatter(0, p, c).start())
    for s in range(stages):
        def step(p, c):
            scatter(s, p, c).wait_recv()
            order = orders[p]
            r0, c0 = place(order, s, False)
            where = (c, pl.ds(r0, sizes[s][0]), pl.ds(c0, sizes[s][1]))
            own = (g_ref if s == 0 else work_ref)[where].astype(F32)
            total = (own + land[s][c].astype(F32)).astype(BF16)
            if s + 1 < stages:
                work_ref[where] = total
                scatter(s + 1, p, c).start()
            else:
                out_ref[where] = total
                gather(s, p, c).start()

        each(step)
    for s in reversed(range(stages)):
        def step(p, c):
            gathered(s, p, c).wait_recv()
            if s > 0:
                gather(s - 1, p, c).start()

        each(step)

    def drain(p, c):
        for s in range(stages):
            scatter(s, p, c).wait_send()
            gather(s, p, c).wait_send()

    each(drain)


def all_sum(g, groups, members):
    orders = bit_orders(groups, members)
    stages = len(orders[0])
    chunks, rows, cols = g.shape
    sizes = region_sizes(stages, rows, cols)
    return pl.pallas_call(
        functools.partial(sum_kernel, orders),
        out_shape=jax.ShapeDtypeStruct(g.shape, BF16),
        in_specs=[pl.BlockSpec(memory_space=pltpu.VMEM)],
        out_specs=pl.BlockSpec(memory_space=pltpu.VMEM),
        scratch_shapes=[pltpu.VMEM((chunks, r, c), BF16) for r, c, _ in sizes]
        + [pltpu.VMEM(g.shape, BF16), pltpu.SemaphoreType.DMA((2 * stages, chunks)), pltpu.SemaphoreType.DMA((2 * stages, chunks))],
        compiler_params=pltpu.CompilerParams(collective_id=0, has_side_effects=True, vmem_limit_bytes=48 << 20),
        name="all_sum",
    )(g)


def rms_scale(values, gain):
    return values * lax.rsqrt(jnp.mean(values * values, axis=-1, keepdims=True) + EPS) * gain


def contract_rows(left, right):
    return lax.dot_general(
        left, right, (((0,), (0,)), ((), ())), preferred_element_type=jnp.float32
    )


def local(
    tokens,
    d_out,
    segment,
    route,
    gain_one,
    w_in,
    conv_w,
    conv_b,
    w_x,
    w_dt,
    b_dt,
    a_log,
    d_skip,
    w_out,
    gain_two,
    w_router,
    w_up,
    w_down,
):
    length, width = tokens.shape
    inner_w = w_in.shape[1] // 2
    experts = w_router.shape[1]
    local_experts = w_up.shape[0]
    groups = lax.axis_size("ep")
    slots = 3 * length // (2 * experts)
    capacity = 5 * length * lax.axis_size("ep") * lax.axis_size("tp") // (4 * experts)
    token_f = tokens.astype(jnp.float32)
    valid = (segment >= 0).astype(jnp.float32)[:, None]
    rank_dt, states = w_dt.shape[0], a_log.shape[0]
    masks = flags(segment)
    vec = jnp.concatenate([conv_w, conv_b[None], b_dt[None], d_skip[None], d_skip[None]], axis=0).astype(F32)
    wx_pad = jnp.pad(w_x, ((0, 0), (0, 128 - rank_dt - 2 * states)))
    wdt_pad = jnp.pad(w_dt, ((0, 128 - rank_dt), (0, 0)))
    rates = -jnp.exp(a_log.astype(F32))
    normed_one, norm_one_pull = jax.vjp(rms_scale, token_f, gain_one.astype(jnp.float32))
    normed_low = normed_one.astype(jnp.bfloat16)
    both = jnp.dot(normed_low, w_in, preferred_element_type=jnp.float32)

    gated_low, pre, pre_dt, scanned, proj, starts = mid_fwd(
        both, masks, vec, wx_pad, wdt_pad, rates * LOG2E, rank_dt
    )
    mixed = jnp.dot(gated_low, w_out, preferred_element_type=jnp.float32)
    after_mix = token_f + mixed * valid
    normed_two, norm_two_pull = jax.vjp(rms_scale, after_mix, gain_two.astype(jnp.float32))
    pick_int = (
        (route == jnp.arange(experts, dtype=jnp.int32)[None, :]) & (segment >= 0)[:, None]
    ).astype(jnp.int32)
    picks = pick_int.astype(jnp.float32)

    def router(normed_in, router_w):
        probs = jax.nn.softmax(jnp.dot(normed_in, router_w, precision=HIGH), axis=-1)
        return jnp.sum(probs * picks, axis=-1)

    gate, router_pull = jax.vjp(router, normed_two, w_router.astype(jnp.float32))
    local_count = jnp.sum(pick_int, axis=0)
    everyone = lax.all_gather(local_count, ("ep", "tp"))
    earlier = jnp.arange(everyone.shape[0]) < lax.axis_index(("ep", "tp"))
    prior = jnp.sum(jnp.where(earlier[:, None], everyone, 0), axis=0)
    named = jnp.sum(everyone, axis=0)
    local_rank = jnp.sum(jnp.cumsum(pick_int, axis=0) * pick_int, axis=1) - 1
    global_rank = jnp.sum(pick_int * prior[None, :], axis=1) + local_rank
    kept = (segment >= 0) & (global_rank < capacity)
    slot_id = jnp.where(kept, route[:, 0] * slots + local_rank, -1)
    dispatch = (jnp.arange(experts * slots, dtype=jnp.int32)[:, None] == slot_id[None, :]).astype(
        jnp.bfloat16
    )
    expert_in = normed_two.astype(jnp.bfloat16)
    outgoing = jnp.dot(dispatch, expert_in, preferred_element_type=jnp.float32).astype(jnp.bfloat16)
    outgoing = outgoing.reshape(groups, local_experts, slots, width)
    received = lax.all_to_all(outgoing, "ep", split_axis=0, concat_axis=2, tiled=True)
    full_up, full_down = (w_up, w_down)
    expert_rows = lax.all_gather(received, "tp", axis=2, tiled=True)
    hidden_pre = jnp.einsum(
        "axrd,xdf->axrf", expert_rows, full_up, preferred_element_type=jnp.float32
    )
    gelu_value, gelu_pull = jax.vjp(partial(jax.nn.gelu, approximate=False), hidden_pre)
    hidden_low = gelu_value.astype(jnp.bfloat16)
    terms = jnp.einsum("axrf,xfd->axrd", hidden_low, full_down, preferred_element_type=jnp.float32)
    expert_out = lax.psum_scatter(terms, "tp", scatter_dimension=2, tiled=True)
    returned = lax.all_to_all(
        expert_out.astype(jnp.bfloat16), "ep", split_axis=2, concat_axis=0, tiled=True
    )
    returned = returned.reshape(experts * slots, width)
    token_out = contract_rows(dispatch, returned)
    keep_f = kept.astype(jnp.float32)[:, None]
    weighting = gate[:, None] * keep_f
    final = after_mix + weighting * token_out
    upstream = d_out.astype(jnp.float32)
    d_token_out = (weighting * upstream).astype(jnp.bfloat16)
    d_slots = jnp.dot(dispatch, d_token_out, preferred_element_type=jnp.float32).astype(
        jnp.bfloat16
    )
    d_slots = d_slots.reshape(groups, local_experts, slots, width)
    d_gate = keep_f[:, 0] * jnp.sum(upstream * token_out, axis=1)
    d_received = lax.all_to_all(d_slots, "ep", split_axis=0, concat_axis=2, tiled=True)
    d_rows_all = lax.all_gather(d_received, "tp", axis=2, tiled=True)
    gelu_back, hidden_back = gelu_pull, hidden_low
    grad_down = jnp.einsum(
        "axrf,axrd->xfd", hidden_back, d_rows_all, preferred_element_type=jnp.float32
    )
    d_hidden = jnp.einsum(
        "axrd,xfd->axrf", d_rows_all, full_down, preferred_element_type=jnp.float32
    )
    d_pre = gelu_back(d_hidden)[0].astype(jnp.bfloat16)
    grad_up = jnp.einsum("axrd,axrf->xdf", expert_rows, d_pre, preferred_element_type=jnp.float32)
    row_terms = jnp.einsum("axrf,xdf->axrd", d_pre, full_up, preferred_element_type=jnp.float32)
    d_expert_in = lax.psum_scatter(row_terms, "tp", scatter_dimension=2, tiled=True)
    d_back = lax.all_to_all(
        d_expert_in.astype(jnp.bfloat16), "ep", split_axis=2, concat_axis=0, tiled=True
    )
    d_normed = contract_rows(dispatch, d_back.reshape(experts * slots, width))
    d_norm_router, grad_router = router_pull(d_gate)
    d_after, grad_gain_two = norm_two_pull(d_normed + d_norm_router)
    d_after = d_after + upstream
    d_mixed = (d_after * valid).astype(jnp.bfloat16)
    grad_out = contract_rows(gated_low, d_mixed)
    d_gated = lax.dot_general(
        d_mixed, w_out, (((1,), (1,)), ((), ())), preferred_element_type=jnp.float32
    )
    d_both, grad_vec, grad_x, grad_dt, grad_rates = mid_bwd(
        both, d_gated, pre, pre_dt, scanned, proj, starts, masks, vec, wx_pad.T, wdt_pad, rates * LOG2E, rank_dt
    )
    grad_in = contract_rows(normed_low, d_both)
    d_normed_one = lax.dot_general(
        d_both, w_in, (((1,), (1,)), ((), ())), preferred_element_type=jnp.float32
    )
    d_tokens_norm, grad_gain_one = norm_one_pull(d_normed_one)
    d_tokens = d_after + d_tokens_norm
    counts = jnp.stack([named, jnp.maximum(named - capacity, 0)])
    used = rank_dt + 2 * states
    small = jnp.concatenate(
        [
            grad_x[:used],
            grad_dt[:rank_dt],
            grad_rates * rates,
            grad_vec,
            jnp.concatenate([grad_gain_one, grad_gain_two])[None],
            grad_router.T.reshape(-1, inner_w),
        ],
        axis=0,
    )
    rows_used = small.shape[0]
    small = jnp.pad(small, ((0, 256 - rows_used), (0, 0))).T
    tall = grad_in.astype(jnp.bfloat16).reshape(width // 256, 256, 2 * inner_w // 1024, 1024)
    tall = tall.transpose(0, 2, 1, 3).reshape(-1, 256, 1024)
    wide = jnp.concatenate([grad_out.astype(jnp.bfloat16), small.astype(jnp.bfloat16)], axis=1)
    summed = all_sum(jnp.concatenate([tall, wide.reshape(-1, 256, 1024)], axis=0), groups, lax.axis_size("tp"))
    total_in = summed[: tall.shape[0]].reshape(width // 256, 2 * inner_w // 1024, 256, 1024)
    total_in = total_in.transpose(0, 2, 1, 3).reshape(width, 2 * inner_w).astype(jnp.float32)
    wide = summed[tall.shape[0] :].reshape(inner_w, 1024)
    total_out = wide[:, :width].astype(jnp.float32)
    small = wide[:, width:].astype(jnp.float32).T
    at = used + rank_dt + states
    taps = conv_w.shape[0]
    gains = small[at + 8].reshape(2, width)
    return (
        final.astype(jnp.bfloat16),
        d_tokens,
        counts,
        gains[0],
        total_in,
        small[at : at + taps],
        small[at + taps],
        small[:used].T,
        small[used : used + rank_dt],
        small[at + taps + 1],
        small[used + rank_dt : at],
        small[at + taps + 2],
        total_out,
        gains[1],
        small[at + 9 : rows_used].reshape(experts, width).T,
        grad_up,
        grad_down,
    )


def solution(mesh):
    in_specs = (
        P(("ep", "tp"), None),
        P(("ep", "tp"), None),
        P(("ep", "tp")),
        P(("ep", "tp"), None),
        P(),
        P(),
        P(),
        P(),
        P(),
        P(),
        P(),
        P(),
        P(),
        P(),
        P(),
        P(),
        P("ep", None, "tp"),
        P("ep", "tp", None),
    )
    out_specs = (
        P(("ep", "tp"), None),
        P(("ep", "tp"), None),
        P(),
        P(),
        P(),
        P(),
        P(),
        P(),
        P(),
        P(),
        P(),
        P(),
        P(),
        P(),
        P(),
        P("ep", None, "tp"),
        P("ep", "tp", None),
    )
    return jax.shard_map(local, mesh=mesh, in_specs=in_specs, out_specs=out_specs, check_vma=False)
```

```python
import functools

import jax
import jax.numpy as jnp
from jax import lax
from jax.experimental import pallas as pl
from jax.experimental.pallas import tpu as pltpu
from jax.sharding import PartitionSpec as P

EPS = 1e-06
HIGH = lax.Precision.HIGHEST
MESH = pl.DeviceIdType.MESH
TB = 128
CH = 16
LB = 512
LOG2E = 1.4426950408889634
LN2 = 0.6931471805599453
F32 = jnp.float32
BF16 = jnp.bfloat16
NN = (((1,), (0,)), ((), ()))
NT = (((1,), (1,)), ((), ()))
TN = (((0,), (0,)), ((), ()))


def mxu(left, right, dims):
    return lax.dot_general(left, right, dims, preferred_element_type=F32)


def split(x):
    high = x.astype(BF16)
    return high, (x - high.astype(F32)).astype(BF16)


def dot2(x, w, dims):
    high, rest = split(x)
    return mxu(high, w, dims) + mxu(rest, w, dims)


def dot3(x, w, dims):
    high, rest = split(x)
    high_w, rest_w = split(w)
    return mxu(high, high_w, dims) + mxu(high, rest_w, dims) + mxu(rest, high_w, dims)


def sigmoid(x):
    return 1.0 / (1.0 + jnp.exp(-x))


def softplus(x):
    return jnp.maximum(x, 0.0) + jnp.log1p(jnp.exp(-jnp.abs(x)))


def mid_fwd_kernel(rank, both_ref, mask_ref, vec_ref, wx_ref, wdt_ref, rates_ref,
                   gated_ref, pre_ref, pdt_ref, y_ref, proj_ref, hs_ref,
                   ext_ref, conv_ref, h_ref, turned_ref):
    states, width = rates_ref.shape

    @pl.when(pl.program_id(0) == 0)
    def _():
        ext_ref[:8, :] = jnp.zeros((8, width), F32)
        h_ref[...] = jnp.zeros_like(h_ref)

    @pl.when(pl.program_id(0) > 0)
    def _():
        ext_ref[:8, :] = ext_ref[TB:, :]

    def conv_chunk(c, _):
        rows = pl.ds(pl.multiple_of(c * CH, CH), CH)
        masks = mask_ref[rows, :]
        for b in range(width // LB):
            lanes = slice(b * LB, (b + 1) * LB)
            ext_ref[pl.ds(pl.multiple_of(c * CH + 8, 8), CH), lanes] = both_ref[rows, lanes]
            window = ext_ref[pl.ds(pl.multiple_of(c * CH, 8), CH + 8), lanes]
            total = vec_ref[4:5, lanes] + vec_ref[3:4, lanes] * window[8:]
            for k in range(1, 4):
                total = total + vec_ref[3 - k:4 - k, lanes] * window[8 - k:8 - k + CH] * masks[:, k - 1:k]
            pre_ref[rows, lanes] = total
            conv_ref[rows, lanes] = total * sigmoid(total)
        return 0

    lax.fori_loop(0, TB // CH, conv_chunk, 0)
    proj = dot2(conv_ref[...], wx_ref[...], NN)
    proj_ref[...] = proj
    turned_ref[...] = proj.T
    pdt_ref[...] = dot2(proj, wdt_ref[...], NN) + vec_ref[5:6, :]

    def scan_chunk(c, _):
        rows = pl.ds(pl.multiple_of(c * CH, CH), CH)
        tile = pltpu.roll(turned_ref[rank:rank + 2 * states, :], TB - c * CH, 1)
        keep = mask_ref[rows, 0:1]
        for b in range(width // LB):
            lanes = slice(b * LB, (b + 1) * LB)
            rates = rates_ref[:, lanes]
            h = h_ref[:, lanes]
            hs_ref[c, :, lanes] = h
            conv = conv_ref[rows, lanes]
            step = softplus(pdt_ref[rows, lanes])
            source = step * conv
            step = jnp.where(keep > 0.0, step, 1e4)
            outs = []
            for k in range(CH):
                h = jnp.exp2(step[k:k + 1, :] * rates) * h + tile[:states, k:k + 1] * source[k:k + 1, :]
                outs.append(jnp.sum(tile[states:, k:k + 1] * h, axis=0, keepdims=True))
            h_ref[:, lanes] = h
            y = jnp.concatenate(outs, axis=0)
            y_ref[rows, lanes] = y
            gate = both_ref[rows, width + b * LB:width + (b + 1) * LB]
            gated_ref[rows, lanes] = ((y + vec_ref[6:7, lanes] * conv) * (gate * sigmoid(gate))).astype(BF16)
        return 0

    lax.fori_loop(0, TB // CH, scan_chunk, 0)


def mid_fwd(both, masks, vec, wx, wdt, rates, rank):
    length = both.shape[0]
    states, width = rates.shape
    row = lambda i: (i, 0)
    fix = lambda i: (0, 0)
    tall = pl.BlockSpec((TB, width), row)
    like = jax.ShapeDtypeStruct((length, width), F32)
    return pl.pallas_call(
        functools.partial(mid_fwd_kernel, rank),
        grid=(length // TB,),
        out_shape=(jax.ShapeDtypeStruct((length, width), BF16), like, like, like,
                   jax.ShapeDtypeStruct((length, 128), F32),
                   jax.ShapeDtypeStruct((length // CH, states, width), F32)),
        in_specs=[pl.BlockSpec((TB, 2 * width), row), pl.BlockSpec((TB, 8), row), pl.BlockSpec(vec.shape, fix),
                  pl.BlockSpec(wx.shape, fix), pl.BlockSpec(wdt.shape, fix), pl.BlockSpec(rates.shape, fix)],
        out_specs=(tall, tall, tall, tall, pl.BlockSpec((TB, 128), row),
                   pl.BlockSpec((TB // CH, states, width), lambda i: (i, 0, 0))),
        scratch_shapes=[pltpu.VMEM((TB + 8, width), F32), pltpu.VMEM((TB, width), F32),
                        pltpu.VMEM((states, width), F32), pltpu.VMEM((128, TB), F32)],
        compiler_params=pltpu.CompilerParams(vmem_limit_bytes=40 << 20),
        name="mid_fwd",
    )(both, masks, vec, wx, wdt, rates)


def mid_bwd_kernel(rank, both_ref, dg_ref, pre_ref, pdt_ref, y_ref, proj_ref, hs_ref, mask_ref, vec_ref, wxt_ref,
                   wdt_ref, rates_ref,
                   dboth_ref, gvec_ref, gwx_ref, gwdt_ref, gr_ref,
                   ext_ref, g_ref, dec_ref, p_ref, part_ref, dproj_ref, dconv_ref, dpdt_ref, conv_ref, turned_ref,
                   acc_ref):
    states, width = rates_ref.shape
    steps = TB // CH

    @pl.when(pl.program_id(0) == 0)
    def _():
        ext_ref[TB:, :] = jnp.zeros((8, width), F32)
        g_ref[...] = jnp.zeros_like(g_ref)
        acc_ref[...] = jnp.zeros_like(acc_ref)
        gwx_ref[...] = jnp.zeros_like(gwx_ref)
        gwdt_ref[...] = jnp.zeros_like(gwdt_ref)
        gr_ref[...] = jnp.zeros_like(gr_ref)

    @pl.when(pl.program_id(0) > 0)
    def _():
        ext_ref[TB:, :] = ext_ref[:8, :]

    turned_ref[...] = proj_ref[...].T
    ones = jnp.ones((128, 128), BF16)
    lane = lax.broadcasted_iota(jnp.int32, (2 * states, 128), 1)
    place = lax.broadcasted_iota(jnp.int32, (2 * states, 128), 0) + rank

    def fold(x):
        out = x[:, :128]
        for i in range(1, LB // 128):
            out = out + x[:, i * 128:(i + 1) * 128]
        return out

    def halves(x):
        out = x[:8]
        for i in range(1, CH // 8):
            out = out + x[i * 8:(i + 1) * 8]
        return out

    def scan_chunk(i, _):
        c = steps - 1 - i
        rows = pl.ds(pl.multiple_of(c * CH, CH), CH)
        tile = pltpu.roll(turned_ref[rank:rank + 2 * states, :], TB - c * CH, 1)
        keep = mask_ref[rows, 0:1]
        for b in range(width // LB):
            lanes = slice(b * LB, (b + 1) * LB)
            rates = rates_ref[:, lanes]
            h = hs_ref[c, :, lanes]
            pre = pre_ref[rows, lanes]
            conv = pre * sigmoid(pre)
            conv_ref[rows, lanes] = conv
            pdt = pdt_ref[rows, lanes]
            step = softplus(pdt)
            source = step * conv
            decay_step = jnp.where(keep > 0.0, step, 1e4)
            skip = vec_ref[6:7, lanes]
            gate = both_ref[rows, width + b * LB:width + (b + 1) * LB]
            sig = sigmoid(gate)
            dg = dg_ref[rows, lanes]
            dboth_ref[rows, width + b * LB:width + (b + 1) * LB] = (
                dg * (y_ref[rows, lanes] + skip * conv) * (sig * (1.0 + gate * (1.0 - sig)))).astype(BF16)
            dy = dg * (gate * sig)
            for k in range(CH):
                dec = jnp.exp2(decay_step[k:k + 1, :] * rates)
                p = dec * h
                dec_ref[k] = dec
                p_ref[k] = p
                h = p + tile[:states, k:k + 1] * source[k:k + 1, :]
                out = fold(dy[k:k + 1, :] * h)
                part_ref[k, states:, :] = out if b == 0 else part_ref[k, states:, :] + out
            g = g_ref[:, lanes]
            dr = gr_ref[:, lanes]
            dus, dss = [None] * CH, [None] * CH
            for k in reversed(range(CH)):
                dh = g + tile[states:, k:k + 1] * dy[k:k + 1, :]
                out = fold(dh * source[k:k + 1, :])
                part_ref[k, :states, :] = out if b == 0 else part_ref[k, :states, :] + out
                dus[k] = jnp.sum(dh * tile[:states, k:k + 1], axis=0, keepdims=True)
                da = dh * p_ref[k]
                dss[k] = jnp.sum(da * rates, axis=0, keepdims=True)
                dr = dr + da * decay_step[k:k + 1, :]
                g = dec_ref[k] * dh
            g_ref[:, lanes] = g
            gr_ref[:, lanes] = dr
            du = jnp.concatenate(dus, axis=0)
            dpdt = (jnp.concatenate(dss, axis=0) * LN2 + du * conv) * sigmoid(pdt)
            dpdt_ref[rows, lanes] = dpdt
            dconv_ref[rows, lanes] = dy * skip + du * step
            acc_ref[5, :, lanes] += halves(dpdt)
            acc_ref[6, :, lanes] += halves(dy * conv)
        high, rest = split(part_ref[...].reshape(CH * 2 * states, 128))
        sums = (mxu(high, ones, NN) + mxu(rest, ones, NN)).reshape(CH, 2 * states, 128)
        picked = jnp.where((lane == place)[None], sums, 0.0)
        dproj_ref[rows, :] = jnp.sum(picked, axis=1)
        return 0

    lax.fori_loop(0, steps, scan_chunk, 0)
    dpdt = dpdt_ref[...]
    dproj = dproj_ref[...] + dot2(dpdt, wdt_ref[...], NT)
    gwdt_ref[...] += dot3(turned_ref[...], dpdt, NN)
    gwx_ref[...] += dot3(dproj.T, conv_ref[...], NN)
    dconv_ref[...] += dot2(dproj, wxt_ref[...], NN)

    def act_chunk(c, _):
        rows = pl.ds(pl.multiple_of(c * CH, CH), CH)
        for b in range(width // LB):
            lanes = slice(b * LB, (b + 1) * LB)
            pre = pre_ref[rows, lanes]
            sig = sigmoid(pre)
            ext_ref[rows, lanes] = dconv_ref[rows, lanes] * (sig * (1.0 + pre * (1.0 - sig)))
        return 0

    lax.fori_loop(0, steps, act_chunk, 0)

    def conv_chunk(c, _):
        rows = pl.ds(pl.multiple_of(c * CH, CH), CH)
        masks = mask_ref[rows, :]
        for b in range(width // LB):
            lanes = slice(b * LB, (b + 1) * LB)
            inner = both_ref[rows, lanes]
            window = ext_ref[pl.ds(pl.multiple_of(c * CH, 8), CH + 8), lanes]
            here = window[:CH]
            total = vec_ref[3:4, lanes] * here
            acc_ref[4, :, lanes] += halves(here)
            acc_ref[3, :, lanes] += halves(here * inner)
            for k in range(1, 4):
                later = window[k:k + CH] * masks[:, 2 + k:3 + k]
                total = total + vec_ref[3 - k:4 - k, lanes] * later
                acc_ref[3 - k, :, lanes] += halves(later * inner)
            dboth_ref[rows, lanes] = total.astype(BF16)
        return 0

    lax.fori_loop(0, steps, conv_chunk, 0)

    @pl.when(pl.program_id(0) == pl.num_programs(0) - 1)
    def _():
        gvec_ref[...] = jnp.concatenate(
            [jnp.sum(acc_ref[k], axis=0, keepdims=True) for k in range(8)], axis=0)


def mid_bwd(both, dg, pre, pdt, y, proj, hs, masks, vec, wxt, wdt, rates, rank):
    length = both.shape[0]
    states, width = rates.shape
    blocks = length // TB
    row = lambda i: (blocks - 1 - i, 0)
    fix = lambda i: (0, 0)
    tall = pl.BlockSpec((TB, width), row)
    return pl.pallas_call(
        functools.partial(mid_bwd_kernel, rank),
        grid=(blocks,),
        out_shape=(jax.ShapeDtypeStruct((length, 2 * width), BF16), jax.ShapeDtypeStruct((8, width), F32),
                   jax.ShapeDtypeStruct((128, width), F32), jax.ShapeDtypeStruct((128, width), F32),
                   jax.ShapeDtypeStruct((states, width), F32)),
        in_specs=[pl.BlockSpec((TB, 2 * width), row), tall, tall, tall, tall, pl.BlockSpec((TB, 128), row),
                  pl.BlockSpec((TB // CH, states, width), lambda i: (blocks - 1 - i, 0, 0)),
                  pl.BlockSpec((TB, 8), row), pl.BlockSpec(vec.shape, fix), pl.BlockSpec(wxt.shape, fix),
                  pl.BlockSpec(wdt.shape, fix), pl.BlockSpec(rates.shape, fix)],
        out_specs=(pl.BlockSpec((TB, 2 * width), row), pl.BlockSpec((8, width), fix),
                   pl.BlockSpec((128, width), fix), pl.BlockSpec((128, width), fix), pl.BlockSpec((states, width), fix)),
        scratch_shapes=[pltpu.VMEM((TB + 8, width), F32), pltpu.VMEM((states, width), F32),
                        pltpu.VMEM((CH, states, LB), F32), pltpu.VMEM((CH, states, LB), F32),
                        pltpu.VMEM((CH, 2 * states, 128), F32), pltpu.VMEM((TB, 128), F32),
                        pltpu.VMEM((TB, width), F32), pltpu.VMEM((TB, width), F32), pltpu.VMEM((TB, width), F32),
                        pltpu.VMEM((128, TB), F32), pltpu.VMEM((8, 8, width), F32)],
        compiler_params=pltpu.CompilerParams(vmem_limit_bytes=56 << 20),
        name="mid_bwd",
    )(both, dg, pre, pdt, y, proj, hs, masks, vec, wxt, wdt, rates)


def flags(segment):
    length = segment.shape[0]
    cols = []
    for k in range(1, 4):
        moved = jnp.concatenate([jnp.full((k,), -2, jnp.int32), segment[:length - k]])
        cols.append(moved == segment)
    for k in range(1, 4):
        moved = jnp.concatenate([segment[k:], jnp.full((k,), -2, jnp.int32)])
        cols.append(moved == segment)
    cols.append(segment >= 0)
    cols.append(segment >= 0)
    return jnp.stack(cols, axis=1).astype(F32)


def bit_orders(groups, members):
    ep_bits, tp_bits = groups.bit_length() - 1, members.bit_length() - 1
    x = [("ep", b) for b in range(ep_bits - 2)]
    z = [("ep", b) for b in range(ep_bits - 2, ep_bits)]
    y = [("tp", b) for b in range(1, tp_bits)]
    core = [("tp", 0)]
    return [core + x + y + z, core + y + x + z]


def region_sizes(stages, rows, cols):
    sizes = []
    for _ in range(stages):
        if rows > 16:
            rows //= 2
            sizes.append((rows, cols, True))
        else:
            cols //= 2
            sizes.append((rows, cols, False))
    return sizes


CHUNK = (256, 1024)


def sum_kernel(orders, tall_ref, wide_ref, tall_out, wide_out, *rest):
    stages = len(orders[0])
    land = rest[:stages]
    work_ref, send_sem, recv_sem = rest[stages:]
    sizes = region_sizes(stages, *CHUNK)
    across = tall_ref.shape[1] // CHUNK[1]
    split_at = across * (tall_ref.shape[0] // CHUNK[0])
    chunks = split_at + wide_ref.shape[0] // CHUNK[0]
    me = {"ep": lax.axis_index("ep"), "tp": lax.axis_index("tp")}

    def bit(stage):
        axis, b = stage
        return lax.rem(me[axis] // (1 << b), 2)

    def partner(stage):
        axis, b = stage
        there = dict(me)
        there[axis] = me[axis] + (1 << b) - 2 * (1 << b) * bit(stage)
        return (there["ep"], there["tp"])

    barrier = pltpu.get_barrier_semaphore()
    for stage in orders[0]:
        pl.semaphore_signal(barrier, inc=1, device_id=partner(stage), device_id_type=MESH)
    pl.semaphore_wait(barrier, stages)

    def window(order, upto, flip):
        r0, c0 = 0, 0
        for s in range(upto + 1):
            b = bit(order[s])
            if s == upto and flip:
                b = 1 - b
            if sizes[s][2]:
                r0 = r0 + b * sizes[s][0]
            else:
                c0 = c0 + b * sizes[s][1]
        return r0, c0

    def in_work(c, order, upto, flip):
        r0, c0 = window(order, upto, flip)
        return (c, pl.ds(pl.multiple_of(r0, 16), sizes[upto][0]),
                pl.ds(c0 if isinstance(c0, int) else pl.multiple_of(c0, 128), sizes[upto][1]))

    def in_array(tall, c, order, upto, flip):
        r0, c0 = window(order, upto, flip)
        if tall:
            r0 = r0 + (c // across) * CHUNK[0]
            c0 = c0 + lax.rem(c, across) * CHUNK[1]
        else:
            r0 = r0 + (c - split_at) * CHUNK[0]
        return (pl.ds(pl.multiple_of(r0, 16), sizes[upto][0]),
                pl.ds(c0 if isinstance(c0, int) else pl.multiple_of(c0, 128), sizes[upto][1]))

    def scatter(s, tall, p, c):
        order = orders[p]
        if s == 0:
            src = (tall_ref if tall else wide_ref).at[in_array(tall, c, order, s, True)]
        else:
            src = work_ref.at[in_work(c, order, s, True)]
        return pltpu.make_async_remote_copy(
            src_ref=src, dst_ref=land[s].at[c], send_sem=send_sem.at[s, c], recv_sem=recv_sem.at[s, c],
            device_id=partner(order[s]), device_id_type=MESH)

    def gather(s, tall, p, c, flip=False):
        order = orders[p]
        piece = (tall_out if tall else wide_out).at[in_array(tall, c, order, s, flip)]
        return pltpu.make_async_remote_copy(
            src_ref=piece, dst_ref=piece, send_sem=send_sem.at[stages + s, c], recv_sem=recv_sem.at[stages + s, c],
            device_id=partner(order[s]), device_id_type=MESH)

    def each(body):
        for tall, low, high in ((True, 0, split_at), (False, split_at, chunks)):
            def pair(i, _, tall=tall, low=low):
                body(tall, 0, low + 2 * i)
                body(tall, 1, low + 2 * i + 1)
                return 0

            lax.fori_loop(0, (high - low) // 2, pair, 0)
            if (high - low) % 2:
                body(tall, 0, high - 1)

    each(lambda tall, p, c: scatter(0, tall, p, c).start())
    for s in range(stages):
        def step(tall, p, c):
            scatter(s, tall, p, c).wait_recv()
            order = orders[p]
            if s == 0:
                own = (tall_ref if tall else wide_ref)[in_array(tall, c, order, s, False)]
            else:
                own = work_ref[in_work(c, order, s, False)]
            total = (own.astype(F32) + land[s][c].astype(F32)).astype(BF16)
            if s + 1 < stages:
                work_ref[in_work(c, order, s, False)] = total
                scatter(s + 1, tall, p, c).start()
            else:
                (tall_out if tall else wide_out)[in_array(tall, c, order, s, False)] = total
                gather(s, tall, p, c).start()

        each(step)
    for s in reversed(range(stages)):
        def step(tall, p, c):
            gather(s, tall, p, c, True).wait_recv()
            if s > 0:
                gather(s - 1, tall, p, c).start()

        each(step)

    def drain(tall, p, c):
        for s in range(stages):
            scatter(s, tall, p, c).wait_send()
            gather(s, tall, p, c).wait_send()

    each(drain)


def all_sum(tall, wide, groups, members):
    orders = bit_orders(groups, members)
    stages = len(orders[0])
    chunks = tall.size // (CHUNK[0] * CHUNK[1]) + wide.size // (CHUNK[0] * CHUNK[1])
    vmem = pl.BlockSpec(memory_space=pltpu.VMEM)
    return pl.pallas_call(
        functools.partial(sum_kernel, orders),
        out_shape=(jax.ShapeDtypeStruct(tall.shape, BF16), jax.ShapeDtypeStruct(wide.shape, BF16)),
        in_specs=[vmem, vmem],
        out_specs=(vmem, vmem),
        scratch_shapes=[pltpu.VMEM((chunks, r, c), BF16) for r, c, _ in region_sizes(stages, *CHUNK)]
        + [pltpu.VMEM((chunks,) + CHUNK, BF16), pltpu.SemaphoreType.DMA((2 * stages, chunks)),
           pltpu.SemaphoreType.DMA((2 * stages, chunks))],
        compiler_params=pltpu.CompilerParams(collective_id=0, has_side_effects=True, vmem_limit_bytes=48 << 20),
        name="all_sum",
    )(tall, wide)


def entry_barrier(groups, chips):
    e, t = lax.axis_index("ep"), lax.axis_index("tp")
    y, c = t // 2, lax.rem(t, 2)
    barrier = pltpu.get_barrier_semaphore()
    for k in range(1, groups):
        pl.semaphore_signal(barrier, inc=1, device_id=(lax.rem(e + k, groups), t), device_id_type=MESH)
    for k in range(1, chips):
        pl.semaphore_signal(barrier, inc=1, device_id=(e, lax.rem(y + k, chips) * 2 + c), device_id_type=MESH)
    pl.semaphore_signal(barrier, inc=1, device_id=(e, t + 1 - 2 * c), device_id_type=MESH)
    pl.semaphore_wait(barrier, groups + chips - 1)
    return e, t, y, c


def dispatch_kernel(groups, chips, rows_ref, count_ref, out_ref, table_ref,
                    own_sem, far_send, far_recv, row_send, row_recv, pair_send, pair_recv):
    e, t, y, c = entry_barrier(groups, chips)
    held = rows_ref.shape[1] // groups
    sibling = (e, t + 1 - 2 * c)

    def block(kind, ref, i, member):
        return ref.at[:, :, member, i] if kind == 0 else ref.at[member, i]

    kinds = ((0, rows_ref, out_ref), (1, count_ref, table_ref))

    def mine(kind, src, peer):
        return src.at[:, pl.ds(peer * held, held)] if kind == 0 else src

    def far(kind, src, dst, peer, source):
        return pltpu.make_async_remote_copy(
            src_ref=mine(kind, src, peer), dst_ref=block(kind, dst, source, t), send_sem=far_send.at[kind, peer],
            recv_sem=far_recv.at[kind, source], device_id=(peer, t), device_id_type=MESH)

    def across(kind, dst, i, to, source):
        there = block(kind, dst, i, source * 2 + c)
        return pltpu.make_async_remote_copy(
            src_ref=there, dst_ref=there, send_sem=row_send.at[kind, i, to], recv_sem=row_recv.at[kind, i, source],
            device_id=(e, to * 2 + c), device_id_type=MESH)

    def beside(kind, dst, i, source, core):
        there = block(kind, dst, i, source * 2 + core)
        return pltpu.make_async_remote_copy(
            src_ref=there, dst_ref=there, send_sem=pair_send.at[kind, i, source],
            recv_sem=pair_recv.at[kind, i, source], device_id=sibling, device_id_type=MESH)

    for kind, src, dst in kinds:
        pltpu.make_async_copy(mine(kind, src, e), block(kind, dst, e, t), own_sem.at[kind]).start()

    def send(k, _):
        peer = lax.rem(e + k, groups)
        for kind, src, dst in kinds:
            far(kind, src, dst, peer, e).start()
        return 0

    lax.fori_loop(1, groups, send, 0)
    for kind, src, dst in kinds:
        pltpu.make_async_copy(mine(kind, src, e), block(kind, dst, e, t), own_sem.at[kind]).wait()

    def pass_on(i):
        for kind, src, dst in kinds:
            for k in range(1, chips):
                across(kind, dst, i, lax.rem(y + k, chips), y).start()
            beside(kind, dst, i, y, c).start()

    def hand_over(i):
        for kind, src, dst in kinds:
            for k in range(1, chips):
                source = lax.rem(y + k, chips)
                across(kind, dst, i, source, source).wait_recv()
                beside(kind, dst, i, source, c).start()

    pass_on(e)

    def middle(k, _):
        i = lax.rem(e + groups - k, groups)
        for kind, src, dst in kinds:
            far(kind, src, dst, i, i).wait_recv()
        pass_on(i)
        hand_over(lax.rem(i + 1, groups))
        return 0

    lax.fori_loop(1, groups, middle, 0)
    hand_over(lax.rem(e + 1, groups))

    def finish(k, _):
        i = lax.rem(e + groups - k, groups)
        for kind, src, dst in kinds:
            for source in range(chips):
                beside(kind, dst, i, source, 1 - c).wait_recv()
                beside(kind, dst, i, source, c).wait_send()
            for j in range(1, chips):
                across(kind, dst, i, lax.rem(y + j, chips), y).wait_send()
        return 0

    lax.fori_loop(0, groups, finish, 0)

    def drain(k, _):
        peer = lax.rem(e + k, groups)
        for kind, src, dst in kinds:
            far(kind, src, dst, peer, e).wait_send()
        return 0

    lax.fori_loop(1, groups, drain, 0)


def dispatch(rows, count, groups, members):
    kinds, experts, slots, width = rows.shape
    chips = members // 2
    any_space = pl.BlockSpec(memory_space=pl.ANY)
    dma = pltpu.SemaphoreType.DMA
    return pl.pallas_call(
        functools.partial(dispatch_kernel, groups, chips),
        out_shape=(jax.ShapeDtypeStruct((kinds, experts // groups, members, groups, slots, width), BF16),
                   jax.ShapeDtypeStruct((members, groups) + count.shape, jnp.int32)),
        in_specs=[any_space, any_space],
        out_specs=(any_space, any_space),
        scratch_shapes=[dma((2,)), dma((2, groups)), dma((2, groups)), dma((2, groups, chips)), dma((2, groups, chips)),
                        dma((2, groups, chips)), dma((2, groups, chips))],
        compiler_params=pltpu.CompilerParams(collective_id=1, has_side_effects=True),
        name="dispatch",
    )(rows, count)


def collect_kernel(groups, chips, part_ref, out_ref, own_ref, pair_ref, row_ref, ready_ref,
                   own_sem, last_sem, pair_send, pair_recv, row_send, row_recv, far_send, far_recv):
    e, t, y, c = entry_barrier(groups, chips)
    kinds, held = part_ref.shape[:2]
    sibling = (e, t + 1 - 2 * c)

    def local(i, to):
        return pltpu.make_async_copy(part_ref.at[:, :, to * 2 + c, i], own_ref.at[to, i], own_sem.at[to, i])

    def beside(i, to):
        return pltpu.make_async_remote_copy(
            src_ref=part_ref.at[:, :, to * 2 + 1 - c, i], dst_ref=pair_ref.at[to, i], send_sem=pair_send.at[to, i],
            recv_sem=pair_recv.at[to, i], device_id=sibling, device_id_type=MESH)

    def across(i, to, source):
        return pltpu.make_async_remote_copy(
            src_ref=own_ref.at[to, i], dst_ref=row_ref.at[source, i], send_sem=row_send.at[to, i],
            recv_sem=row_recv.at[source, i], device_id=(e, to * 2 + c), device_id_type=MESH)

    def far(i, source):
        return pltpu.make_async_remote_copy(
            src_ref=ready_ref.at[i], dst_ref=out_ref.at[:, pl.ds(source * held, held)], send_sem=far_send.at[i],
            recv_sem=far_recv.at[source], device_id=(i, t), device_id_type=MESH)

    def turn(k):
        return lax.rem(e + k, groups)

    def start(k, _):
        i = turn(k)
        for j in range(1, chips + 1):
            to = lax.rem(y + j, chips)
            local(i, to).start()
            beside(i, to).start()
        return 0

    lax.fori_loop(1, groups + 1, start, 0)

    def first(k, _):
        i = turn(k)
        for j in range(1, chips):
            to = lax.rem(y + j, chips)
            local(i, to).wait()
            beside(i, to).wait_recv()
            for a in range(kinds):
                for x in range(held):
                    own_ref[to, i, a, x] = (own_ref[to, i, a, x].astype(F32) + pair_ref[to, i, a, x].astype(F32)).astype(BF16)
            across(i, to, y).start()
        local(i, y).wait()
        beside(i, y).wait_recv()
        return 0

    lax.fori_loop(1, groups + 1, first, 0)

    def total(i):
        for j in range(1, chips):
            source = lax.rem(y + j, chips)
            across(i, source, source).wait_recv()
        for a in range(kinds):
            for x in range(held):
                value = own_ref[y, i, a, x].astype(F32) + pair_ref[y, i, a, x].astype(F32)
                for j in range(1, chips):
                    value = value + row_ref[lax.rem(y + j, chips), i, a, x].astype(F32)
                ready_ref[i, a, x] = value.astype(BF16)

    def second(k, _):
        i = turn(k)
        total(i)
        far(i, e).start()
        return 0

    lax.fori_loop(1, groups, second, 0)
    total(e)
    last = pltpu.make_async_copy(ready_ref.at[e], out_ref.at[:, pl.ds(e * held, held)], last_sem)
    last.start()

    def finish(k, _):
        i = turn(k)
        far(i, e).wait_send()
        far(i, i).wait_recv()
        return 0

    lax.fori_loop(1, groups, finish, 0)

    def drain(k, _):
        i = turn(k)
        for j in range(1, chips + 1):
            beside(i, lax.rem(y + j, chips)).wait_send()
        for j in range(1, chips):
            across(i, lax.rem(y + j, chips), y).wait_send()
        return 0

    lax.fori_loop(1, groups + 1, drain, 0)
    last.wait()


def collect(parts, groups, members):
    kinds, held, _, _, slots, width = parts.shape
    chips = members // 2
    any_space = pl.BlockSpec(memory_space=pl.ANY)
    dma = pltpu.SemaphoreType.DMA
    block = (kinds, held, slots, width)
    return pl.pallas_call(
        functools.partial(collect_kernel, groups, chips),
        out_shape=jax.ShapeDtypeStruct((kinds, held * groups, slots, width), BF16),
        in_specs=[any_space],
        out_specs=any_space,
        scratch_shapes=[pltpu.VMEM((chips, groups) + block, BF16), pltpu.VMEM((chips, groups) + block, BF16),
                        pltpu.VMEM((chips, groups) + block, BF16), pltpu.VMEM((groups,) + block, BF16),
                        dma((chips, groups)), dma(()), dma((chips, groups)), dma((chips, groups)),
                        dma((chips, groups)), dma((chips, groups)), dma((groups,)), dma((groups,))],
        compiler_params=pltpu.CompilerParams(collective_id=2, has_side_effects=True, vmem_limit_bytes=58 << 20),
        name="collect",
    )(parts)


def expert_kernel(rows_ref, mask_ref, up_ref, down_ref, out_ref, gup_ref, gdown_ref):
    @pl.when(pl.program_id(1) == 0)
    def _():
        gup_ref[...] = jnp.zeros_like(gup_ref)
        gdown_ref[...] = jnp.zeros_like(gdown_ref)

    x = rows_ref[0, 0]
    d = (rows_ref[1, 0].astype(F32) * mask_ref[0]).astype(BF16)
    up, down = up_ref[0], down_ref[0]
    pre = mxu(x, up, NN)
    cdf = 0.5 * (1.0 + lax.erf(pre * 0.7071067811865476))
    hidden = (pre * cdf).astype(BF16)
    slope = cdf + pre * (0.3989422804014327 * jnp.exp(-0.5 * pre * pre))
    out_ref[0, 0] = mxu(hidden, down, NN).astype(BF16)
    d_pre = (mxu(d, down, NT) * slope).astype(BF16)
    out_ref[1, 0] = mxu(d_pre, up, NT).astype(BF16)
    gdown_ref[0] += mxu(hidden, d, TN)
    gup_ref[0] += mxu(x, d_pre, TN)


def expert_block(rows, mask, w_up, w_down, block=256):
    kinds, held, count, width = rows.shape
    hidden = w_up.shape[2]
    both = pl.BlockSpec((kinds, 1, block, width), lambda x, r: (0, x, r, 0))
    up = pl.BlockSpec((1, width, hidden), lambda x, r: (x, 0, 0))
    down = pl.BlockSpec((1, hidden, width), lambda x, r: (x, 0, 0))
    return pl.pallas_call(
        expert_kernel,
        grid=(held, count // block),
        out_shape=(jax.ShapeDtypeStruct(rows.shape, BF16), jax.ShapeDtypeStruct(w_up.shape, F32),
                   jax.ShapeDtypeStruct(w_down.shape, F32)),
        in_specs=[both, pl.BlockSpec((1, block, 1), lambda x, r: (x, r, 0)), up, down],
        out_specs=(both, up, down),
        compiler_params=pltpu.CompilerParams(vmem_limit_bytes=56 << 20),
        name="experts",
    )(rows, mask, w_up, w_down)


def rms_scale(values, gain):
    return values * lax.rsqrt(jnp.mean(values * values, axis=-1, keepdims=True) + EPS) * gain


def contract_rows(left, right):
    return lax.dot_general(left, right, TN, preferred_element_type=F32)


def local(tokens, d_out, segment, route, gain_one, w_in, conv_w, conv_b, w_x, w_dt, b_dt, a_log, d_skip, w_out,
          gain_two, w_router, w_up, w_down):
    length, width = tokens.shape
    inner_w = w_in.shape[1] // 2
    experts = w_router.shape[1]
    held = w_up.shape[0]
    groups, members = lax.axis_size("ep"), lax.axis_size("tp")
    slots = 3 * length // (2 * experts)
    capacity = 5 * length * groups * members // (4 * experts)
    rank_dt, states = w_dt.shape[0], a_log.shape[0]
    used = rank_dt + 2 * states
    taps = conv_w.shape[0]
    is_valid = segment >= 0
    valid = is_valid.astype(F32)[:, None]
    masks = flags(segment)
    vec = jnp.concatenate([conv_w, conv_b[None], b_dt[None], d_skip[None], d_skip[None]], axis=0).astype(F32)
    wx_pad = jnp.pad(w_x, ((0, 0), (0, 128 - used)))
    wdt_pad = jnp.pad(w_dt, ((0, 128 - rank_dt), (0, 0)))
    rates = -jnp.exp(a_log.astype(F32))

    pick_int = ((route == jnp.arange(experts, dtype=jnp.int32)[None, :]) & is_valid[:, None]).astype(jnp.int32)
    picks = pick_int.astype(F32)
    local_count = jnp.sum(pick_int, axis=0)
    local_rank = jnp.sum(jnp.cumsum(pick_int, axis=0) * pick_int, axis=1) - 1
    slot_id = jnp.where(is_valid, route[:, 0] * slots + local_rank, -1)
    places = (jnp.arange(experts * slots, dtype=jnp.int32)[:, None] == slot_id[None, :]).astype(BF16)

    token_f = tokens.astype(F32)
    normed_one, norm_one_pull = jax.vjp(rms_scale, token_f, gain_one.astype(F32))
    normed_low = normed_one.astype(BF16)
    both = jnp.dot(normed_low, w_in, preferred_element_type=F32)
    gated_low, pre, pre_dt, scanned, proj, starts = mid_fwd(both, masks, vec, wx_pad, wdt_pad, rates * LOG2E, rank_dt)
    mixed = jnp.dot(gated_low, w_out, preferred_element_type=F32)
    after_mix = token_f + mixed * valid
    normed_two, norm_two_pull = jax.vjp(rms_scale, after_mix, gain_two.astype(F32))

    def router(normed_in, router_w):
        probs = jax.nn.softmax(jnp.dot(normed_in, router_w, precision=HIGH), axis=-1)
        return jnp.sum(probs * picks, axis=-1)

    gate, router_pull = jax.vjp(router, normed_two, w_router.astype(F32))
    upstream = d_out.astype(F32)
    leaving = jnp.stack(
        [
            jnp.dot(places, normed_two.astype(BF16), preferred_element_type=F32).astype(BF16),
            jnp.dot(places, (gate[:, None] * upstream).astype(BF16), preferred_element_type=F32).astype(BF16),
        ]
    ).reshape(2, experts, slots, width)
    count_tile = jnp.broadcast_to(jnp.pad(local_count, (0, 128 - experts))[None], (8, 128))
    rows, table = dispatch(leaving, count_tile, groups, members)

    everyone = table[:, :, 0, :experts].transpose(1, 0, 2).reshape(groups * members, experts)
    device = jnp.arange(groups * members)
    before = device[None, :] < device[:, None]
    prior = jnp.sum(jnp.where(before[:, :, None], everyone[None], 0), axis=1)
    named = jnp.sum(everyone, axis=0)
    counts = jnp.stack([named, jnp.maximum(named - capacity, 0)])
    mine = lax.dynamic_slice_in_dim(prior.reshape(groups, members, experts), lax.axis_index("ep") * held, held, 2)
    room = mine.transpose(2, 1, 0)[..., None] + jnp.arange(slots)[None, None, None] < capacity
    room = room.reshape(held, members * groups * slots, 1).astype(F32)
    here = jnp.sum(jnp.where((device == lax.axis_index(("ep", "tp")))[:, None], prior, 0), axis=0)
    keep = (is_valid & (jnp.sum(pick_int * here[None, :], axis=1) + local_rank < capacity)).astype(F32)[:, None]

    parts, grad_up, grad_down = expert_block(rows.reshape(2, held, members * groups * slots, width), room, w_up, w_down)
    returned = collect(parts.reshape(rows.shape), groups, members).reshape(2, experts * slots, width)
    token_out = contract_rows(places, returned[0])
    d_normed = contract_rows(places, returned[1])

    final = after_mix + gate[:, None] * keep * token_out
    d_gate = keep[:, 0] * jnp.sum(upstream * token_out, axis=1)
    d_norm_router, grad_router = router_pull(d_gate)
    d_after, grad_gain_two = norm_two_pull(d_normed + d_norm_router)
    d_after = d_after + upstream
    d_mixed = (d_after * valid).astype(BF16)
    grad_out = contract_rows(gated_low, d_mixed)
    d_gated = lax.dot_general(d_mixed, w_out, NT, preferred_element_type=F32)
    d_both, grad_vec, grad_x, grad_dt, grad_rates = mid_bwd(
        both, d_gated, pre, pre_dt, scanned, proj, starts, masks, vec, wx_pad.T, wdt_pad, rates * LOG2E, rank_dt
    )
    grad_in = contract_rows(normed_low, d_both)
    d_normed_one = lax.dot_general(d_both, w_in, NT, preferred_element_type=F32)
    d_tokens_norm, grad_gain_one = norm_one_pull(d_normed_one)
    d_tokens = d_after + d_tokens_norm

    small = jnp.concatenate(
        [
            grad_x[:used],
            grad_dt[:rank_dt],
            grad_rates * rates,
            grad_vec,
            jnp.concatenate([grad_gain_one, grad_gain_two])[None],
            grad_router.T.reshape(-1, inner_w),
        ],
        axis=0,
    )
    rows_used = small.shape[0]
    small = jnp.pad(small, ((0, 256 - rows_used), (0, 0))).astype(BF16).T
    wide = jnp.concatenate([grad_out.astype(BF16), small], axis=1)
    total_in, wide = all_sum(grad_in.astype(BF16), wide, groups, members)
    small = wide[:, width:].astype(F32).T
    at = used + rank_dt + states
    gains = small[at + 8].reshape(2, width)
    return (
        final.astype(BF16),
        d_tokens,
        counts,
        gains[0],
        total_in.astype(F32),
        small[at : at + taps],
        small[at + taps],
        wide[:, width : width + used].astype(F32),
        small[used : used + rank_dt],
        small[at + taps + 1],
        small[used + rank_dt : at],
        small[at + taps + 2],
        wide[:, :width].astype(F32),
        gains[1],
        small[at + 9 : rows_used].reshape(experts, width).T,
        grad_up,
        grad_down,
    )


def solution(mesh):
    in_specs = (
        P(("ep", "tp"), None),
        P(("ep", "tp"), None),
        P(("ep", "tp")),
        P(("ep", "tp"), None),
        P(),
        P(),
        P(),
        P(),
        P(),
        P(),
        P(),
        P(),
        P(),
        P(),
        P(),
        P(),
        P("ep", None, "tp"),
        P("ep", "tp", None),
    )
    out_specs = (
        P(("ep", "tp"), None),
        P(("ep", "tp"), None),
        P(),
        P(),
        P(),
        P(),
        P(),
        P(),
        P(),
        P(),
        P(),
        P(),
        P(),
        P(),
        P(),
        P("ep", None, "tp"),
        P("ep", "tp", None),
    )
    return jax.shard_map(local, mesh=mesh, in_specs=in_specs, out_specs=out_specs, check_vma=False)
```

```python
import functools

import jax
import jax.numpy as jnp
from jax import lax
from jax.experimental import pallas as pl
from jax.experimental.pallas import tpu as pltpu
from jax.sharding import PartitionSpec as P

EPS = 1e-06
MESH = pl.DeviceIdType.MESH
TB = 128
CH = 16
LB = 256
LOG2E = 1.4426950408889634
LN2 = 0.6931471805599453
F32 = jnp.float32
BF16 = jnp.bfloat16
NN = (((1,), (0,)), ((), ()))
NT = (((1,), (1,)), ((), ()))
TN = (((0,), (0,)), ((), ()))


def mxu(left, right, dims):
    return lax.dot_general(left, right, dims, preferred_element_type=F32)


def split(x):
    high = x.astype(BF16)
    return high, (x - high.astype(F32)).astype(BF16)


def dot2(x, w, dims):
    high, rest = split(x)
    return mxu(high, w, dims) + mxu(rest, w, dims)


def dot3(x, w, dims):
    high, rest = split(x)
    high_w, rest_w = split(w)
    return mxu(high, high_w, dims) + mxu(high, rest_w, dims) + mxu(rest, high_w, dims)


def sigmoid(x):
    return 1.0 / (1.0 + jnp.exp(-x))


def softplus(x):
    return jnp.maximum(x, 0.0) + jnp.log1p(jnp.exp(-jnp.abs(x)))


def row_sums(items):
    items = [sum((x[8 * i:8 * i + 8] for i in range(1, x.shape[0] // 8)), x[:8]) for x in items]
    place = lax.broadcasted_iota(jnp.int32, items[0].shape, 0)
    for level in (1, 2, 4):
        odd = (place // level) % 2 == 1
        merged = []
        for low, high in zip(items[::2], items[1::2]):
            merged.append(jnp.where(odd, high, low) + pltpu.roll(jnp.where(odd, low, high), level, 0))
        items = merged
    return items[0]


def mid_fwd_kernel(rank, both_ref, segment_ref, vec_ref, wx_ref, wdt_ref, rates_ref,
                   gated_ref, conv_ref, bend_ref, step_ref, rise_ref, gate_ref, slope_ref, proj_ref, hs_ref,
                   ext_ref, h_ref, turned_ref, seg_ref, spread_ref, decay_ref, source_ref, pdt_ref):
    states, width = rates_ref.shape

    @pl.when(pl.program_id(0) == 0)
    def _():
        ext_ref[:8, :] = jnp.zeros((8, width), F32)
        seg_ref[:8, :] = jnp.full((8, 128), -2, jnp.int32)
        h_ref[...] = jnp.zeros_like(h_ref)

    @pl.when(pl.program_id(0) > 0)
    def _():
        ext_ref[:8, :] = ext_ref[TB:, :]
        seg_ref[:8, :] = seg_ref[TB:, :]

    seg_ref[8:, :] = segment_ref[...]

    def same(c, k):
        at = c * CH + 8
        return (seg_ref[at - k:at - k + CH, :] == seg_ref[at:at + CH, :]).astype(F32)[:, :1]

    def conv_chunk(c):
        rows = slice(c * CH, c * CH + CH)
        masks = [same(c, k) for k in range(1, 4)]
        for b in range(width // LB):
            lanes = slice(b * LB, (b + 1) * LB)
            at = c * CH + 8
            here = both_ref[rows, lanes]
            ext_ref[at:at + CH, lanes] = here
            total = vec_ref[4:5, lanes] + vec_ref[3:4, lanes] * here
            for k in range(1, 4):
                total = total + vec_ref[3 - k:4 - k, lanes] * ext_ref[at - k:at - k + CH, lanes] * masks[k - 1]
            sig = sigmoid(total)
            conv_ref[rows, lanes] = total * sig
            bend_ref[rows, lanes] = sig * (1.0 + total * (1.0 - sig))

    for c in range(TB // CH):
        conv_chunk(c)
    proj = dot2(conv_ref[...], wx_ref[...], NN)
    lane = lax.broadcasted_iota(jnp.int32, (TB, 128), 1)
    keep = (seg_ref[7:7 + TB, :] == seg_ref[8:, :]).astype(F32)
    proj_ref[...] = jnp.where(lane == 127, keep, proj)
    turned_ref[...] = proj.T
    pdt_ref[...] = dot2(proj, wdt_ref[...], NN) + vec_ref[5:6, :]

    def every(ref, k):
        row = ref[pl.ds(k, 8, stride=0), :]
        return jnp.concatenate([row] * (states // 8), axis=0)

    def wide(k, side):
        return jnp.concatenate([spread_ref[k, side * states:(side + 1) * states, :]] * (LB // 128), axis=1)

    def scan_chunk(c, _):
        rows = pl.ds(pl.multiple_of(c * CH, CH), CH)
        tile = pltpu.roll(turned_ref[rank:rank + 2 * states, :], TB - c * CH, 1)
        keep = proj_ref[rows, 127:]
        for k in range(CH):
            spread_ref[k] = jnp.broadcast_to(tile[:, k:k + 1], (2 * states, 128))
        for b in range(width // LB):
            lanes = slice(b * LB, (b + 1) * LB)
            rates = rates_ref[:, lanes]
            h = h_ref[:, lanes]
            hs_ref[c, :, lanes] = h
            conv = conv_ref[rows, lanes]
            pdt = pdt_ref[rows, lanes]
            step = softplus(pdt)
            step_ref[rows, lanes] = step
            rise_ref[rows, lanes] = sigmoid(pdt)
            source_ref[b, :CH] = step * conv
            decay_ref[b, :CH] = jnp.where(keep > 0.0, step, 1e4)
            outs = []
            for k in range(CH):
                h = jnp.exp2(every(decay_ref.at[b], k) * rates) * h + wide(k, 0) * every(source_ref.at[b], k)
                outs.append(wide(k, 1) * h)
            h_ref[:, lanes] = h
            y = jnp.concatenate([row_sums(outs[:8]), row_sums(outs[8:])], axis=0)
            gate = both_ref[rows, width + b * LB:width + (b + 1) * LB]
            sig = sigmoid(gate)
            mixed = y + vec_ref[6:7, lanes] * conv
            gate_ref[rows, lanes] = gate * sig
            gated_ref[rows, lanes] = (mixed * (gate * sig)).astype(BF16)
            slope_ref[rows, lanes] = mixed * (sig * (1.0 + gate * (1.0 - sig)))
        return 0

    lax.fori_loop(0, TB // CH, scan_chunk, 0)


def mid_fwd(both, segment, vec, wx, wdt, rates, rank):
    length = both.shape[0]
    states, width = rates.shape
    row = lambda i: (i, 0)
    fix = lambda i: (0, 0)
    tall = pl.BlockSpec((TB, width), row)
    like = jax.ShapeDtypeStruct((length, width), F32)
    return pl.pallas_call(
        functools.partial(mid_fwd_kernel, rank),
        grid=(length // TB,),
        out_shape=(jax.ShapeDtypeStruct((length, width), BF16), like, like, like, like, like, like,
                   jax.ShapeDtypeStruct((length, 128), F32),
                   jax.ShapeDtypeStruct((length // CH, states, width), F32)),
        in_specs=[pl.BlockSpec((TB, 2 * width), row), pl.BlockSpec((TB, 128), row), pl.BlockSpec(vec.shape, fix),
                  pl.BlockSpec(wx.shape, fix), pl.BlockSpec(wdt.shape, fix), pl.BlockSpec(rates.shape, fix)],
        out_specs=(tall, tall, tall, tall, tall, tall, tall, pl.BlockSpec((TB, 128), row),
                   pl.BlockSpec((TB // CH, states, width), lambda i: (i, 0, 0))),
        scratch_shapes=[pltpu.VMEM((TB + 8, width), F32),
                        pltpu.VMEM((states, width), F32), pltpu.VMEM((128, TB), F32),
                        pltpu.VMEM((TB + 8, 128), jnp.int32), pltpu.VMEM((CH, 2 * states, 128), F32),
                        pltpu.VMEM((width // LB, CH + 8, LB), F32), pltpu.VMEM((width // LB, CH + 8, LB), F32),
                        pltpu.VMEM((TB, width), F32)],
        compiler_params=pltpu.CompilerParams(vmem_limit_bytes=60 << 20),
        name="mid_fwd",
    )(both, segment, vec, wx, wdt, rates)


def mid_bwd_kernel(rank, both_ref, dg_ref, conv_ref, bend_ref, step_ref, rise_ref, gate_ref, slope_ref, proj_ref, hs_ref, segment_ref, vec_ref, wxt_ref,
                   wdt_ref, rates_ref,
                   dboth_ref, gvec_ref, gwx_ref, gwdt_ref, gr_ref,
                   ext_ref, g_ref, dec_ref, p_ref, part_ref, dproj_ref, dconv_ref, dpdt_ref, turned_ref,
                   acc_ref, seg_ref, spread_ref, decay_ref, source_ref, dy_ref):
    states, width = rates_ref.shape
    steps = TB // CH

    @pl.when(pl.program_id(0) == 0)
    def _():
        ext_ref[TB:, :] = jnp.zeros((8, width), F32)
        seg_ref[TB:, :] = jnp.full((8, 128), -2, jnp.int32)
        g_ref[...] = jnp.zeros_like(g_ref)
        acc_ref[...] = jnp.zeros_like(acc_ref)
        gwx_ref[...] = jnp.zeros_like(gwx_ref)
        gwdt_ref[...] = jnp.zeros_like(gwdt_ref)
        gr_ref[...] = jnp.zeros_like(gr_ref)

    @pl.when(pl.program_id(0) > 0)
    def _():
        ext_ref[TB:, :] = ext_ref[:8, :]
        seg_ref[TB:, :] = seg_ref[:8, :]

    turned_ref[...] = proj_ref[...].T
    seg_ref[:TB, :] = segment_ref[...]
    ones = jnp.ones((128, 128), BF16)
    lane = lax.broadcasted_iota(jnp.int32, (2 * states, 128), 1)
    place = lax.broadcasted_iota(jnp.int32, (2 * states, 128), 0) + rank

    def fold(x):
        out = x[:, :128]
        for i in range(1, LB // 128):
            out = out + x[:, i * 128:(i + 1) * 128]
        return out

    def halves(x):
        out = x[:8]
        for i in range(1, CH // 8):
            out = out + x[i * 8:(i + 1) * 8]
        return out

    def every(ref, k):
        row = ref[pl.ds(k, 8, stride=0), :]
        return jnp.concatenate([row] * (states // 8), axis=0)

    def wide(k, side):
        return jnp.concatenate([spread_ref[k, side * states:(side + 1) * states, :]] * (LB // 128), axis=1)

    def scan_chunk(i, _):
        c = steps - 1 - i
        rows = pl.ds(pl.multiple_of(c * CH, CH), CH)
        tile = pltpu.roll(turned_ref[rank:rank + 2 * states, :], TB - c * CH, 1)
        keep = proj_ref[rows, 127:]
        for k in range(CH):
            spread_ref[k] = jnp.broadcast_to(tile[:, k:k + 1], (2 * states, 128))
        for b in range(width // LB):
            lanes = slice(b * LB, (b + 1) * LB)
            rates = rates_ref[:, lanes]
            h = hs_ref[c, :, lanes]
            conv = conv_ref[rows, lanes]
            step = step_ref[rows, lanes]
            source_ref[b, :CH] = step * conv
            decay_ref[b, :CH] = jnp.where(keep > 0.0, step, 1e4)
            skip = vec_ref[6:7, lanes]
            dg = dg_ref[rows, lanes]
            dboth_ref[rows, width + b * LB:width + (b + 1) * LB] = (dg * slope_ref[rows, lanes]).astype(BF16)
            dy = dg * gate_ref[rows, lanes]
            dy_ref[b, :CH] = dy
            for k in range(CH):
                dec = jnp.exp2(every(decay_ref.at[b], k) * rates)
                p = dec * h
                dec_ref[k] = dec
                p_ref[k] = p
                h = p + wide(k, 0) * every(source_ref.at[b], k)
                out = fold(every(dy_ref.at[b], k) * h)
                part_ref[k, states:, :] = out if b == 0 else part_ref[k, states:, :] + out
            g = g_ref[:, lanes]
            dr = gr_ref[:, lanes]
            dus, dss = [None] * CH, [None] * CH
            for k in reversed(range(CH)):
                dh = g + wide(k, 1) * every(dy_ref.at[b], k)
                out = fold(dh * every(source_ref.at[b], k))
                part_ref[k, :states, :] = out if b == 0 else part_ref[k, :states, :] + out
                dus[k] = halves(dh * wide(k, 0))
                da = dh * p_ref[k]
                dss[k] = halves(da * rates)
                dr = dr + da * every(decay_ref.at[b], k)
                g = dec_ref[k] * dh
            g_ref[:, lanes] = g
            gr_ref[:, lanes] = dr
            du = jnp.concatenate([row_sums(dus[:8]), row_sums(dus[8:])], axis=0)
            dpdt = (jnp.concatenate([row_sums(dss[:8]), row_sums(dss[8:])], axis=0) * LN2 + du * conv) * rise_ref[rows, lanes]
            dpdt_ref[rows, lanes] = dpdt
            dconv_ref[rows, lanes] = dy * skip + du * step
            acc_ref[5, :, lanes] += halves(dpdt)
            acc_ref[6, :, lanes] += halves(dy * conv)
        high, rest = split(part_ref[...].reshape(CH * 2 * states, 128))
        sums = (mxu(high, ones, NN) + mxu(rest, ones, NN)).reshape(CH, 2 * states, 128)
        picked = jnp.where((lane == place)[None], sums, 0.0)
        dproj_ref[rows, :] = jnp.sum(picked, axis=1)
        return 0

    lax.fori_loop(0, steps, scan_chunk, 0)
    dpdt = dpdt_ref[...]
    dproj = dproj_ref[...] + dot2(dpdt, wdt_ref[...], NT)
    gwdt_ref[...] += dot3(turned_ref[...], dpdt, NN)
    gwx_ref[...] += dot3(dproj.T, conv_ref[...], NN)
    dconv_ref[...] += dot2(dproj, wxt_ref[...], NN)

    def act_chunk(c, _):
        rows = pl.ds(pl.multiple_of(c * CH, CH), CH)
        ext_ref[rows, :] = dconv_ref[rows, :] * bend_ref[rows, :]
        return 0

    lax.fori_loop(0, steps, act_chunk, 0)

    def conv_chunk(c):
        at = c * CH
        rows = slice(at, at + CH)
        masks = [(seg_ref[at + k:at + k + CH, :] == seg_ref[rows, :]).astype(F32)[:, :1] for k in range(1, 4)]
        for b in range(width // LB):
            lanes = slice(b * LB, (b + 1) * LB)
            inner = both_ref[rows, lanes]
            here = ext_ref[rows, lanes]
            total = vec_ref[3:4, lanes] * here
            acc_ref[4, :, lanes] += halves(here)
            acc_ref[3, :, lanes] += halves(here * inner)
            for k in range(1, 4):
                later = ext_ref[at + k:at + k + CH, lanes] * masks[k - 1]
                total = total + vec_ref[3 - k:4 - k, lanes] * later
                acc_ref[3 - k, :, lanes] += halves(later * inner)
            dboth_ref[rows, lanes] = total.astype(BF16)

    for c in range(steps):
        conv_chunk(c)

    @pl.when(pl.program_id(0) == pl.num_programs(0) - 1)
    def _():
        gvec_ref[...] = jnp.concatenate(
            [jnp.sum(acc_ref[k], axis=0, keepdims=True) for k in range(8)], axis=0)


def mid_bwd(both, dg, saved, proj, hs, segment, vec, wxt, wdt, rates, rank):
    length = both.shape[0]
    states, width = rates.shape
    blocks = length // TB
    row = lambda i: (blocks - 1 - i, 0)
    fix = lambda i: (0, 0)
    tall = pl.BlockSpec((TB, width), row)
    return pl.pallas_call(
        functools.partial(mid_bwd_kernel, rank),
        grid=(blocks,),
        out_shape=(jax.ShapeDtypeStruct((length, 2 * width), BF16), jax.ShapeDtypeStruct((8, width), F32),
                   jax.ShapeDtypeStruct((128, width), F32), jax.ShapeDtypeStruct((128, width), F32),
                   jax.ShapeDtypeStruct((states, width), F32)),
        in_specs=[tall, tall] + [tall] * 6 + [pl.BlockSpec((TB, 128), row),
                  pl.BlockSpec((TB // CH, states, width), lambda i: (blocks - 1 - i, 0, 0)),
                  pl.BlockSpec((TB, 128), row), pl.BlockSpec(vec.shape, fix), pl.BlockSpec(wxt.shape, fix),
                  pl.BlockSpec(wdt.shape, fix), pl.BlockSpec(rates.shape, fix)],
        out_specs=(pl.BlockSpec((TB, 2 * width), row), pl.BlockSpec((8, width), fix),
                   pl.BlockSpec((128, width), fix), pl.BlockSpec((128, width), fix), pl.BlockSpec((states, width), fix)),
        scratch_shapes=[pltpu.VMEM((TB + 8, width), F32), pltpu.VMEM((states, width), F32),
                        pltpu.VMEM((CH, states, LB), F32), pltpu.VMEM((CH, states, LB), F32),
                        pltpu.VMEM((CH, 2 * states, 128), F32), pltpu.VMEM((TB, 128), F32),
                        pltpu.VMEM((TB, width), F32), pltpu.VMEM((TB, width), F32),
                        pltpu.VMEM((128, TB), F32), pltpu.VMEM((8, 8, width), F32),
                        pltpu.VMEM((TB + 8, 128), jnp.int32), pltpu.VMEM((CH, 2 * states, 128), F32),
                        pltpu.VMEM((width // LB, CH + 8, LB), F32), pltpu.VMEM((width // LB, CH + 8, LB), F32), pltpu.VMEM((width // LB, CH + 8, LB), F32)],
        compiler_params=pltpu.CompilerParams(vmem_limit_bytes=60 << 20),
        name="mid_bwd",
    )(both, dg, *saved, proj, hs, segment, vec, wxt, wdt, rates)


CHUNK = (256, 1024)


def bit_orders(groups, members):
    ep_bits, tp_bits = groups.bit_length() - 1, members.bit_length() - 1
    x = [("ep", b) for b in range(ep_bits - 2)]
    z = [("ep", b) for b in range(ep_bits - 2, ep_bits)]
    y = [("tp", b) for b in range(1, tp_bits)]
    core = [("tp", 0)]
    return [core + x + y + z, core + y + x + z, core + x + z + y, core + y + z + x]


def region_sizes(stages, rows, cols):
    sizes = []
    for _ in range(stages):
        if rows > 16:
            rows //= 2
            sizes.append((rows, cols, True))
        else:
            cols //= 2
            sizes.append((rows, cols, False))
    return sizes


def sum_scratch(chunks, stages):
    return [pltpu.VMEM((chunks, r, c), BF16) for r, c, _ in region_sizes(stages, *CHUNK)] + [
        pltpu.VMEM((chunks,) + CHUNK, BF16),
        pltpu.VMEM((chunks,) + CHUNK, BF16),
        pltpu.SemaphoreType.DMA((2 * stages, chunks)),
        pltpu.SemaphoreType.DMA((2 * stages, chunks)),
        pltpu.SemaphoreType.DMA((chunks,)),
    ]


def sum_steps(orders, g_ref, out_ref, scratch):
    stages = len(orders[0])
    land = scratch[:stages]
    work_ref, full_ref, send_sem, recv_sem, done_sem = scratch[stages:]
    sizes = region_sizes(stages, *CHUNK)
    me = {"ep": lax.axis_index("ep"), "tp": lax.axis_index("tp")}

    def bit(stage):
        axis, b = stage
        return lax.rem(me[axis] // (1 << b), 2)

    def partner(stage):
        axis, b = stage
        there = dict(me)
        there[axis] = me[axis] + (1 << b) - 2 * (1 << b) * bit(stage)
        return (there["ep"], there["tp"])

    def greet():
        barrier = pltpu.get_barrier_semaphore()
        for stage in orders[0]:
            pl.semaphore_signal(barrier, inc=1, device_id=partner(stage), device_id_type=MESH)
        pl.semaphore_wait(barrier, stages)

    def part(c, order, upto, flip):
        r0, c0 = 0, 0
        for s in range(upto + 1):
            b = bit(order[s])
            if s == upto and flip:
                b = 1 - b
            if sizes[s][2]:
                r0 = r0 + b * sizes[s][0]
            else:
                c0 = c0 + b * sizes[s][1]
        return (c, pl.ds(pl.multiple_of(r0, 16), sizes[upto][0]),
                pl.ds(c0 if isinstance(c0, int) else pl.multiple_of(c0, 128), sizes[upto][1]))

    def scatter(s, v, c):
        order = orders[v]
        return pltpu.make_async_remote_copy(
            src_ref=(g_ref if s == 0 else work_ref).at[part(c, order, s, True)], dst_ref=land[s].at[c],
            send_sem=send_sem.at[s, c], recv_sem=recv_sem.at[s, c], device_id=partner(order[s]), device_id_type=MESH)

    def gather(s, v, c, flip=False):
        order = orders[v]
        piece = full_ref.at[part(c, order, s, flip)]
        return pltpu.make_async_remote_copy(
            src_ref=piece, dst_ref=piece, send_sem=send_sem.at[stages + s, c], recv_sem=recv_sem.at[stages + s, c],
            device_id=partner(order[s]), device_id_type=MESH)

    def done(c):
        return pltpu.make_async_copy(full_ref.at[c], out_ref.at[c], done_sem.at[c])

    def step(n, v, c):
        if n == 0:
            scatter(0, v, c).start()
        elif n <= stages:
            s = n - 1
            scatter(s, v, c).wait_recv()
            where = part(c, orders[v], s, False)
            total = ((g_ref if s == 0 else work_ref)[where].astype(F32) + land[s][c].astype(F32)).astype(BF16)
            if s + 1 < stages:
                work_ref[where] = total
                scatter(s + 1, v, c).start()
            else:
                full_ref[where] = total
                gather(s, v, c).start()
        else:
            s = 2 * stages - n
            gather(s, v, c, True).wait_recv()
            if s > 0:
                gather(s - 1, v, c).start()
            else:
                done(c).start()

    def settle(v, c):
        for s in range(stages):
            scatter(s, v, c).wait_send()
            gather(s, v, c).wait_send()
        done(c).wait()

    return greet, step, settle, 2 * stages + 1


def tail_kernel(orders, tall, across, used, rank, normed_ref, d_both_ref, vec_ref, g_two_ref, gx_ref, gdt_ref, gr_ref,
                rates_ref, gvec_ref, router_ref, w_in_hbm, gated_hbm, d_mixed_hbm, tokens_hbm, d_after_hbm,
                out_ref, d_tokens_ref, g_ref, gains_ref, w_in_ref, gated_ref, d_mixed_ref, tokens_ref, d_after_ref, load_sem,
                *scratch):
    greet, step, settle, steps = sum_steps(orders, g_ref, out_ref, scratch)
    kinds, chunks = len(orders), g_ref.shape[0]
    rows, cols = CHUNK
    width = d_mixed_ref.shape[1]
    loads = [pltpu.make_async_copy(src, dst, load_sem.at[n]) for n, (src, dst) in enumerate(
        ((w_in_hbm, w_in_ref), (tokens_hbm, tokens_ref), (d_after_hbm, d_after_ref), (gated_hbm, gated_ref),
         (d_mixed_hbm, d_mixed_ref)))]
    for load in loads:
        load.start()
    greet()

    def produce(c):
        @pl.when(c < tall)
        def _():
            left = pl.multiple_of(c // across * rows, rows)
            right = pl.multiple_of(lax.rem(c, across) * cols, cols)
            g_ref[c] = mxu(normed_ref[:, pl.ds(left, rows)], d_both_ref[:, pl.ds(right, cols)], TN).astype(BF16)

        @pl.when(c >= tall)
        def _():
            at = pl.ds(pl.multiple_of((c - tall) * rows, rows), rows)
            g_ref[c, :, :width] = mxu(gated_ref[:, at], d_mixed_ref[...], TN).astype(BF16)
            pieces = [gx_ref[:used, at], gdt_ref[:rank, at], gr_ref[:, at] * rates_ref[:, at] * LN2, gvec_ref[:, at],
                      gains_ref[:, at]]
            high = sum(p.shape[0] for p in pieces) + router_ref.shape[0]
            pieces += [jnp.zeros((256 - high, rows), F32), router_ref[:, at]]
            g_ref[c, :, width:] = jnp.concatenate(pieces, axis=0).T.astype(BF16)

    def input_grads():
        for load in loads[:3]:
            load.wait()
        values = tokens_ref[...].astype(F32)
        scale = lax.rsqrt(jnp.mean(values * values, axis=-1, keepdims=True) + EPS)
        plain = values * scale
        d_normed = mxu(d_both_ref[...], w_in_ref[...], NT)
        gains_ref[:, :width] = jnp.broadcast_to(jnp.sum(d_normed * plain, axis=0, keepdims=True), (8, width))
        gains_ref[:, width:] = g_two_ref[...]
        d_plain = d_normed * vec_ref[7:8, :width]
        d_tokens_ref[...] = d_after_ref[...] + scale * (d_plain - plain * jnp.mean(d_plain * plain, axis=-1, keepdims=True))
        for load in loads[3:]:
            load.wait()

    waves = -(-chunks // kinds)
    ready = tall // kinds

    def slot(i, _):
        for n in reversed(range(1, steps)):
            group = i - n
            for v in range(kinds):
                c = group * kinds + v

                @pl.when((group >= 0) & (c < chunks))
                def _(n=n, v=v, c=c):
                    step(n, v, c)

        @pl.when(i == ready)
        def _():
            input_grads()

        def begin(v, _):
            c = i * kinds + v

            @pl.when(c < chunks)
            def _():
                produce(c)
                step(0, 0, c)
            return 0

        lax.fori_loop(0, kinds, begin, 0)
        return 0

    lax.fori_loop(0, waves + steps - 1, slot, 0)

    def drain(group, _):
        for v in range(kinds):
            c = group * kinds + v

            @pl.when(c < chunks)
            def _(v=v, c=c):
                settle(v, c)
        return 0

    lax.fori_loop(0, waves, drain, 0)


SUM_ORDERS = (0, 1, 2, 3)


def tail_sum(normed, d_both, w_in, gated, d_mixed, tokens, d_after, vec, g_two, gx, gdt, gr, rates, gvec, router, used, rank,
             groups, members):
    length, width = normed.shape
    rows, cols = CHUNK
    across = d_both.shape[1] // cols
    tall = width // rows * across
    chunks = tall + gated.shape[1] // rows
    orders = [bit_orders(groups, members)[v] for v in SUM_ORDERS]
    vmem, anywhere = pl.BlockSpec(memory_space=pltpu.VMEM), pl.BlockSpec(memory_space=pl.ANY)
    held = lambda a: pltpu.VMEM(a.shape, a.dtype)
    return pl.pallas_call(
        functools.partial(tail_kernel, orders, tall, across, used, rank),
        out_shape=(jax.ShapeDtypeStruct((chunks,) + CHUNK, BF16), jax.ShapeDtypeStruct((length, width), F32)),
        in_specs=[vmem] * 10 + [anywhere] * 5,
        out_specs=(anywhere, vmem),
        scratch_shapes=[pltpu.VMEM((chunks,) + CHUNK, BF16), pltpu.VMEM((8, 2 * width), F32), held(w_in), held(gated),
                        held(d_mixed), held(tokens), held(d_after), pltpu.SemaphoreType.DMA((5,))]
        + sum_scratch(chunks, len(orders[0])),
        compiler_params=pltpu.CompilerParams(collective_id=0, has_side_effects=True, vmem_limit_bytes=60 << 20),
        name="tail_sum",
    )(normed, d_both, vec, g_two, gx, gdt, gr, rates, gvec, router, w_in, gated, d_mixed, tokens, d_after)


CARRIED = 3


def unpack_kernel(tall_ref, wide_ref, *refs):
    sources, refs = refs[:CARRIED], refs[CARRIED:]
    in_ref, out_ref, x_ref, router_ref, *row_refs = refs[:-CARRIED]
    in_ref[...] = tall_ref[0].astype(F32)

    @pl.when(pl.program_id(0) < 8)
    def _():
        for source, target in zip(sources, refs[-CARRIED:]):
            target[...] = source[...]

    width = out_ref.shape[1]

    @pl.when(pl.program_id(0) < pl.num_programs(0) * 2 // 3)
    def _():
        out_ref[...] = wide_ref[0, :, :width].astype(F32)
        small = wide_ref[0, :, width:].astype(F32)
        turned = small.T
        at = x_ref.shape[0]
        x_ref[...] = turned[:at]
        router_ref[...] = turned[256 - router_ref.shape[0] :]
        for ref in row_refs[:3]:
            ref[...] = turned[at : at + ref.shape[0]]
            at += ref.shape[0]
        for ref in row_refs[3:6]:
            ref[...] = turned[at]
            at += 1
        c, half = pl.program_id(0), width // CHUNK[0]

        @pl.when(c < half)
        def _():
            row_refs[6][...] = turned[at + 1]

        @pl.when(c >= half)
        def _():
            row_refs[7][...] = turned[at + 1]


def unpack_grads(total, carried, width, inner, used, experts, heights):
    rows, cols = CHUNK
    across = 2 * inner // cols
    tall, wide = width // rows * across, inner // rows
    hold = lambda c: jnp.minimum(c, wide - 1)
    half = width // rows
    eighth = [pl.BlockSpec((a.shape[0] // 8, a.shape[1]), lambda c: (jnp.minimum(c, 7), 0)) for a in carried]
    return pl.pallas_call(
        unpack_kernel,
        grid=(tall,),
        out_shape=(jax.ShapeDtypeStruct((width, 2 * inner), F32), jax.ShapeDtypeStruct((inner, width), F32),
                   jax.ShapeDtypeStruct((used, inner), F32), jax.ShapeDtypeStruct((experts, inner), F32))
        + tuple(jax.ShapeDtypeStruct((h, inner), F32) for h in heights)
        + tuple(jax.ShapeDtypeStruct((w,), F32) for w in (inner, inner, inner, width, width))
        + tuple(jax.ShapeDtypeStruct(a.shape, a.dtype) for a in carried),
        in_specs=[pl.BlockSpec((1,) + CHUNK, lambda c: (c, 0, 0)),
                  pl.BlockSpec((1,) + CHUNK, lambda c: (tall + hold(c), 0, 0))] + eighth,
        out_specs=(pl.BlockSpec(CHUNK, lambda c: (c // across, lax.rem(c, across))),
                   pl.BlockSpec((rows, width), lambda c: (hold(c), 0)),
                   pl.BlockSpec((used, rows), lambda c: (0, hold(c))),
                   pl.BlockSpec((experts, rows), lambda c: (0, hold(c))))
        + tuple(pl.BlockSpec((h, rows), lambda c: (0, hold(c))) for h in heights)
        + (pl.BlockSpec((rows,), lambda c: (hold(c),)),) * 3
        + (pl.BlockSpec((rows,), lambda c: (jnp.minimum(c, half - 1),)), pl.BlockSpec((rows,), lambda c: (jnp.maximum(hold(c) - half, 0),)))
        + tuple(eighth),
        compiler_params=pltpu.CompilerParams(vmem_limit_bytes=60 << 20),
        name="unpack_grads",
    )(total, total, *carried)


def front_kernel(rank, used, tokens_ref, taps_ref, bias_ref, step_ref, skip_ref, gain_one_ref, gain_two_ref, segment_ref,
                 route_ref, w_in_ref, wx_ref, wdt_ref, log_ref,
                 normed_ref, both_ref, wx_out, wxt_out, wdt_out, rates_out, vec_ref, segment_out, route_out):
    @pl.when(pl.program_id(0) == 0)
    def _():
        values = tokens_ref[...].astype(F32)
        width = values.shape[1]
        vec_ref[:4, :] = taps_ref[...].astype(F32)
        for n, ref in ((4, bias_ref), (5, step_ref), (6, skip_ref)):
            vec_ref[n:n + 1, :] = ref[...].astype(F32).reshape(1, -1)
        vec_ref[7:8, :width] = gain_one_ref[...].astype(F32).reshape(1, -1)
        vec_ref[7:8, width:] = gain_two_ref[...].astype(F32).reshape(1, -1)
        for source, target in ((segment_ref, segment_out), (route_ref, route_out)):
            for n in range(source.shape[0]):
                row = source[n:n + 1, :].astype(F32)
                target[n * 128:(n + 1) * 128, :] = jnp.broadcast_to(row, (128, 128)).T.astype(jnp.int32)
        scale = lax.rsqrt(jnp.mean(values * values, axis=-1, keepdims=True) + EPS)
        normed_ref[...] = (values * scale * vec_ref[7:8, :width]).astype(BF16)
        wxt_out[...] = jnp.zeros_like(wxt_out)
        wxt_out[:used, :] = wx_ref[...]
        wx_out[...] = wxt_out[...].astype(F32).T.astype(BF16)
        wdt_out[...] = jnp.zeros_like(wdt_out)
        wdt_out[:rank, :] = wdt_ref[...]
        rates_out[...] = -jnp.exp(log_ref[...].astype(F32)) * LOG2E

    both_ref[...] = mxu(normed_ref[...], w_in_ref[...], NN)


def front(tokens, rows, w_in, w_x, w_dt, a_log):
    length, width = tokens.shape
    used, inner = w_x.shape
    rank, states = w_dt.shape[0], a_log.shape[0]
    cols = inner // 2
    fix = lambda a: pl.BlockSpec(a, lambda j: (0,) * len(a))
    return pl.pallas_call(
        functools.partial(front_kernel, rank, used),
        grid=(w_in.shape[1] // cols,),
        out_shape=(jax.ShapeDtypeStruct((length, width), BF16), jax.ShapeDtypeStruct((length, w_in.shape[1]), F32),
                   jax.ShapeDtypeStruct((inner, 128), BF16), jax.ShapeDtypeStruct((128, inner), BF16),
                   jax.ShapeDtypeStruct((128, inner), BF16), jax.ShapeDtypeStruct((states, inner), F32),
                   jax.ShapeDtypeStruct((8, inner), F32), jax.ShapeDtypeStruct((length, 128), jnp.int32),
                   jax.ShapeDtypeStruct((length, 128), jnp.int32)),
        in_specs=[fix(tokens.shape)] + [fix(a.shape) for a in rows] + [ pl.BlockSpec((width, cols), lambda j: (0, j)), fix(w_x.shape),
                  fix(w_dt.shape), fix(a_log.shape)],
        out_specs=(fix((length, width)), pl.BlockSpec((length, cols), lambda j: (0, j)), fix((inner, 128)),
                   fix((128, inner)), fix((128, inner)), fix((states, inner)), fix((8, inner)), fix((length, 128)),
                   fix((length, 128))),
        compiler_params=pltpu.CompilerParams(vmem_limit_bytes=60 << 20),
        name="front",
    )(tokens, *rows, w_in, w_x, w_dt, a_log)


def choose(experts, segment, route):
    lane = lax.broadcasted_iota(jnp.int32, (segment.shape[0], 128), 1)
    return (lane == route) & (segment >= 0)


def route_kernel(slots, gated_ref, w_out_ref, tokens_ref, d_out_ref, segment_ref, route_ref, gain_ref, w_router_ref,
                 after_ref, leaving_ref, count_ref, aux_ref):
    length, width = tokens_ref.shape
    experts = w_router_ref.shape[0]
    segment, route = segment_ref[:, :1], route_ref[:, :1]
    picked = choose(experts, segment, route)
    picks = picked.astype(F32)
    row = lax.broadcasted_iota(jnp.int32, (length, length), 0)
    col = lax.broadcasted_iota(jnp.int32, (length, length), 1)
    upto = mxu((col <= row).astype(BF16), picks.astype(BF16), NN)
    rank = jnp.sum(picks * upto, axis=1, keepdims=True) - 1.0
    slot = jnp.where(segment >= 0, route * slots + rank.astype(jnp.int32), -1)
    count_ref[...] = jnp.broadcast_to(jnp.sum(picks, axis=0, keepdims=True).astype(jnp.int32), count_ref.shape)

    mixed = mxu(gated_ref[...], w_out_ref[...], NN)
    after = tokens_ref[...].astype(F32) + jnp.where(segment >= 0, mixed, 0.0)
    after_ref[...] = after
    normed = after * lax.rsqrt(jnp.mean(after * after, axis=-1, keepdims=True) + EPS) * gain_ref[7:8, width:]
    logits = dot2(normed, w_router_ref[...], NT)
    logits = logits - jnp.max(logits, axis=-1, keepdims=True)
    weights = jnp.exp(logits)
    probs = weights / jnp.sum(weights, axis=-1, keepdims=True)
    aux_ref[...] = jnp.zeros_like(aux_ref)
    aux_ref[:, :experts] = probs
    gate = jnp.sum(aux_ref[...] * picks, axis=1, keepdims=True)
    lane = lax.broadcasted_iota(jnp.int32, (length, 128), 1)
    extra = jnp.where(lane == 125, rank, jnp.where(lane == 126, slot.astype(F32), jnp.where(lane == 127, gate, 0.0)))
    aux_ref[...] += extra
    places = (lax.broadcasted_iota(jnp.int32, (length, experts * slots), 1) == slot).astype(BF16)
    leaving_ref[0] = mxu(places, normed.astype(BF16), TN).astype(BF16)
    leaving_ref[1] = mxu(places, (gate * d_out_ref[...].astype(F32)).astype(BF16), TN).astype(BF16)


def route_out(gated, w_out, tokens, d_out, segment, route, gain, w_router, slots):
    length, width = tokens.shape
    experts = w_router.shape[0]
    return pl.pallas_call(
        functools.partial(route_kernel, slots),
        out_shape=(jax.ShapeDtypeStruct((length, width), F32), jax.ShapeDtypeStruct((2, experts * slots, width), BF16),
                   jax.ShapeDtypeStruct((8, 128), jnp.int32), jax.ShapeDtypeStruct((length, 128), F32)),
        compiler_params=pltpu.CompilerParams(vmem_limit_bytes=60 << 20),
        name="route_out",
    )(gated, w_out, tokens, d_out, segment, route, gain, w_router)


def home_kernel(slots, capacity, back_ref, after_ref, d_out_ref, aux_ref, segment_ref, route_ref, here_ref, gain_ref,
                w_router_ref, w_out_ref, final_ref, d_after_ref, d_mixed_ref, d_gated_ref, g_gain_ref, g_router_ref,
                counts_ref):
    length, width = after_ref.shape
    experts = w_router_ref.shape[0]
    segment, route, aux = segment_ref[:, :1], route_ref[:, :1], aux_ref[...]
    picks = choose(experts, segment, route).astype(F32)
    lane = lax.broadcasted_iota(jnp.int32, (length, 128), 1)
    rank, slot, gate = (jnp.sum(jnp.where(lane == n, aux, 0.0), axis=1, keepdims=True) for n in (125, 126, 127))
    prior = jnp.sum(picks * here_ref[0:1, :], axis=1, keepdims=True)
    keep = jnp.where((segment >= 0) & (prior + rank < capacity), 1.0, 0.0)
    named = here_ref[1:2, :].astype(jnp.int32)
    counts_ref[0:1, :] = named[:, :experts]
    counts_ref[1:2, :] = jnp.maximum(named - capacity, 0)[:, :experts]

    places = (lax.broadcasted_iota(jnp.int32, (length, experts * slots), 1) == slot.astype(jnp.int32)).astype(BF16)
    token_out = mxu(places, back_ref[0], NN)
    upstream = d_out_ref[...].astype(F32)
    after = after_ref[...]
    final_ref[...] = (after + gate * keep * token_out).astype(BF16)
    d_gate = keep * jnp.sum(upstream * token_out, axis=1, keepdims=True)
    probs = jnp.where(lane < experts, aux, 0.0)
    d_logits = (gate * d_gate * (picks - probs))[:, :experts]
    scale = lax.rsqrt(jnp.mean(after * after, axis=-1, keepdims=True) + EPS)
    plain = after * scale
    gain = gain_ref[7:8, width:]
    g_router_ref[...] = jnp.zeros_like(g_router_ref)
    g_router_ref[:, :width] = dot3(d_logits, plain * gain, TN)
    d_normed = mxu(places, back_ref[1], NN) + dot2(d_logits, w_router_ref[...], NN)
    g_gain_ref[...] = jnp.broadcast_to(jnp.sum(d_normed * plain, axis=0, keepdims=True), g_gain_ref.shape)
    d_plain = d_normed * gain
    d_after = upstream + scale * (d_plain - plain * jnp.mean(d_plain * plain, axis=-1, keepdims=True))
    d_after_ref[...] = d_after
    d_mixed = jnp.where(segment >= 0, d_after, 0.0).astype(BF16)
    d_mixed_ref[...] = d_mixed
    d_gated_ref[...] = mxu(d_mixed, w_out_ref[...], NT)


def come_home(back, after, d_out, aux, segment, route, here, gain, w_router, w_out, slots, capacity):
    length, width = after.shape
    inner, experts = w_out.shape[0], w_router.shape[0]
    return pl.pallas_call(
        functools.partial(home_kernel, slots, capacity),
        out_shape=(jax.ShapeDtypeStruct((length, width), BF16), jax.ShapeDtypeStruct((length, width), F32),
                   jax.ShapeDtypeStruct((length, width), BF16), jax.ShapeDtypeStruct((length, inner), F32),
                   jax.ShapeDtypeStruct((8, width), F32), jax.ShapeDtypeStruct((experts, inner), F32),
                   jax.ShapeDtypeStruct((2, experts), jnp.int32)),
        compiler_params=pltpu.CompilerParams(vmem_limit_bytes=60 << 20),
        name="come_home",
    )(back, after, d_out, aux, segment, route, here, gain, w_router, w_out)


def entry_barrier(groups, chips):
    e, t = lax.axis_index("ep"), lax.axis_index("tp")
    y, c = t // 2, lax.rem(t, 2)
    barrier = pltpu.get_barrier_semaphore()
    for k in range(1, groups):
        pl.semaphore_signal(barrier, inc=1, device_id=(lax.rem(e + k, groups), t), device_id_type=MESH)
    for k in range(1, chips):
        pl.semaphore_signal(barrier, inc=1, device_id=(e, lax.rem(y + k, chips) * 2 + c), device_id_type=MESH)
    pl.semaphore_signal(barrier, inc=1, device_id=(e, t + 1 - 2 * c), device_id_type=MESH)
    pl.semaphore_wait(barrier, groups + chips - 1)
    return e, t, y, c


def dispatch_kernel(groups, chips, rows_ref, count_ref, out_ref, table_ref,
                    own_sem, far_send, far_recv, row_send, row_recv, pair_send, pair_recv):
    e, t, y, c = entry_barrier(groups, chips)
    held = rows_ref.shape[1] // groups
    sibling = (e, t + 1 - 2 * c)

    def block(kind, ref, i, member):
        return ref.at[:, :, member, i] if kind == 0 else ref.at[member, i]

    kinds = ((0, rows_ref, out_ref), (1, count_ref, table_ref))

    def mine(kind, src, peer):
        return src.at[:, pl.ds(peer * held, held)] if kind == 0 else src

    def far(kind, src, dst, peer, source):
        return pltpu.make_async_remote_copy(
            src_ref=mine(kind, src, peer), dst_ref=block(kind, dst, source, t), send_sem=far_send.at[kind, peer],
            recv_sem=far_recv.at[kind, source], device_id=(peer, t), device_id_type=MESH)

    def across(kind, dst, i, to, source):
        there = block(kind, dst, i, source * 2 + c)
        return pltpu.make_async_remote_copy(
            src_ref=there, dst_ref=there, send_sem=row_send.at[kind, i, to], recv_sem=row_recv.at[kind, i, source],
            device_id=(e, to * 2 + c), device_id_type=MESH)

    def beside(kind, dst, i, source, core):
        there = block(kind, dst, i, source * 2 + core)
        return pltpu.make_async_remote_copy(
            src_ref=there, dst_ref=there, send_sem=pair_send.at[kind, i, source],
            recv_sem=pair_recv.at[kind, i, source], device_id=sibling, device_id_type=MESH)

    for kind, src, dst in kinds:
        pltpu.make_async_copy(mine(kind, src, e), block(kind, dst, e, t), own_sem.at[kind]).start()

    def send(k, _):
        peer = lax.rem(e + k, groups)
        for kind, src, dst in kinds:
            far(kind, src, dst, peer, e).start()
        return 0

    lax.fori_loop(1, groups, send, 0)
    for kind, src, dst in kinds:
        pltpu.make_async_copy(mine(kind, src, e), block(kind, dst, e, t), own_sem.at[kind]).wait()

    def pass_on(i):
        for kind, src, dst in kinds:
            for k in range(1, chips):
                across(kind, dst, i, lax.rem(y + k, chips), y).start()
            beside(kind, dst, i, y, c).start()

    def hand_over(i):
        for kind, src, dst in kinds:
            for k in range(1, chips):
                source = lax.rem(y + k, chips)
                across(kind, dst, i, source, source).wait_recv()
                beside(kind, dst, i, source, c).start()

    pass_on(e)

    def middle(k, _):
        i = lax.rem(e + groups - k, groups)
        for kind, src, dst in kinds:
            far(kind, src, dst, i, i).wait_recv()
        pass_on(i)
        hand_over(lax.rem(i + 1, groups))
        return 0

    lax.fori_loop(1, groups, middle, 0)
    hand_over(lax.rem(e + 1, groups))

    def finish(k, _):
        i = lax.rem(e + groups - k, groups)
        for kind, src, dst in kinds:
            for source in range(chips):
                beside(kind, dst, i, source, 1 - c).wait_recv()
                beside(kind, dst, i, source, c).wait_send()
            for j in range(1, chips):
                across(kind, dst, i, lax.rem(y + j, chips), y).wait_send()
        return 0

    lax.fori_loop(0, groups, finish, 0)

    def drain(k, _):
        peer = lax.rem(e + k, groups)
        for kind, src, dst in kinds:
            far(kind, src, dst, peer, e).wait_send()
        return 0

    lax.fori_loop(1, groups, drain, 0)


def dispatch(rows, count, groups, members):
    kinds, experts, slots, width = rows.shape
    chips = members // 2
    any_space = pl.BlockSpec(memory_space=pl.ANY)
    dma = pltpu.SemaphoreType.DMA
    return pl.pallas_call(
        functools.partial(dispatch_kernel, groups, chips),
        out_shape=(jax.ShapeDtypeStruct((kinds, experts // groups, members, groups, slots, width), BF16),
                   jax.ShapeDtypeStruct((members, groups) + count.shape, jnp.int32)),
        in_specs=[any_space, any_space],
        out_specs=(any_space, any_space),
        scratch_shapes=[dma((2,)), dma((2, groups)), dma((2, groups)), dma((2, groups, chips)), dma((2, groups, chips)),
                        dma((2, groups, chips)), dma((2, groups, chips))],
        compiler_params=pltpu.CompilerParams(collective_id=1, has_side_effects=True),
        name="dispatch",
    )(rows, count)


def collect_kernel(groups, chips, part_ref, out_ref, own_ref, pair_ref, row_ref, ready_ref,
                   own_sem, last_sem, pair_send, pair_recv, row_send, row_recv, far_send, far_recv):
    e, t, y, c = entry_barrier(groups, chips)
    kinds, held = part_ref.shape[:2]
    sibling = (e, t + 1 - 2 * c)

    def local(i, to):
        return pltpu.make_async_copy(part_ref.at[:, :, to * 2 + c, i], own_ref.at[to, i], own_sem.at[to, i])

    def beside(i, to):
        return pltpu.make_async_remote_copy(
            src_ref=part_ref.at[:, :, to * 2 + 1 - c, i], dst_ref=pair_ref.at[to, i], send_sem=pair_send.at[to, i],
            recv_sem=pair_recv.at[to, i], device_id=sibling, device_id_type=MESH)

    def across(i, to, source):
        return pltpu.make_async_remote_copy(
            src_ref=own_ref.at[to, i], dst_ref=row_ref.at[source, i], send_sem=row_send.at[to, i],
            recv_sem=row_recv.at[source, i], device_id=(e, to * 2 + c), device_id_type=MESH)

    def far(i, source):
        return pltpu.make_async_remote_copy(
            src_ref=ready_ref.at[i], dst_ref=out_ref.at[:, pl.ds(source * held, held)], send_sem=far_send.at[i],
            recv_sem=far_recv.at[source], device_id=(i, t), device_id_type=MESH)

    def turn(k):
        return lax.rem(e + k, groups)

    def start(k, _):
        i = turn(k)
        for j in range(1, chips + 1):
            to = lax.rem(y + j, chips)
            local(i, to).start()
            beside(i, to).start()
        return 0

    lax.fori_loop(1, groups + 1, start, 0)

    def first(k, _):
        i = turn(k)
        for j in range(1, chips):
            to = lax.rem(y + j, chips)
            local(i, to).wait()
            beside(i, to).wait_recv()
            for a in range(kinds):
                for x in range(held):
                    own_ref[to, i, a, x] = (own_ref[to, i, a, x].astype(F32) + pair_ref[to, i, a, x].astype(F32)).astype(BF16)
            across(i, to, y).start()
        local(i, y).wait()
        beside(i, y).wait_recv()
        return 0

    lax.fori_loop(1, groups + 1, first, 0)

    def total(i):
        for j in range(1, chips):
            source = lax.rem(y + j, chips)
            across(i, source, source).wait_recv()
        for a in range(kinds):
            for x in range(held):
                value = own_ref[y, i, a, x].astype(F32) + pair_ref[y, i, a, x].astype(F32)
                for j in range(1, chips):
                    value = value + row_ref[lax.rem(y + j, chips), i, a, x].astype(F32)
                ready_ref[i, a, x] = value.astype(BF16)

    def second(k, _):
        i = turn(k)
        total(i)
        far(i, e).start()
        return 0

    lax.fori_loop(1, groups, second, 0)
    total(e)
    last = pltpu.make_async_copy(ready_ref.at[e], out_ref.at[:, pl.ds(e * held, held)], last_sem)
    last.start()

    def finish(k, _):
        i = turn(k)
        far(i, e).wait_send()
        far(i, i).wait_recv()
        return 0

    lax.fori_loop(1, groups, finish, 0)

    def drain(k, _):
        i = turn(k)
        for j in range(1, chips + 1):
            beside(i, lax.rem(y + j, chips)).wait_send()
        for j in range(1, chips):
            across(i, lax.rem(y + j, chips), y).wait_send()
        return 0

    lax.fori_loop(1, groups + 1, drain, 0)
    last.wait()


def collect(parts, groups, members):
    kinds, held, _, _, slots, width = parts.shape
    chips = members // 2
    any_space = pl.BlockSpec(memory_space=pl.ANY)
    dma = pltpu.SemaphoreType.DMA
    block = (kinds, held, slots, width)
    return pl.pallas_call(
        functools.partial(collect_kernel, groups, chips),
        out_shape=jax.ShapeDtypeStruct((kinds, held * groups, slots, width), BF16),
        in_specs=[any_space],
        out_specs=any_space,
        scratch_shapes=[pltpu.VMEM((chips, groups) + block, BF16), pltpu.VMEM((chips, groups) + block, BF16),
                        pltpu.VMEM((chips, groups) + block, BF16), pltpu.VMEM((groups,) + block, BF16),
                        dma((chips, groups)), dma(()), dma((chips, groups)), dma((chips, groups)),
                        dma((chips, groups)), dma((chips, groups)), dma((groups,)), dma((groups,))],
        compiler_params=pltpu.CompilerParams(collective_id=2, has_side_effects=True, vmem_limit_bytes=60 << 20),
        name="collect",
    )(parts)


def expert_kernel(rows_ref, mask_ref, up_ref, down_ref, out_ref, gup_ref, gdown_ref):
    @pl.when(pl.program_id(1) == 0)
    def _():
        gup_ref[...] = jnp.zeros_like(gup_ref)
        gdown_ref[...] = jnp.zeros_like(gdown_ref)

    x = rows_ref[0, 0]
    d = (rows_ref[1, 0].astype(F32) * mask_ref[0]).astype(BF16)
    up, down = up_ref[0], down_ref[0]
    pre = mxu(x, up, NN)
    cdf = 0.5 * (1.0 + lax.erf(pre * 0.7071067811865476))
    hidden = (pre * cdf).astype(BF16)
    slope = cdf + pre * (0.3989422804014327 * jnp.exp(-0.5 * pre * pre))
    out_ref[0, 0] = mxu(hidden, down, NN).astype(BF16)
    d_pre = (mxu(d, down, NT) * slope).astype(BF16)
    out_ref[1, 0] = mxu(d_pre, up, NT).astype(BF16)
    gdown_ref[0] += mxu(hidden, d, TN)
    gup_ref[0] += mxu(x, d_pre, TN)


def expert_block(rows, mask, w_up, w_down, block=256):
    kinds, held, count, width = rows.shape
    hidden = w_up.shape[2]
    both = pl.BlockSpec((kinds, 1, block, width), lambda x, r: (0, x, r, 0))
    up = pl.BlockSpec((1, width, hidden), lambda x, r: (x, 0, 0))
    down = pl.BlockSpec((1, hidden, width), lambda x, r: (x, 0, 0))
    return pl.pallas_call(
        expert_kernel,
        grid=(held, count // block),
        out_shape=(jax.ShapeDtypeStruct(rows.shape, BF16), jax.ShapeDtypeStruct(w_up.shape, F32),
                   jax.ShapeDtypeStruct(w_down.shape, F32)),
        in_specs=[both, pl.BlockSpec((1, block, 1), lambda x, r: (x, r, 0)), up, down],
        out_specs=(both, up, down),
        compiler_params=pltpu.CompilerParams(vmem_limit_bytes=60 << 20),
        name="experts",
    )(rows, mask, w_up, w_down)


ORDER = (0, 1, 4, 2, 5, 3, 6, 7)
WINDOW, AHEAD = 3, 2


def visit_kernel(groups, members, capacity, send_ref, count_ref, up_ref, down_ref,
                 out_ref, gup_ref, gdown_ref, here_ref,
                 rows_ref, parts_ref, hidden_ref, dpre_ref, pair_ref, row_ref, table_ref, grad_ref, prior_ref,
                 own_sem, last_sem, grad_sem, count_send, count_recv, far_send, far_recv, row_send, row_recv,
                 core_send, core_recv, pair_send, pair_recv, back_send, back_recv, home_send, home_recv):
    kinds, held = rows_ref.shape[:2]
    slots, width = rows_ref.shape[4:]
    chips = members // 2
    devices = groups * members
    e, t = lax.axis_index("ep"), lax.axis_index("tp")
    y, c = t // 2, lax.rem(t, 2)
    me = e * members + t
    sibling = (e, t + 1 - 2 * c)

    def other(k):
        d = lax.rem(me + k, devices)
        return d, (d // members, lax.rem(d, members))

    def far(peer, source):
        return pltpu.make_async_remote_copy(
            src_ref=send_ref.at[:, pl.ds(peer * held, held)], dst_ref=rows_ref.at[:, :, source, t],
            send_sem=far_send.at[peer], recv_sem=far_recv.at[source], device_id=(peer, t), device_id_type=MESH)

    def tell(to, device, source):
        return pltpu.make_async_remote_copy(
            src_ref=count_ref, dst_ref=table_ref.at[source], send_sem=count_send.at[to],
            recv_sem=count_recv.at[source], device_id=device, device_id_type=MESH)

    def across(i, to, source):
        there = rows_ref.at[:, :, i, source * 2 + c]
        return pltpu.make_async_remote_copy(
            src_ref=there, dst_ref=there, send_sem=row_send.at[i, to], recv_sem=row_recv.at[i, source],
            device_id=(e, to * 2 + c), device_id_type=MESH)

    def beside(i, source, core):
        there = rows_ref.at[:, :, i, source * 2 + core]
        return pltpu.make_async_remote_copy(
            src_ref=there, dst_ref=there, send_sem=core_send.at[i, source], recv_sem=core_recv.at[i, source],
            device_id=sibling, device_id_type=MESH)

    def to_pair(i, to):
        return pltpu.make_async_remote_copy(
            src_ref=parts_ref.at[:, :, i, to * 2 + 1 - c], dst_ref=pair_ref.at[i, to], send_sem=pair_send.at[i, to],
            recv_sem=pair_recv.at[i, to], device_id=sibling, device_id_type=MESH)

    def lap(source, to):
        return lax.rem(source - to - 1 + 2 * chips, chips)

    def to_row(i, to, source):
        return pltpu.make_async_remote_copy(
            src_ref=pair_ref.at[i, to], dst_ref=row_ref.at[i, lap(source, to)], send_sem=back_send.at[i, to],
            recv_sem=back_recv.at[i, source], device_id=(e, to * 2 + c), device_id_type=MESH)

    def from_row(i, source):
        there = row_ref.at[i, lap(source, y)]
        return pltpu.make_async_remote_copy(
            src_ref=there, dst_ref=there, send_sem=back_send.at[i, source], recv_sem=back_recv.at[i, source],
            device_id=(e, source * 2 + c), device_id_type=MESH)

    def home(i, source):
        return pltpu.make_async_remote_copy(
            src_ref=pair_ref.at[i, y], dst_ref=out_ref.at[:, pl.ds(source * held, held)], send_sem=home_send.at[i],
            recv_sem=home_recv.at[source], device_id=(i, t), device_id_type=MESH)

    def came(n):
        out, k, span = 0, 0, groups * groups
        for m in range(groups):
            k = k + ORDER[m] * ((span - (n - m) * (n - m)) // span)
        for b in range(groups.bit_length() - 1):
            w = 1 << b
            mine, its = lax.rem(e // w, 2), lax.rem(k // w, 2)
            out = out + w * (mine + its - 2 * mine * its)
        return out

    own = pltpu.make_async_copy(send_ref.at[:, pl.ds(e * held, held)], rows_ref.at[:, :, e, t], own_sem)
    own.start()
    barrier = pltpu.get_barrier_semaphore()

    def greet(k, _):
        pl.semaphore_signal(barrier, inc=1, device_id=other(k)[1], device_id_type=MESH)
        return 0

    lax.fori_loop(1, devices, greet, 0)
    pl.semaphore_wait(barrier, devices - 1)

    def send(k, _):
        far(came(k), e).start()
        return 0

    lax.fori_loop(1, WINDOW, send, 0)

    def spread(k, _):
        d, device = other(k)
        tell(d, device, me).start()
        return 0

    lax.fori_loop(1, devices, spread, 0)
    table_ref[me] = count_ref[...]
    own.wait()

    def pass_on(k):
        i = came(k)

        @pl.when(k > 0)
        def _():
            far(i, i).wait_recv()

        @pl.when((k >= WINDOW - AHEAD) & (k + AHEAD < groups))
        def _():
            far(came(k + AHEAD), e).start()

        for j in range(1, chips):
            across(i, lax.rem(y + j, chips), y).start()
        beside(i, y, c).start()

    def hand_over(k):
        i = came(k)
        for j in range(1, chips):
            source = lax.rem(y + j, chips)
            across(i, source, source).wait_recv()
            beside(i, source, c).start()

    def ranks():
        def hear(k, _):
            d, device = other(k)
            tell(d, device, d).wait_recv()
            return 0

        lax.fori_loop(1, devices, hear, 0)
        counts = table_ref[:, 0, :].astype(F32).astype(BF16)
        row = lax.broadcasted_iota(jnp.int32, (devices, devices), 0)
        col = lax.broadcasted_iota(jnp.int32, (devices, devices), 1)
        prior_ref[...] = mxu((col < row).astype(BF16), counts, NN)
        top = lax.broadcasted_iota(jnp.int32, (8, 128), 0) == 0
        here_ref[...] = jnp.where(top, prior_ref[pl.ds(me, 1), :], mxu(jnp.ones((8, devices), BF16), counts, NN))

    def compute(k):
        i = came(k)
        for source in range(chips):
            beside(i, source, 1 - c).wait_recv()
        for x in range(held):
            lane = lax.broadcasted_iota(jnp.int32, (1, 128), 1)
            place = lax.broadcasted_iota(jnp.int32, (slots, 1), 0).astype(F32)
            kept = []
            for j in range(members):
                prior = prior_ref[pl.ds(i * members + j, 1), :]
                prior = jnp.sum(jnp.where(lane == e * held + x, prior, 0.0), axis=1, keepdims=True)
                kept.append((prior + place < capacity).astype(F32))
            kept = jnp.concatenate(kept, axis=0)
            rows = rows_ref[0, x, i].reshape(members * slots, width)
            grads = rows_ref[1, x, i].reshape(members * slots, width)
            pre = mxu(rows, up_ref[x], NN)
            cdf = 0.5 * (1.0 + lax.erf(pre * 0.7071067811865476))
            hidden = (pre * cdf * kept).astype(BF16)
            slope = (cdf + pre * (0.3989422804014327 * jnp.exp(-0.5 * pre * pre))) * kept
            hidden_ref[x, i] = hidden
            parts_ref[0, x, i] = mxu(hidden, down_ref[x], NN).astype(BF16).reshape(members, slots, width)
            d_pre = (mxu(grads, down_ref[x], NT) * slope).astype(BF16)
            dpre_ref[x, i] = d_pre
            parts_ref[1, x, i] = mxu(d_pre, up_ref[x], NT).astype(BF16).reshape(members, slots, width)
        for to in range(chips):
            to_pair(i, to).start()

    def first(k):
        i = came(k)
        for j in range(1, chips + 1):
            to = lax.rem(y + j, chips)
            to_pair(i, to).wait_recv()
            if j < chips:
                for a in range(kinds):
                    for x in range(held):
                        mine = parts_ref[a, x, i, to * 2 + c].astype(F32)
                        pair_ref[i, to, a, x] = (mine + pair_ref[i, to, a, x].astype(F32)).astype(BF16)
                to_row(i, to, y).start()

    def second(k):
        i = came(k)
        for j in range(1, chips):
            source = lax.rem(y + j, chips)
            from_row(i, source).wait_recv()
        for a in range(kinds):
            for x in range(held):
                value = parts_ref[a, x, i, t].astype(F32) + pair_ref[i, y, a, x].astype(F32)
                for j in range(chips - 1):
                    value = value + row_ref[i, j, a, x].astype(F32)
                pair_ref[i, y, a, x] = value.astype(BF16)

        @pl.when(k > 0)
        def _():
            home(i, e).start()

    def slot(n, _):
        @pl.when((n >= 4) & (n < groups + 4))
        def _():
            second(n - 4)

        @pl.when((n >= 3) & (n < groups + 3))
        def _():
            first(n - 3)

        @pl.when(n < groups)
        def _():
            pass_on(n)

        @pl.when((n >= 1) & (n < groups + 1))
        def _():
            hand_over(n - 1)

        @pl.when(n == 2)
        def _():
            ranks()

        @pl.when((n >= 2) & (n < groups + 2))
        def _():
            compute(n - 2)
        return 0

    lax.fori_loop(0, groups + 2, slot, 0)

    def weight_grad(n, x, buffer, which):
        if which == 0:
            left, right, dst = hidden_ref, rows_ref.at[1], gdown_ref
        else:
            left, right, dst = rows_ref.at[0], dpre_ref, gup_ref
        total = mxu(left[x].reshape(-1, width), right[x].reshape(-1, width), TN)
        grad_ref[buffer] = total
        return pltpu.make_async_copy(grad_ref.at[buffer], dst.at[x], grad_sem.at[n])

    copies = []
    plan = [(x, which) for x in range(held) for which in range(2)]
    for n, (x, which) in enumerate(plan):
        if n >= 2:
            copies[n - 2].wait()
        copies.append(weight_grad(n, x, n % 2, which))
        copies[n].start()
        if n < 2:
            slot(groups + 2 + n, 0)
    last = pltpu.make_async_copy(pair_ref.at[e, y], out_ref.at[:, pl.ds(e * held, held)], last_sem)
    last.start()
    for n in range(max(0, len(plan) - 2), len(plan)):
        copies[n].wait()

    def finish(k, _):
        i = lax.rem(e + k, groups)
        home(i, e).wait_send()
        home(i, i).wait_recv()
        far(i, e).wait_send()
        return 0

    lax.fori_loop(1, groups, finish, 0)

    def drain(i, _):
        for source in range(chips):
            beside(i, source, c).wait_send()
            to_pair(i, source).wait_send()
        for j in range(1, chips):
            to = lax.rem(y + j, chips)
            across(i, to, y).wait_send()
            to_row(i, to, y).wait_send()
        return 0

    lax.fori_loop(0, groups, drain, 0)

    def told(k, _):
        d, device = other(k)
        tell(d, device, me).wait_send()
        return 0

    lax.fori_loop(1, devices, told, 0)
    last.wait()


def expert_visit(rows, count, w_up, w_down, groups, members, capacity):
    kinds, experts, slots, width = rows.shape
    held, hidden = w_up.shape[0], w_up.shape[2]
    chips, devices = members // 2, groups * members
    any_space = pl.BlockSpec(memory_space=pl.ANY)
    vmem = pl.BlockSpec(memory_space=pltpu.VMEM)
    dma = pltpu.SemaphoreType.DMA
    block = (kinds, held, slots, width)
    buffer = pltpu.VMEM((kinds, held, groups, members, slots, width), BF16)
    return pl.pallas_call(
        functools.partial(visit_kernel, groups, members, capacity),
        out_shape=(jax.ShapeDtypeStruct(rows.shape, BF16), jax.ShapeDtypeStruct(w_up.shape, F32),
                   jax.ShapeDtypeStruct(w_down.shape, F32), jax.ShapeDtypeStruct((8, 128), F32)),
        in_specs=[any_space, vmem, vmem, vmem],
        out_specs=(any_space, any_space, any_space, vmem),
        scratch_shapes=[buffer, buffer, pltpu.VMEM((held, groups, members * slots, hidden), BF16),
                        pltpu.VMEM((held, groups, members * slots, hidden), BF16),
                        pltpu.VMEM((groups, chips) + block, BF16), pltpu.VMEM((groups, chips - 1) + block, BF16),
                        pltpu.VMEM((devices,) + count.shape, jnp.int32), pltpu.VMEM((2,) + w_up.shape[1:], F32), pltpu.VMEM((devices, 128), F32),
                        dma(()), dma(()), dma((2 * held,)), dma((devices,)), dma((devices,)), dma((groups,)), dma((groups,)),
                        dma((groups, chips)), dma((groups, chips)), dma((groups, chips)), dma((groups, chips)),
                        dma((groups, chips)), dma((groups, chips)), dma((groups, chips)), dma((groups, chips)),
                        dma((groups,)), dma((groups,))],
        compiler_params=pltpu.CompilerParams(collective_id=3, has_side_effects=True, vmem_limit_bytes=60 << 20),
        name="expert_visit",
    )(rows, count, w_up, w_down)


def expert_steps(rows, count, w_up, w_down, groups, members, capacity):
    _, experts, slots, width = rows.shape
    held = w_up.shape[0]
    rows, table = dispatch(rows, count, groups, members)
    everyone = table[:, :, 0, :experts].transpose(1, 0, 2).reshape(groups * members, experts)
    device = jnp.arange(groups * members)
    before = device[None, :] < device[:, None]
    prior = jnp.sum(jnp.where(before[:, :, None], everyone[None], 0), axis=1)
    named = jnp.sum(everyone, axis=0)
    mine = lax.dynamic_slice_in_dim(prior.reshape(groups, members, experts), lax.axis_index("ep") * held, held, 2)
    room = mine.transpose(2, 1, 0)[..., None] + jnp.arange(slots)[None, None, None] < capacity
    room = room.reshape(held, members * groups * slots, 1).astype(F32)
    parts, grad_up, grad_down = expert_block(rows.reshape(2, held, members * groups * slots, width), room, w_up, w_down)
    return collect(parts.reshape(rows.shape), groups, members), grad_up, grad_down, prior, named


def local(tokens, d_out, segment, route, gain_one, w_in, conv_w, conv_b, w_x, w_dt, b_dt, a_log, d_skip, w_out,
          gain_two, w_router, w_up, w_down):
    length, width = tokens.shape
    inner = w_in.shape[1] // 2
    experts = w_router.shape[1]
    groups, members = lax.axis_size("ep"), lax.axis_size("tp")
    slots = 3 * length // (2 * experts)
    capacity = 5 * length * groups * members // (4 * experts)
    rank, states, taps = w_dt.shape[0], a_log.shape[0], conv_w.shape[0]
    used = rank + 2 * states
    labels = (segment.reshape(-1, 128), route.reshape(-1, 128))
    rows = (conv_w, conv_b, b_dt, d_skip, gain_one, gain_two) + labels
    normed, both, wx, wxt, wdt, rates, vec, column, route = front(tokens, rows, w_in, w_x.T, w_dt, a_log)
    gated, *saved, proj, starts = mid_fwd(both, column, vec, wx, wdt, rates, rank)
    after, leaving, count, aux = route_out(gated, w_out, tokens, d_out, column, route, vec, w_router.T, slots)
    leaving = leaving.reshape(2, experts, slots, width)
    if members == 4:
        back, grad_up, grad_down, here = expert_visit(leaving, count, w_up, w_down, groups, members, capacity)
    else:
        back, grad_up, grad_down, prior, named = expert_steps(leaving, count, w_up, w_down, groups, members, capacity)
        this = jnp.arange(groups * members) == lax.axis_index(("ep", "tp"))
        here = jnp.stack([jnp.sum(jnp.where(this[:, None], prior, 0), axis=0), named]).astype(F32)
        here = jnp.pad(here, ((0, 6), (0, 128 - experts)))
    final, d_after, d_mixed, d_gated, g_two, g_router, counts = come_home(
        back.reshape(2, experts * slots, width), after, d_out, aux, column, route, here, vec, w_router.T, w_out, slots,
        capacity,
    )
    d_both, g_vec, g_x, g_dt, g_rates = mid_bwd(
        both, d_gated, saved, proj, starts, column, vec, wxt, wdt, rates, rank
    )
    total, d_tokens = tail_sum(
        normed, d_both, w_in, gated, d_mixed, tokens, d_after, vec, g_two, g_x, g_dt, g_rates, rates, g_vec, g_router, used,
        rank, groups, members,
    )
    total_in, total_out, total_x, total_router, total_dt, total_log, total_taps, total_bias, total_step, total_skip, *gains, up_rows, down_rows, d_tokens = (
        unpack_grads(total, (grad_up.reshape(-1, w_up.shape[2]), grad_down.reshape(-1, width), d_tokens), width, inner, used, experts, (rank, states, taps))
    )
    return (
        final,
        d_tokens,
        counts,
        gains[0],
        total_in,
        total_taps,
        total_bias,
        total_x.T,
        total_dt,
        total_step,
        total_log,
        total_skip,
        total_out,
        gains[1],
        total_router[:, :width].T,
        up_rows.reshape(w_up.shape),
        down_rows.reshape(w_down.shape),
    )


def solution(mesh):
    in_specs = (
        P(("ep", "tp"), None),
        P(("ep", "tp"), None),
        P(("ep", "tp")),
        P(("ep", "tp"), None),
        P(),
        P(),
        P(),
        P(),
        P(),
        P(),
        P(),
        P(),
        P(),
        P(),
        P(),
        P(),
        P("ep", None, "tp"),
        P("ep", "tp", None),
    )
    out_specs = (
        P(("ep", "tp"), None),
        P(("ep", "tp"), None),
        P(),
        P(),
        P(),
        P(),
        P(),
        P(),
        P(),
        P(),
        P(),
        P(),
        P(),
        P(),
        P(),
        P("ep", None, "tp"),
        P("ep", "tp", None),
    )
    return jax.shard_map(local, mesh=mesh, in_specs=in_specs, out_specs=out_specs, check_vma=False)
```

```python
import functools

import jax
import jax.numpy as jnp
from jax import lax
from jax.experimental import pallas as pl
from jax.experimental.pallas import tpu as pltpu
from jax.sharding import PartitionSpec as P

EPS = 1e-06
MESH = pl.DeviceIdType.MESH
TB = 128
CH = 16
LB = 256
LOG2E = 1.4426950408889634
LN2 = 0.6931471805599453
F32 = jnp.float32
BF16 = jnp.bfloat16
NN = (((1,), (0,)), ((), ()))
NT = (((1,), (1,)), ((), ()))
TN = (((0,), (0,)), ((), ()))


def mxu(left, right, dims):
    return lax.dot_general(left, right, dims, preferred_element_type=F32)


def split(x):
    high = x.astype(BF16)
    return high, (x - high.astype(F32)).astype(BF16)


def dot2(x, w, dims):
    high, rest = split(x)
    return mxu(high, w, dims) + mxu(rest, w, dims)


def dot3(x, w, dims):
    high, rest = split(x)
    high_w, rest_w = split(w)
    return mxu(high, high_w, dims) + mxu(high, rest_w, dims) + mxu(rest, high_w, dims)


def sigmoid(x):
    return 1.0 / (1.0 + jnp.exp(-x))


def softplus(x):
    return jnp.maximum(x, 0.0) + jnp.log1p(jnp.exp(-jnp.abs(x)))


def row_sums(items):
    items = [sum((x[8 * i:8 * i + 8] for i in range(1, x.shape[0] // 8)), x[:8]) for x in items]
    place = lax.broadcasted_iota(jnp.int32, items[0].shape, 0)
    for level in (1, 2, 4):
        odd = (place // level) % 2 == 1
        merged = []
        for low, high in zip(items[::2], items[1::2]):
            merged.append(jnp.where(odd, high, low) + pltpu.roll(jnp.where(odd, low, high), level, 0))
        items = merged
    return items[0]


def mid_fwd_kernel(rank, both_ref, segment_ref, vec_ref, wx_ref, wdt_ref, rates_ref,
                   gated_ref, conv_ref, bend_ref, step_ref, rise_ref, gate_ref, slope_ref, proj_ref, hs_ref,
                   ext_ref, h_ref, turned_ref, seg_ref, spread_ref, decay_ref, source_ref, pdt_ref):
    states, width = rates_ref.shape

    @pl.when(pl.program_id(0) == 0)
    def _():
        ext_ref[:8, :] = jnp.zeros((8, width), F32)
        seg_ref[:8, :] = jnp.full((8, 128), -2, jnp.int32)
        h_ref[...] = jnp.zeros_like(h_ref)

    @pl.when(pl.program_id(0) > 0)
    def _():
        ext_ref[:8, :] = ext_ref[TB:, :]
        seg_ref[:8, :] = seg_ref[TB:, :]

    seg_ref[8:, :] = segment_ref[...]

    def same(c, k):
        at = c * CH + 8
        return (seg_ref[at - k:at - k + CH, :] == seg_ref[at:at + CH, :]).astype(F32)[:, :1]

    def conv_chunk(c):
        rows = slice(c * CH, c * CH + CH)
        masks = [same(c, k) for k in range(1, 4)]
        for b in range(width // LB):
            lanes = slice(b * LB, (b + 1) * LB)
            at = c * CH + 8
            here = both_ref[rows, lanes]
            ext_ref[at:at + CH, lanes] = here
            total = vec_ref[4:5, lanes] + vec_ref[3:4, lanes] * here
            for k in range(1, 4):
                total = total + vec_ref[3 - k:4 - k, lanes] * ext_ref[at - k:at - k + CH, lanes] * masks[k - 1]
            sig = sigmoid(total)
            conv_ref[rows, lanes] = total * sig
            bend_ref[rows, lanes] = sig * (1.0 + total * (1.0 - sig))

    for c in range(TB // CH):
        conv_chunk(c)
    proj = dot2(conv_ref[...], wx_ref[...], NN)
    lane = lax.broadcasted_iota(jnp.int32, (TB, 128), 1)
    keep = (seg_ref[7:7 + TB, :] == seg_ref[8:, :]).astype(F32)
    proj_ref[...] = jnp.where(lane == 127, keep, proj)
    turned_ref[...] = proj.T
    pdt_ref[...] = dot2(proj, wdt_ref[...], NN) + vec_ref[5:6, :]

    def every(ref, k):
        row = ref[pl.ds(k, 8, stride=0), :]
        return jnp.concatenate([row] * (states // 8), axis=0)

    def wide(k, side):
        return jnp.concatenate([spread_ref[k, side * states:(side + 1) * states, :]] * (LB // 128), axis=1)

    def scan_chunk(c, _):
        rows = pl.ds(pl.multiple_of(c * CH, CH), CH)
        tile = pltpu.roll(turned_ref[rank:rank + 2 * states, :], TB - c * CH, 1)
        keep = proj_ref[rows, 127:]
        for k in range(CH):
            spread_ref[k] = jnp.broadcast_to(tile[:, k:k + 1], (2 * states, 128))
        for b in range(width // LB):
            lanes = slice(b * LB, (b + 1) * LB)
            rates = rates_ref[:, lanes]
            h = h_ref[:, lanes]
            hs_ref[c, :, lanes] = h
            conv = conv_ref[rows, lanes]
            pdt = pdt_ref[rows, lanes]
            step = softplus(pdt)
            step_ref[rows, lanes] = step
            rise_ref[rows, lanes] = sigmoid(pdt)
            source_ref[b, :CH] = step * conv
            decay_ref[b, :CH] = jnp.where(keep > 0.0, step, 1e4)
            outs = []
            for k in range(CH):
                h = jnp.exp2(every(decay_ref.at[b], k) * rates) * h + wide(k, 0) * every(source_ref.at[b], k)
                outs.append(wide(k, 1) * h)
            h_ref[:, lanes] = h
            y = jnp.concatenate([row_sums(outs[:8]), row_sums(outs[8:])], axis=0)
            gate = both_ref[rows, width + b * LB:width + (b + 1) * LB]
            sig = sigmoid(gate)
            mixed = y + vec_ref[6:7, lanes] * conv
            gate_ref[rows, lanes] = gate * sig
            gated_ref[rows, lanes] = (mixed * (gate * sig)).astype(BF16)
            slope_ref[rows, lanes] = mixed * (sig * (1.0 + gate * (1.0 - sig)))
        return 0

    lax.fori_loop(0, TB // CH, scan_chunk, 0)


def mid_fwd(both, segment, vec, wx, wdt, rates, rank):
    length = both.shape[0]
    states, width = rates.shape
    row = lambda i: (i, 0)
    fix = lambda i: (0, 0)
    tall = pl.BlockSpec((TB, width), row)
    like = jax.ShapeDtypeStruct((length, width), F32)
    return pl.pallas_call(
        functools.partial(mid_fwd_kernel, rank),
        grid=(length // TB,),
        out_shape=(jax.ShapeDtypeStruct((length, width), BF16), like, like, like, like, like, like,
                   jax.ShapeDtypeStruct((length, 128), F32),
                   jax.ShapeDtypeStruct((length // CH, states, width), F32)),
        in_specs=[pl.BlockSpec((TB, 2 * width), row), pl.BlockSpec((TB, 128), row), pl.BlockSpec(vec.shape, fix),
                  pl.BlockSpec(wx.shape, fix), pl.BlockSpec(wdt.shape, fix), pl.BlockSpec(rates.shape, fix)],
        out_specs=(tall, tall, tall, tall, tall, tall, tall, pl.BlockSpec((TB, 128), row),
                   pl.BlockSpec((TB // CH, states, width), lambda i: (i, 0, 0))),
        scratch_shapes=[pltpu.VMEM((TB + 8, width), F32),
                        pltpu.VMEM((states, width), F32), pltpu.VMEM((128, TB), F32),
                        pltpu.VMEM((TB + 8, 128), jnp.int32), pltpu.VMEM((CH, 2 * states, 128), F32),
                        pltpu.VMEM((width // LB, CH + 8, LB), F32), pltpu.VMEM((width // LB, CH + 8, LB), F32),
                        pltpu.VMEM((TB, width), F32)],
        compiler_params=pltpu.CompilerParams(vmem_limit_bytes=60 << 20),
        name="mid_fwd",
    )(both, segment, vec, wx, wdt, rates)


def mid_bwd_kernel(rank, both_ref, dg_ref, conv_ref, bend_ref, step_ref, rise_ref, gate_ref, slope_ref, proj_ref, hs_ref, segment_ref, vec_ref, wxt_ref,
                   wdt_ref, rates_ref,
                   dboth_ref, gvec_ref, gwx_ref, gwdt_ref, gr_ref,
                   ext_ref, g_ref, dec_ref, p_ref, part_ref, dproj_ref, dconv_ref, dpdt_ref, turned_ref,
                   acc_ref, seg_ref, spread_ref, decay_ref, source_ref, dy_ref):
    states, width = rates_ref.shape
    steps = TB // CH

    @pl.when(pl.program_id(0) == 0)
    def _():
        ext_ref[TB:, :] = jnp.zeros((8, width), F32)
        seg_ref[TB:, :] = jnp.full((8, 128), -2, jnp.int32)
        g_ref[...] = jnp.zeros_like(g_ref)
        acc_ref[...] = jnp.zeros_like(acc_ref)
        gwx_ref[...] = jnp.zeros_like(gwx_ref)
        gwdt_ref[...] = jnp.zeros_like(gwdt_ref)
        gr_ref[...] = jnp.zeros_like(gr_ref)

    @pl.when(pl.program_id(0) > 0)
    def _():
        ext_ref[TB:, :] = ext_ref[:8, :]
        seg_ref[TB:, :] = seg_ref[:8, :]

    turned_ref[...] = proj_ref[...].T
    seg_ref[:TB, :] = segment_ref[...]
    ones = jnp.ones((128, 128), BF16)
    lane = lax.broadcasted_iota(jnp.int32, (2 * states, 128), 1)
    place = lax.broadcasted_iota(jnp.int32, (2 * states, 128), 0) + rank

    def fold(x):
        out = x[:, :128]
        for i in range(1, LB // 128):
            out = out + x[:, i * 128:(i + 1) * 128]
        return out

    def halves(x):
        out = x[:8]
        for i in range(1, CH // 8):
            out = out + x[i * 8:(i + 1) * 8]
        return out

    def every(ref, k):
        row = ref[pl.ds(k, 8, stride=0), :]
        return jnp.concatenate([row] * (states // 8), axis=0)

    def wide(k, side):
        return jnp.concatenate([spread_ref[k, side * states:(side + 1) * states, :]] * (LB // 128), axis=1)

    def scan_chunk(i, _):
        c = steps - 1 - i
        rows = pl.ds(pl.multiple_of(c * CH, CH), CH)
        tile = pltpu.roll(turned_ref[rank:rank + 2 * states, :], TB - c * CH, 1)
        keep = proj_ref[rows, 127:]
        for k in range(CH):
            spread_ref[k] = jnp.broadcast_to(tile[:, k:k + 1], (2 * states, 128))
        for b in range(width // LB):
            lanes = slice(b * LB, (b + 1) * LB)
            rates = rates_ref[:, lanes]
            h = hs_ref[c, :, lanes]
            conv = conv_ref[rows, lanes]
            step = step_ref[rows, lanes]
            source_ref[b, :CH] = step * conv
            decay_ref[b, :CH] = jnp.where(keep > 0.0, step, 1e4)
            skip = vec_ref[6:7, lanes]
            dg = dg_ref[rows, lanes]
            dboth_ref[rows, width + b * LB:width + (b + 1) * LB] = (dg * slope_ref[rows, lanes]).astype(BF16)
            dy = dg * gate_ref[rows, lanes]
            dy_ref[b, :CH] = dy
            for k in range(CH):
                dec = jnp.exp2(every(decay_ref.at[b], k) * rates)
                p = dec * h
                dec_ref[k] = dec
                p_ref[k] = p
                h = p + wide(k, 0) * every(source_ref.at[b], k)
                out = fold(every(dy_ref.at[b], k) * h)
                part_ref[k, states:, :] = out if b == 0 else part_ref[k, states:, :] + out
            g = g_ref[:, lanes]
            dr = gr_ref[:, lanes]
            dus, dss = [None] * CH, [None] * CH
            for k in reversed(range(CH)):
                dh = g + wide(k, 1) * every(dy_ref.at[b], k)
                out = fold(dh * every(source_ref.at[b], k))
                part_ref[k, :states, :] = out if b == 0 else part_ref[k, :states, :] + out
                dus[k] = halves(dh * wide(k, 0))
                da = dh * p_ref[k]
                dss[k] = halves(da * rates)
                dr = dr + da * every(decay_ref.at[b], k)
                g = dec_ref[k] * dh
            g_ref[:, lanes] = g
            gr_ref[:, lanes] = dr
            du = jnp.concatenate([row_sums(dus[:8]), row_sums(dus[8:])], axis=0)
            dpdt = (jnp.concatenate([row_sums(dss[:8]), row_sums(dss[8:])], axis=0) * LN2 + du * conv) * rise_ref[rows, lanes]
            dpdt_ref[rows, lanes] = dpdt
            dconv_ref[rows, lanes] = dy * skip + du * step
            acc_ref[5, :, lanes] += halves(dpdt)
            acc_ref[6, :, lanes] += halves(dy * conv)
        high, rest = split(part_ref[...].reshape(CH * 2 * states, 128))
        sums = (mxu(high, ones, NN) + mxu(rest, ones, NN)).reshape(CH, 2 * states, 128)
        picked = jnp.where((lane == place)[None], sums, 0.0)
        dproj_ref[rows, :] = jnp.sum(picked, axis=1)
        return 0

    lax.fori_loop(0, steps, scan_chunk, 0)
    dpdt = dpdt_ref[...]
    dproj = dproj_ref[...] + dot2(dpdt, wdt_ref[...], NT)
    gwdt_ref[...] += dot3(turned_ref[...], dpdt, NN)
    gwx_ref[...] += dot3(dproj.T, conv_ref[...], NN)
    dconv_ref[...] += dot2(dproj, wxt_ref[...], NN)

    def act_chunk(c, _):
        rows = pl.ds(pl.multiple_of(c * CH, CH), CH)
        ext_ref[rows, :] = dconv_ref[rows, :] * bend_ref[rows, :]
        return 0

    lax.fori_loop(0, steps, act_chunk, 0)

    def conv_chunk(c):
        at = c * CH
        rows = slice(at, at + CH)
        masks = [(seg_ref[at + k:at + k + CH, :] == seg_ref[rows, :]).astype(F32)[:, :1] for k in range(1, 4)]
        for b in range(width // LB):
            lanes = slice(b * LB, (b + 1) * LB)
            inner = both_ref[rows, lanes]
            here = ext_ref[rows, lanes]
            total = vec_ref[3:4, lanes] * here
            acc_ref[4, :, lanes] += halves(here)
            acc_ref[3, :, lanes] += halves(here * inner)
            for k in range(1, 4):
                later = ext_ref[at + k:at + k + CH, lanes] * masks[k - 1]
                total = total + vec_ref[3 - k:4 - k, lanes] * later
                acc_ref[3 - k, :, lanes] += halves(later * inner)
            dboth_ref[rows, lanes] = total.astype(BF16)

    for c in range(steps):
        conv_chunk(c)

    @pl.when(pl.program_id(0) == pl.num_programs(0) - 1)
    def _():
        gvec_ref[...] = jnp.concatenate(
            [jnp.sum(acc_ref[k], axis=0, keepdims=True) for k in range(8)], axis=0)


def mid_bwd(both, dg, saved, proj, hs, segment, vec, wxt, wdt, rates, rank):
    length = both.shape[0]
    states, width = rates.shape
    blocks = length // TB
    row = lambda i: (blocks - 1 - i, 0)
    fix = lambda i: (0, 0)
    tall = pl.BlockSpec((TB, width), row)
    return pl.pallas_call(
        functools.partial(mid_bwd_kernel, rank),
        grid=(blocks,),
        out_shape=(jax.ShapeDtypeStruct((length, 2 * width), BF16), jax.ShapeDtypeStruct((8, width), F32),
                   jax.ShapeDtypeStruct((128, width), F32), jax.ShapeDtypeStruct((128, width), F32),
                   jax.ShapeDtypeStruct((states, width), F32)),
        in_specs=[tall, tall] + [tall] * 6 + [pl.BlockSpec((TB, 128), row),
                  pl.BlockSpec((TB // CH, states, width), lambda i: (blocks - 1 - i, 0, 0)),
                  pl.BlockSpec((TB, 128), row), pl.BlockSpec(vec.shape, fix), pl.BlockSpec(wxt.shape, fix),
                  pl.BlockSpec(wdt.shape, fix), pl.BlockSpec(rates.shape, fix)],
        out_specs=(pl.BlockSpec((TB, 2 * width), row), pl.BlockSpec((8, width), fix),
                   pl.BlockSpec((128, width), fix), pl.BlockSpec((128, width), fix), pl.BlockSpec((states, width), fix)),
        scratch_shapes=[pltpu.VMEM((TB + 8, width), F32), pltpu.VMEM((states, width), F32),
                        pltpu.VMEM((CH, states, LB), F32), pltpu.VMEM((CH, states, LB), F32),
                        pltpu.VMEM((CH, 2 * states, 128), F32), pltpu.VMEM((TB, 128), F32),
                        pltpu.VMEM((TB, width), F32), pltpu.VMEM((TB, width), F32),
                        pltpu.VMEM((128, TB), F32), pltpu.VMEM((8, 8, width), F32),
                        pltpu.VMEM((TB + 8, 128), jnp.int32), pltpu.VMEM((CH, 2 * states, 128), F32),
                        pltpu.VMEM((width // LB, CH + 8, LB), F32), pltpu.VMEM((width // LB, CH + 8, LB), F32), pltpu.VMEM((width // LB, CH + 8, LB), F32)],
        compiler_params=pltpu.CompilerParams(vmem_limit_bytes=60 << 20),
        name="mid_bwd",
    )(both, dg, *saved, proj, hs, segment, vec, wxt, wdt, rates)


CHUNK = (256, 1024)


def bit_orders(groups, members):
    ep_bits, tp_bits = groups.bit_length() - 1, members.bit_length() - 1
    x = [("ep", b) for b in range(ep_bits - 2)]
    z = [("ep", b) for b in range(ep_bits - 2, ep_bits)]
    y = [("tp", b) for b in range(1, tp_bits)]
    core = [("tp", 0)]
    return [core + x + y + z, core + y + x + z, core + x + z + y, core + y + z + x]


def region_sizes(stages, rows, cols):
    sizes = []
    for _ in range(stages):
        if rows > 16:
            rows //= 2
            sizes.append((rows, cols, True))
        else:
            cols //= 2
            sizes.append((rows, cols, False))
    return sizes


def sum_scratch(chunks, stages):
    return [pltpu.VMEM((chunks, r, c), BF16) for r, c, _ in region_sizes(stages, *CHUNK)] + [
        pltpu.VMEM((chunks,) + CHUNK, BF16),
        pltpu.VMEM((chunks,) + CHUNK, BF16),
        pltpu.SemaphoreType.DMA((2 * stages, chunks)),
        pltpu.SemaphoreType.DMA((2 * stages, chunks)),
        pltpu.SemaphoreType.DMA((chunks,)),
    ]


def sum_steps(orders, g_ref, out_ref, scratch):
    stages = len(orders[0])
    land = scratch[:stages]
    work_ref, full_ref, send_sem, recv_sem, done_sem = scratch[stages:]
    sizes = region_sizes(stages, *CHUNK)
    me = {"ep": lax.axis_index("ep"), "tp": lax.axis_index("tp")}

    def bit(stage):
        axis, b = stage
        return lax.rem(me[axis] // (1 << b), 2)

    def partner(stage):
        axis, b = stage
        there = dict(me)
        there[axis] = me[axis] + (1 << b) - 2 * (1 << b) * bit(stage)
        return (there["ep"], there["tp"])

    def greet():
        barrier = pltpu.get_barrier_semaphore()
        for stage in orders[0]:
            pl.semaphore_signal(barrier, inc=1, device_id=partner(stage), device_id_type=MESH)
        pl.semaphore_wait(barrier, stages)

    def part(c, order, upto, flip):
        r0, c0 = 0, 0
        for s in range(upto + 1):
            b = bit(order[s])
            if s == upto and flip:
                b = 1 - b
            if sizes[s][2]:
                r0 = r0 + b * sizes[s][0]
            else:
                c0 = c0 + b * sizes[s][1]
        return (c, pl.ds(pl.multiple_of(r0, 16), sizes[upto][0]),
                pl.ds(c0 if isinstance(c0, int) else pl.multiple_of(c0, 128), sizes[upto][1]))

    def scatter(s, v, c):
        order = orders[v]
        return pltpu.make_async_remote_copy(
            src_ref=(g_ref if s == 0 else work_ref).at[part(c, order, s, True)], dst_ref=land[s].at[c],
            send_sem=send_sem.at[s, c], recv_sem=recv_sem.at[s, c], device_id=partner(order[s]), device_id_type=MESH)

    def gather(s, v, c, flip=False):
        order = orders[v]
        piece = full_ref.at[part(c, order, s, flip)]
        return pltpu.make_async_remote_copy(
            src_ref=piece, dst_ref=piece, send_sem=send_sem.at[stages + s, c], recv_sem=recv_sem.at[stages + s, c],
            device_id=partner(order[s]), device_id_type=MESH)

    def done(c):
        return pltpu.make_async_copy(full_ref.at[c], out_ref.at[c], done_sem.at[c])

    def step(n, v, c):
        if n == 0:
            scatter(0, v, c).start()
        elif n <= stages:
            s = n - 1
            scatter(s, v, c).wait_recv()
            where = part(c, orders[v], s, False)
            total = ((g_ref if s == 0 else work_ref)[where].astype(F32) + land[s][c].astype(F32)).astype(BF16)
            if s + 1 < stages:
                work_ref[where] = total
                scatter(s + 1, v, c).start()
            else:
                full_ref[where] = total
                gather(s, v, c).start()
        else:
            s = 2 * stages - n
            gather(s, v, c, True).wait_recv()
            if s > 0:
                gather(s - 1, v, c).start()
            else:
                done(c).start()

    def settle(v, c):
        for s in range(stages):
            scatter(s, v, c).wait_send()
            gather(s, v, c).wait_send()
        done(c).wait()

    return greet, step, settle, 2 * stages + 1


def tail_kernel(orders, tall, across, used, rank, normed_ref, d_both_ref, vec_ref, g_two_ref, gx_ref, gdt_ref, gr_ref,
                rates_ref, gvec_ref, router_ref, w_in_hbm, gated_hbm, d_mixed_hbm, tokens_hbm, d_after_hbm,
                out_ref, d_tokens_ref, g_ref, gains_ref, w_in_ref, gated_ref, d_mixed_ref, tokens_ref, d_after_ref, load_sem,
                *scratch):
    greet, step, settle, steps = sum_steps(orders, g_ref, out_ref, scratch)
    kinds, chunks = len(orders), g_ref.shape[0]
    rows, cols = CHUNK
    width = d_mixed_ref.shape[1]
    loads = [pltpu.make_async_copy(src, dst, load_sem.at[n]) for n, (src, dst) in enumerate(
        ((w_in_hbm, w_in_ref), (tokens_hbm, tokens_ref), (d_after_hbm, d_after_ref), (gated_hbm, gated_ref),
         (d_mixed_hbm, d_mixed_ref)))]
    for load in loads:
        load.start()
    greet()

    def produce(c):
        @pl.when(c < tall)
        def _():
            left = pl.multiple_of(c // across * rows, rows)
            right = pl.multiple_of(lax.rem(c, across) * cols, cols)
            g_ref[c] = mxu(normed_ref[:, pl.ds(left, rows)], d_both_ref[:, pl.ds(right, cols)], TN).astype(BF16)

        @pl.when(c >= tall)
        def _():
            at = pl.ds(pl.multiple_of((c - tall) * rows, rows), rows)
            g_ref[c, :, :width] = mxu(gated_ref[:, at], d_mixed_ref[...], TN).astype(BF16)
            pieces = [gx_ref[:used, at], gdt_ref[:rank, at], gr_ref[:, at] * rates_ref[:, at] * LN2, gvec_ref[:, at],
                      gains_ref[:, at]]
            high = sum(p.shape[0] for p in pieces) + router_ref.shape[0]
            pieces += [jnp.zeros((256 - high, rows), F32), router_ref[:, at]]
            g_ref[c, :, width:] = jnp.concatenate(pieces, axis=0).T.astype(BF16)

    def input_grads():
        for load in loads[:3]:
            load.wait()
        values = tokens_ref[...].astype(F32)
        scale = lax.rsqrt(jnp.mean(values * values, axis=-1, keepdims=True) + EPS)
        plain = values * scale
        d_normed = mxu(d_both_ref[...], w_in_ref[...], NT)
        gains_ref[:, :width] = jnp.broadcast_to(jnp.sum(d_normed * plain, axis=0, keepdims=True), (8, width))
        gains_ref[:, width:] = g_two_ref[...]
        d_plain = d_normed * vec_ref[7:8, :width]
        d_tokens_ref[...] = d_after_ref[...] + scale * (d_plain - plain * jnp.mean(d_plain * plain, axis=-1, keepdims=True))
        for load in loads[3:]:
            load.wait()

    waves = -(-chunks // kinds)
    ready = tall // kinds

    def slot(i, _):
        for n in reversed(range(1, steps)):
            group = i - n
            for v in range(kinds):
                c = group * kinds + v

                @pl.when((group >= 0) & (c < chunks))
                def _(n=n, v=v, c=c):
                    step(n, v, c)

        @pl.when(i == ready)
        def _():
            input_grads()

        def begin(v, _):
            c = i * kinds + v

            @pl.when(c < chunks)
            def _():
                produce(c)
                step(0, 0, c)
            return 0

        lax.fori_loop(0, kinds, begin, 0)
        return 0

    lax.fori_loop(0, waves + steps - 1, slot, 0)

    def drain(group, _):
        for v in range(kinds):
            c = group * kinds + v

            @pl.when(c < chunks)
            def _(v=v, c=c):
                settle(v, c)
        return 0

    lax.fori_loop(0, waves, drain, 0)


SUM_ORDERS = (0, 1, 2, 3)


def tail_sum(normed, d_both, w_in, gated, d_mixed, tokens, d_after, vec, g_two, gx, gdt, gr, rates, gvec, router, used, rank,
             groups, members):
    length, width = normed.shape
    rows, cols = CHUNK
    across = d_both.shape[1] // cols
    tall = width // rows * across
    chunks = tall + gated.shape[1] // rows
    orders = [bit_orders(groups, members)[v] for v in SUM_ORDERS]
    vmem, anywhere = pl.BlockSpec(memory_space=pltpu.VMEM), pl.BlockSpec(memory_space=pl.ANY)
    held = lambda a: pltpu.VMEM(a.shape, a.dtype)
    return pl.pallas_call(
        functools.partial(tail_kernel, orders, tall, across, used, rank),
        out_shape=(jax.ShapeDtypeStruct((chunks,) + CHUNK, BF16), jax.ShapeDtypeStruct((length, width), F32)),
        in_specs=[vmem] * 10 + [anywhere] * 5,
        out_specs=(anywhere, vmem),
        scratch_shapes=[pltpu.VMEM((chunks,) + CHUNK, BF16), pltpu.VMEM((8, 2 * width), F32), held(w_in), held(gated),
                        held(d_mixed), held(tokens), held(d_after), pltpu.SemaphoreType.DMA((5,))]
        + sum_scratch(chunks, len(orders[0])),
        compiler_params=pltpu.CompilerParams(collective_id=0, has_side_effects=True, vmem_limit_bytes=60 << 20),
        name="tail_sum",
    )(normed, d_both, vec, g_two, gx, gdt, gr, rates, gvec, router, w_in, gated, d_mixed, tokens, d_after)


CARRIED = 3


def unpack_kernel(tall_ref, wide_ref, *refs):
    sources, refs = refs[:CARRIED], refs[CARRIED:]
    in_ref, out_ref, x_ref, router_ref, *row_refs = refs[:-CARRIED]
    in_ref[...] = tall_ref[0].astype(F32)

    @pl.when(pl.program_id(0) < 8)
    def _():
        for source, target in zip(sources, refs[-CARRIED:]):
            target[...] = source[...]

    width = out_ref.shape[1]

    @pl.when(pl.program_id(0) < pl.num_programs(0) * 2 // 3)
    def _():
        out_ref[...] = wide_ref[0, :, :width].astype(F32)
        small = wide_ref[0, :, width:].astype(F32)
        turned = small.T
        at = x_ref.shape[0]
        x_ref[...] = turned[:at]
        router_ref[...] = turned[256 - router_ref.shape[0] :]
        for ref in row_refs[:3]:
            ref[...] = turned[at : at + ref.shape[0]]
            at += ref.shape[0]
        for ref in row_refs[3:6]:
            ref[...] = turned[at]
            at += 1
        c, half = pl.program_id(0), width // CHUNK[0]

        @pl.when(c < half)
        def _():
            row_refs[6][...] = turned[at + 1]

        @pl.when(c >= half)
        def _():
            row_refs[7][...] = turned[at + 1]


def unpack_grads(total, carried, width, inner, used, experts, heights):
    rows, cols = CHUNK
    across = 2 * inner // cols
    tall, wide = width // rows * across, inner // rows
    hold = lambda c: jnp.minimum(c, wide - 1)
    half = width // rows
    eighth = [pl.BlockSpec((a.shape[0] // 8, a.shape[1]), lambda c: (jnp.minimum(c, 7), 0)) for a in carried]
    return pl.pallas_call(
        unpack_kernel,
        grid=(tall,),
        out_shape=(jax.ShapeDtypeStruct((width, 2 * inner), F32), jax.ShapeDtypeStruct((inner, width), F32),
                   jax.ShapeDtypeStruct((used, inner), F32), jax.ShapeDtypeStruct((experts, inner), F32))
        + tuple(jax.ShapeDtypeStruct((h, inner), F32) for h in heights)
        + tuple(jax.ShapeDtypeStruct((w,), F32) for w in (inner, inner, inner, width, width))
        + tuple(jax.ShapeDtypeStruct(a.shape, a.dtype) for a in carried),
        in_specs=[pl.BlockSpec((1,) + CHUNK, lambda c: (c, 0, 0)),
                  pl.BlockSpec((1,) + CHUNK, lambda c: (tall + hold(c), 0, 0))] + eighth,
        out_specs=(pl.BlockSpec(CHUNK, lambda c: (c // across, lax.rem(c, across))),
                   pl.BlockSpec((rows, width), lambda c: (hold(c), 0)),
                   pl.BlockSpec((used, rows), lambda c: (0, hold(c))),
                   pl.BlockSpec((experts, rows), lambda c: (0, hold(c))))
        + tuple(pl.BlockSpec((h, rows), lambda c: (0, hold(c))) for h in heights)
        + (pl.BlockSpec((rows,), lambda c: (hold(c),)),) * 3
        + (pl.BlockSpec((rows,), lambda c: (jnp.minimum(c, half - 1),)), pl.BlockSpec((rows,), lambda c: (jnp.maximum(hold(c) - half, 0),)))
        + tuple(eighth),
        compiler_params=pltpu.CompilerParams(vmem_limit_bytes=60 << 20),
        name="unpack_grads",
    )(total, total, *carried)


def front_kernel(rank, used, tokens_ref, taps_ref, bias_ref, step_ref, skip_ref, gain_one_ref, gain_two_ref, segment_ref,
                 route_ref, w_in_ref, wx_ref, wdt_ref, log_ref,
                 normed_ref, both_ref, wx_out, wxt_out, wdt_out, rates_out, vec_ref, segment_out, route_out):
    @pl.when(pl.program_id(0) == 0)
    def _():
        values = tokens_ref[...].astype(F32)
        width = values.shape[1]
        vec_ref[:4, :] = taps_ref[...].astype(F32)
        for n, ref in ((4, bias_ref), (5, step_ref), (6, skip_ref)):
            vec_ref[n:n + 1, :] = ref[...].astype(F32).reshape(1, -1)
        vec_ref[7:8, :width] = gain_one_ref[...].astype(F32).reshape(1, -1)
        vec_ref[7:8, width:] = gain_two_ref[...].astype(F32).reshape(1, -1)
        for source, target in ((segment_ref, segment_out), (route_ref, route_out)):
            for n in range(source.shape[0]):
                row = source[n:n + 1, :].astype(F32)
                target[n * 128:(n + 1) * 128, :] = jnp.broadcast_to(row, (128, 128)).T.astype(jnp.int32)
        scale = lax.rsqrt(jnp.mean(values * values, axis=-1, keepdims=True) + EPS)
        normed_ref[...] = (values * scale * vec_ref[7:8, :width]).astype(BF16)
        wxt_out[...] = jnp.zeros_like(wxt_out)
        wxt_out[:used, :] = wx_ref[...]
        wx_out[...] = wxt_out[...].astype(F32).T.astype(BF16)
        wdt_out[...] = jnp.zeros_like(wdt_out)
        wdt_out[:rank, :] = wdt_ref[...]
        rates_out[...] = -jnp.exp(log_ref[...].astype(F32)) * LOG2E

    both_ref[...] = mxu(normed_ref[...], w_in_ref[...], NN)


def front(tokens, rows, w_in, w_x, w_dt, a_log):
    length, width = tokens.shape
    used, inner = w_x.shape
    rank, states = w_dt.shape[0], a_log.shape[0]
    cols = inner // 2
    fix = lambda a: pl.BlockSpec(a, lambda j: (0,) * len(a))
    return pl.pallas_call(
        functools.partial(front_kernel, rank, used),
        grid=(w_in.shape[1] // cols,),
        out_shape=(jax.ShapeDtypeStruct((length, width), BF16), jax.ShapeDtypeStruct((length, w_in.shape[1]), F32),
                   jax.ShapeDtypeStruct((inner, 128), BF16), jax.ShapeDtypeStruct((128, inner), BF16),
                   jax.ShapeDtypeStruct((128, inner), BF16), jax.ShapeDtypeStruct((states, inner), F32),
                   jax.ShapeDtypeStruct((8, inner), F32), jax.ShapeDtypeStruct((length, 128), jnp.int32),
                   jax.ShapeDtypeStruct((length, 128), jnp.int32)),
        in_specs=[fix(tokens.shape)] + [fix(a.shape) for a in rows] + [ pl.BlockSpec((width, cols), lambda j: (0, j)), fix(w_x.shape),
                  fix(w_dt.shape), fix(a_log.shape)],
        out_specs=(fix((length, width)), pl.BlockSpec((length, cols), lambda j: (0, j)), fix((inner, 128)),
                   fix((128, inner)), fix((128, inner)), fix((states, inner)), fix((8, inner)), fix((length, 128)),
                   fix((length, 128))),
        compiler_params=pltpu.CompilerParams(vmem_limit_bytes=60 << 20),
        name="front",
    )(tokens, *rows, w_in, w_x, w_dt, a_log)


def choose(experts, segment, route):
    lane = lax.broadcasted_iota(jnp.int32, (segment.shape[0], 128), 1)
    return (lane == route) & (segment >= 0)


def route_kernel(slots, gated_ref, w_out_ref, tokens_ref, d_out_ref, segment_ref, route_ref, gain_ref, w_router_ref,
                 after_ref, leaving_ref, count_ref, aux_ref):
    length, width = tokens_ref.shape
    experts = w_router_ref.shape[0]
    segment, route = segment_ref[:, :1], route_ref[:, :1]
    picked = choose(experts, segment, route)
    picks = picked.astype(F32)
    row = lax.broadcasted_iota(jnp.int32, (length, length), 0)
    col = lax.broadcasted_iota(jnp.int32, (length, length), 1)
    upto = mxu((col <= row).astype(BF16), picks.astype(BF16), NN)
    rank = jnp.sum(picks * upto, axis=1, keepdims=True) - 1.0
    slot = jnp.where(segment >= 0, route * slots + rank.astype(jnp.int32), -1)
    count_ref[...] = jnp.broadcast_to(jnp.sum(picks, axis=0, keepdims=True).astype(jnp.int32), count_ref.shape)

    mixed = mxu(gated_ref[...], w_out_ref[...], NN)
    after = tokens_ref[...].astype(F32) + jnp.where(segment >= 0, mixed, 0.0)
    after_ref[...] = after
    normed = after * lax.rsqrt(jnp.mean(after * after, axis=-1, keepdims=True) + EPS) * gain_ref[7:8, width:]
    logits = dot2(normed, w_router_ref[...], NT)
    logits = logits - jnp.max(logits, axis=-1, keepdims=True)
    weights = jnp.exp(logits)
    probs = weights / jnp.sum(weights, axis=-1, keepdims=True)
    aux_ref[...] = jnp.zeros_like(aux_ref)
    aux_ref[:, :experts] = probs
    gate = jnp.sum(aux_ref[...] * picks, axis=1, keepdims=True)
    lane = lax.broadcasted_iota(jnp.int32, (length, 128), 1)
    extra = jnp.where(lane == 125, rank, jnp.where(lane == 126, slot.astype(F32), jnp.where(lane == 127, gate, 0.0)))
    aux_ref[...] += extra
    places = (lax.broadcasted_iota(jnp.int32, (length, experts * slots), 1) == slot).astype(BF16)
    leaving_ref[0] = mxu(places, normed.astype(BF16), TN).astype(BF16)
    leaving_ref[1] = mxu(places, (gate * d_out_ref[...].astype(F32)).astype(BF16), TN).astype(BF16)


def route_out(gated, w_out, tokens, d_out, segment, route, gain, w_router, slots):
    length, width = tokens.shape
    experts = w_router.shape[0]
    return pl.pallas_call(
        functools.partial(route_kernel, slots),
        out_shape=(jax.ShapeDtypeStruct((length, width), F32), jax.ShapeDtypeStruct((2, experts * slots, width), BF16),
                   jax.ShapeDtypeStruct((8, 128), jnp.int32), jax.ShapeDtypeStruct((length, 128), F32)),
        compiler_params=pltpu.CompilerParams(vmem_limit_bytes=60 << 20),
        name="route_out",
    )(gated, w_out, tokens, d_out, segment, route, gain, w_router)


def home_kernel(slots, capacity, back_ref, after_ref, d_out_ref, aux_ref, segment_ref, route_ref, here_ref, gain_ref,
                w_router_ref, w_out_ref, final_ref, d_after_ref, d_mixed_ref, d_gated_ref, g_gain_ref, g_router_ref,
                counts_ref):
    length, width = after_ref.shape
    experts = w_router_ref.shape[0]
    segment, route, aux = segment_ref[:, :1], route_ref[:, :1], aux_ref[...]
    picks = choose(experts, segment, route).astype(F32)
    lane = lax.broadcasted_iota(jnp.int32, (length, 128), 1)
    rank, slot, gate = (jnp.sum(jnp.where(lane == n, aux, 0.0), axis=1, keepdims=True) for n in (125, 126, 127))
    prior = jnp.sum(picks * here_ref[0:1, :], axis=1, keepdims=True)
    keep = jnp.where((segment >= 0) & (prior + rank < capacity), 1.0, 0.0)
    named = here_ref[1:2, :].astype(jnp.int32)
    counts_ref[0:1, :] = named[:, :experts]
    counts_ref[1:2, :] = jnp.maximum(named - capacity, 0)[:, :experts]

    places = (lax.broadcasted_iota(jnp.int32, (length, experts * slots), 1) == slot.astype(jnp.int32)).astype(BF16)
    token_out = mxu(places, back_ref[0], NN)
    upstream = d_out_ref[...].astype(F32)
    after = after_ref[...]
    final_ref[...] = (after + gate * keep * token_out).astype(BF16)
    d_gate = keep * jnp.sum(upstream * token_out, axis=1, keepdims=True)
    probs = jnp.where(lane < experts, aux, 0.0)
    d_logits = (gate * d_gate * (picks - probs))[:, :experts]
    scale = lax.rsqrt(jnp.mean(after * after, axis=-1, keepdims=True) + EPS)
    plain = after * scale
    gain = gain_ref[7:8, width:]
    g_router_ref[...] = jnp.zeros_like(g_router_ref)
    g_router_ref[:, :width] = dot3(d_logits, plain * gain, TN)
    d_normed = mxu(places, back_ref[1], NN) + dot2(d_logits, w_router_ref[...], NN)
    g_gain_ref[...] = jnp.broadcast_to(jnp.sum(d_normed * plain, axis=0, keepdims=True), g_gain_ref.shape)
    d_plain = d_normed * gain
    d_after = upstream + scale * (d_plain - plain * jnp.mean(d_plain * plain, axis=-1, keepdims=True))
    d_after_ref[...] = d_after
    d_mixed = jnp.where(segment >= 0, d_after, 0.0).astype(BF16)
    d_mixed_ref[...] = d_mixed
    d_gated_ref[...] = mxu(d_mixed, w_out_ref[...], NT)


def come_home(back, after, d_out, aux, segment, route, here, gain, w_router, w_out, slots, capacity):
    length, width = after.shape
    inner, experts = w_out.shape[0], w_router.shape[0]
    return pl.pallas_call(
        functools.partial(home_kernel, slots, capacity),
        out_shape=(jax.ShapeDtypeStruct((length, width), BF16), jax.ShapeDtypeStruct((length, width), F32),
                   jax.ShapeDtypeStruct((length, width), BF16), jax.ShapeDtypeStruct((length, inner), F32),
                   jax.ShapeDtypeStruct((8, width), F32), jax.ShapeDtypeStruct((experts, inner), F32),
                   jax.ShapeDtypeStruct((2, experts), jnp.int32)),
        compiler_params=pltpu.CompilerParams(vmem_limit_bytes=60 << 20),
        name="come_home",
    )(back, after, d_out, aux, segment, route, here, gain, w_router, w_out)


def entry_barrier(groups, chips):
    e, t = lax.axis_index("ep"), lax.axis_index("tp")
    y, c = t // 2, lax.rem(t, 2)
    barrier = pltpu.get_barrier_semaphore()
    for k in range(1, groups):
        pl.semaphore_signal(barrier, inc=1, device_id=(lax.rem(e + k, groups), t), device_id_type=MESH)
    for k in range(1, chips):
        pl.semaphore_signal(barrier, inc=1, device_id=(e, lax.rem(y + k, chips) * 2 + c), device_id_type=MESH)
    pl.semaphore_signal(barrier, inc=1, device_id=(e, t + 1 - 2 * c), device_id_type=MESH)
    pl.semaphore_wait(barrier, groups + chips - 1)
    return e, t, y, c


def dispatch_kernel(groups, chips, rows_ref, count_ref, out_ref, table_ref,
                    own_sem, far_send, far_recv, row_send, row_recv, pair_send, pair_recv):
    e, t, y, c = entry_barrier(groups, chips)
    held = rows_ref.shape[1] // groups
    sibling = (e, t + 1 - 2 * c)

    def block(kind, ref, i, member):
        return ref.at[:, :, member, i] if kind == 0 else ref.at[member, i]

    kinds = ((0, rows_ref, out_ref), (1, count_ref, table_ref))

    def mine(kind, src, peer):
        return src.at[:, pl.ds(peer * held, held)] if kind == 0 else src

    def far(kind, src, dst, peer, source):
        return pltpu.make_async_remote_copy(
            src_ref=mine(kind, src, peer), dst_ref=block(kind, dst, source, t), send_sem=far_send.at[kind, peer],
            recv_sem=far_recv.at[kind, source], device_id=(peer, t), device_id_type=MESH)

    def across(kind, dst, i, to, source):
        there = block(kind, dst, i, source * 2 + c)
        return pltpu.make_async_remote_copy(
            src_ref=there, dst_ref=there, send_sem=row_send.at[kind, i, to], recv_sem=row_recv.at[kind, i, source],
            device_id=(e, to * 2 + c), device_id_type=MESH)

    def beside(kind, dst, i, source, core):
        there = block(kind, dst, i, source * 2 + core)
        return pltpu.make_async_remote_copy(
            src_ref=there, dst_ref=there, send_sem=pair_send.at[kind, i, source],
            recv_sem=pair_recv.at[kind, i, source], device_id=sibling, device_id_type=MESH)

    for kind, src, dst in kinds:
        pltpu.make_async_copy(mine(kind, src, e), block(kind, dst, e, t), own_sem.at[kind]).start()

    def send(k, _):
        peer = lax.rem(e + k, groups)
        for kind, src, dst in kinds:
            far(kind, src, dst, peer, e).start()
        return 0

    lax.fori_loop(1, groups, send, 0)
    for kind, src, dst in kinds:
        pltpu.make_async_copy(mine(kind, src, e), block(kind, dst, e, t), own_sem.at[kind]).wait()

    def pass_on(i):
        for kind, src, dst in kinds:
            for k in range(1, chips):
                across(kind, dst, i, lax.rem(y + k, chips), y).start()
            beside(kind, dst, i, y, c).start()

    def hand_over(i):
        for kind, src, dst in kinds:
            for k in range(1, chips):
                source = lax.rem(y + k, chips)
                across(kind, dst, i, source, source).wait_recv()
                beside(kind, dst, i, source, c).start()

    pass_on(e)

    def middle(k, _):
        i = lax.rem(e + groups - k, groups)
        for kind, src, dst in kinds:
            far(kind, src, dst, i, i).wait_recv()
        pass_on(i)
        hand_over(lax.rem(i + 1, groups))
        return 0

    lax.fori_loop(1, groups, middle, 0)
    hand_over(lax.rem(e + 1, groups))

    def finish(k, _):
        i = lax.rem(e + groups - k, groups)
        for kind, src, dst in kinds:
            for source in range(chips):
                beside(kind, dst, i, source, 1 - c).wait_recv()
                beside(kind, dst, i, source, c).wait_send()
            for j in range(1, chips):
                across(kind, dst, i, lax.rem(y + j, chips), y).wait_send()
        return 0

    lax.fori_loop(0, groups, finish, 0)

    def drain(k, _):
        peer = lax.rem(e + k, groups)
        for kind, src, dst in kinds:
            far(kind, src, dst, peer, e).wait_send()
        return 0

    lax.fori_loop(1, groups, drain, 0)


def dispatch(rows, count, groups, members):
    kinds, experts, slots, width = rows.shape
    chips = members // 2
    any_space = pl.BlockSpec(memory_space=pl.ANY)
    dma = pltpu.SemaphoreType.DMA
    return pl.pallas_call(
        functools.partial(dispatch_kernel, groups, chips),
        out_shape=(jax.ShapeDtypeStruct((kinds, experts // groups, members, groups, slots, width), BF16),
                   jax.ShapeDtypeStruct((members, groups) + count.shape, jnp.int32)),
        in_specs=[any_space, any_space],
        out_specs=(any_space, any_space),
        scratch_shapes=[dma((2,)), dma((2, groups)), dma((2, groups)), dma((2, groups, chips)), dma((2, groups, chips)),
                        dma((2, groups, chips)), dma((2, groups, chips))],
        compiler_params=pltpu.CompilerParams(collective_id=1, has_side_effects=True),
        name="dispatch",
    )(rows, count)


def collect_kernel(groups, chips, part_ref, out_ref, own_ref, pair_ref, row_ref, ready_ref,
                   own_sem, last_sem, pair_send, pair_recv, row_send, row_recv, far_send, far_recv):
    e, t, y, c = entry_barrier(groups, chips)
    kinds, held = part_ref.shape[:2]
    sibling = (e, t + 1 - 2 * c)

    def local(i, to):
        return pltpu.make_async_copy(part_ref.at[:, :, to * 2 + c, i], own_ref.at[to, i], own_sem.at[to, i])

    def beside(i, to):
        return pltpu.make_async_remote_copy(
            src_ref=part_ref.at[:, :, to * 2 + 1 - c, i], dst_ref=pair_ref.at[to, i], send_sem=pair_send.at[to, i],
            recv_sem=pair_recv.at[to, i], device_id=sibling, device_id_type=MESH)

    def across(i, to, source):
        return pltpu.make_async_remote_copy(
            src_ref=own_ref.at[to, i], dst_ref=row_ref.at[source, i], send_sem=row_send.at[to, i],
            recv_sem=row_recv.at[source, i], device_id=(e, to * 2 + c), device_id_type=MESH)

    def far(i, source):
        return pltpu.make_async_remote_copy(
            src_ref=ready_ref.at[i], dst_ref=out_ref.at[:, pl.ds(source * held, held)], send_sem=far_send.at[i],
            recv_sem=far_recv.at[source], device_id=(i, t), device_id_type=MESH)

    def turn(k):
        return lax.rem(e + k, groups)

    def start(k, _):
        i = turn(k)
        for j in range(1, chips + 1):
            to = lax.rem(y + j, chips)
            local(i, to).start()
            beside(i, to).start()
        return 0

    lax.fori_loop(1, groups + 1, start, 0)

    def first(k, _):
        i = turn(k)
        for j in range(1, chips):
            to = lax.rem(y + j, chips)
            local(i, to).wait()
            beside(i, to).wait_recv()
            for a in range(kinds):
                for x in range(held):
                    own_ref[to, i, a, x] = (own_ref[to, i, a, x].astype(F32) + pair_ref[to, i, a, x].astype(F32)).astype(BF16)
            across(i, to, y).start()
        local(i, y).wait()
        beside(i, y).wait_recv()
        return 0

    lax.fori_loop(1, groups + 1, first, 0)

    def total(i):
        for j in range(1, chips):
            source = lax.rem(y + j, chips)
            across(i, source, source).wait_recv()
        for a in range(kinds):
            for x in range(held):
                value = own_ref[y, i, a, x].astype(F32) + pair_ref[y, i, a, x].astype(F32)
                for j in range(1, chips):
                    value = value + row_ref[lax.rem(y + j, chips), i, a, x].astype(F32)
                ready_ref[i, a, x] = value.astype(BF16)

    def second(k, _):
        i = turn(k)
        total(i)
        far(i, e).start()
        return 0

    lax.fori_loop(1, groups, second, 0)
    total(e)
    last = pltpu.make_async_copy(ready_ref.at[e], out_ref.at[:, pl.ds(e * held, held)], last_sem)
    last.start()

    def finish(k, _):
        i = turn(k)
        far(i, e).wait_send()
        far(i, i).wait_recv()
        return 0

    lax.fori_loop(1, groups, finish, 0)

    def drain(k, _):
        i = turn(k)
        for j in range(1, chips + 1):
            beside(i, lax.rem(y + j, chips)).wait_send()
        for j in range(1, chips):
            across(i, lax.rem(y + j, chips), y).wait_send()
        return 0

    lax.fori_loop(1, groups + 1, drain, 0)
    last.wait()


def collect(parts, groups, members):
    kinds, held, _, _, slots, width = parts.shape
    chips = members // 2
    any_space = pl.BlockSpec(memory_space=pl.ANY)
    dma = pltpu.SemaphoreType.DMA
    block = (kinds, held, slots, width)
    return pl.pallas_call(
        functools.partial(collect_kernel, groups, chips),
        out_shape=jax.ShapeDtypeStruct((kinds, held * groups, slots, width), BF16),
        in_specs=[any_space],
        out_specs=any_space,
        scratch_shapes=[pltpu.VMEM((chips, groups) + block, BF16), pltpu.VMEM((chips, groups) + block, BF16),
                        pltpu.VMEM((chips, groups) + block, BF16), pltpu.VMEM((groups,) + block, BF16),
                        dma((chips, groups)), dma(()), dma((chips, groups)), dma((chips, groups)),
                        dma((chips, groups)), dma((chips, groups)), dma((groups,)), dma((groups,))],
        compiler_params=pltpu.CompilerParams(collective_id=2, has_side_effects=True, vmem_limit_bytes=60 << 20),
        name="collect",
    )(parts)


def expert_kernel(rows_ref, mask_ref, up_ref, down_ref, out_ref, gup_ref, gdown_ref):
    @pl.when(pl.program_id(1) == 0)
    def _():
        gup_ref[...] = jnp.zeros_like(gup_ref)
        gdown_ref[...] = jnp.zeros_like(gdown_ref)

    x = rows_ref[0, 0]
    d = (rows_ref[1, 0].astype(F32) * mask_ref[0]).astype(BF16)
    up, down = up_ref[0], down_ref[0]
    pre = mxu(x, up, NN)
    cdf = 0.5 * (1.0 + lax.erf(pre * 0.7071067811865476))
    hidden = (pre * cdf).astype(BF16)
    slope = cdf + pre * (0.3989422804014327 * jnp.exp(-0.5 * pre * pre))
    out_ref[0, 0] = mxu(hidden, down, NN).astype(BF16)
    d_pre = (mxu(d, down, NT) * slope).astype(BF16)
    out_ref[1, 0] = mxu(d_pre, up, NT).astype(BF16)
    gdown_ref[0] += mxu(hidden, d, TN)
    gup_ref[0] += mxu(x, d_pre, TN)


def expert_block(rows, mask, w_up, w_down, block=256):
    kinds, held, count, width = rows.shape
    hidden = w_up.shape[2]
    both = pl.BlockSpec((kinds, 1, block, width), lambda x, r: (0, x, r, 0))
    up = pl.BlockSpec((1, width, hidden), lambda x, r: (x, 0, 0))
    down = pl.BlockSpec((1, hidden, width), lambda x, r: (x, 0, 0))
    return pl.pallas_call(
        expert_kernel,
        grid=(held, count // block),
        out_shape=(jax.ShapeDtypeStruct(rows.shape, BF16), jax.ShapeDtypeStruct(w_up.shape, F32),
                   jax.ShapeDtypeStruct(w_down.shape, F32)),
        in_specs=[both, pl.BlockSpec((1, block, 1), lambda x, r: (x, r, 0)), up, down],
        out_specs=(both, up, down),
        compiler_params=pltpu.CompilerParams(vmem_limit_bytes=60 << 20),
        name="experts",
    )(rows, mask, w_up, w_down)


ORDER = (0, 1, 4, 2, 5, 3, 6, 7)
WINDOW, AHEAD = 3, 2


def visit_kernel(groups, members, capacity, send_ref, count_ref, up_ref, down_ref,
                 out_ref, gup_ref, gdown_ref, here_ref,
                 rows_ref, parts_ref, hidden_ref, dpre_ref, pair_ref, row_ref, table_ref, grad_ref, prior_ref,
                 own_sem, last_sem, grad_sem, count_send, count_recv, far_send, far_recv, row_send, row_recv,
                 core_send, core_recv, pair_send, pair_recv, back_send, back_recv, home_send, home_recv):
    kinds, held = rows_ref.shape[:2]
    slots, width = rows_ref.shape[4:]
    chips = members // 2
    devices = groups * members
    e, t = lax.axis_index("ep"), lax.axis_index("tp")
    y, c = t // 2, lax.rem(t, 2)
    me = e * members + t
    sibling = (e, t + 1 - 2 * c)

    def other(k):
        d = lax.rem(me + k, devices)
        return d, (d // members, lax.rem(d, members))

    def far(peer, source):
        return pltpu.make_async_remote_copy(
            src_ref=send_ref.at[:, pl.ds(peer * held, held)], dst_ref=rows_ref.at[:, :, source, t],
            send_sem=far_send.at[peer], recv_sem=far_recv.at[source], device_id=(peer, t), device_id_type=MESH)

    def tell(to, device, source):
        return pltpu.make_async_remote_copy(
            src_ref=count_ref, dst_ref=table_ref.at[source], send_sem=count_send.at[to],
            recv_sem=count_recv.at[source], device_id=device, device_id_type=MESH)

    def across(i, to, source):
        there = rows_ref.at[:, :, i, source * 2 + c]
        return pltpu.make_async_remote_copy(
            src_ref=there, dst_ref=there, send_sem=row_send.at[i, to], recv_sem=row_recv.at[i, source],
            device_id=(e, to * 2 + c), device_id_type=MESH)

    def beside(i, source, core):
        there = rows_ref.at[:, :, i, source * 2 + core]
        return pltpu.make_async_remote_copy(
            src_ref=there, dst_ref=there, send_sem=core_send.at[i, source], recv_sem=core_recv.at[i, source],
            device_id=sibling, device_id_type=MESH)

    def to_pair(i, to):
        return pltpu.make_async_remote_copy(
            src_ref=parts_ref.at[:, :, i, to * 2 + 1 - c], dst_ref=pair_ref.at[i, to], send_sem=pair_send.at[i, to],
            recv_sem=pair_recv.at[i, to], device_id=sibling, device_id_type=MESH)

    def lap(source, to):
        return lax.rem(source - to - 1 + 2 * chips, chips)

    def to_row(i, to, source):
        return pltpu.make_async_remote_copy(
            src_ref=pair_ref.at[i, to], dst_ref=row_ref.at[i, lap(source, to)], send_sem=back_send.at[i, to],
            recv_sem=back_recv.at[i, source], device_id=(e, to * 2 + c), device_id_type=MESH)

    def from_row(i, source):
        there = row_ref.at[i, lap(source, y)]
        return pltpu.make_async_remote_copy(
            src_ref=there, dst_ref=there, send_sem=back_send.at[i, source], recv_sem=back_recv.at[i, source],
            device_id=(e, source * 2 + c), device_id_type=MESH)

    def home(i, source):
        return pltpu.make_async_remote_copy(
            src_ref=pair_ref.at[i, y], dst_ref=out_ref.at[:, pl.ds(source * held, held)], send_sem=home_send.at[i],
            recv_sem=home_recv.at[source], device_id=(i, t), device_id_type=MESH)

    def came(n):
        out, k, span = 0, 0, groups * groups
        for m in range(groups):
            k = k + ORDER[m] * ((span - (n - m) * (n - m)) // span)
        for b in range(groups.bit_length() - 1):
            w = 1 << b
            mine, its = lax.rem(e // w, 2), lax.rem(k // w, 2)
            out = out + w * (mine + its - 2 * mine * its)
        return out

    own = pltpu.make_async_copy(send_ref.at[:, pl.ds(e * held, held)], rows_ref.at[:, :, e, t], own_sem)
    own.start()
    barrier = pltpu.get_barrier_semaphore()

    def greet(k, _):
        pl.semaphore_signal(barrier, inc=1, device_id=other(k)[1], device_id_type=MESH)
        return 0

    lax.fori_loop(1, devices, greet, 0)
    pl.semaphore_wait(barrier, devices - 1)

    def send(k, _):
        far(came(k), e).start()
        return 0

    lax.fori_loop(1, WINDOW, send, 0)

    def spread(k, _):
        d, device = other(k)
        tell(d, device, me).start()
        return 0

    own.wait()

    def pass_on(k):
        i = came(k)

        @pl.when(k > 0)
        def _():
            far(i, i).wait_recv()

        @pl.when((k >= WINDOW - AHEAD) & (k + AHEAD < groups))
        def _():
            far(came(k + AHEAD), e).start()

        for j in range(1, chips):
            across(i, lax.rem(y + j, chips), y).start()
        beside(i, y, c).start()

    def hand_over(k):
        i = came(k)
        for j in range(1, chips):
            source = lax.rem(y + j, chips)
            across(i, source, source).wait_recv()
            beside(i, source, c).start()

    def ranks():
        def hear(k, _):
            d, device = other(k)
            tell(d, device, d).wait_recv()
            return 0

        lax.fori_loop(1, devices, hear, 0)
        counts = table_ref[:, 0, :].astype(F32).astype(BF16)
        row = lax.broadcasted_iota(jnp.int32, (devices, devices), 0)
        col = lax.broadcasted_iota(jnp.int32, (devices, devices), 1)
        prior_ref[...] = mxu((col < row).astype(BF16), counts, NN)
        top = lax.broadcasted_iota(jnp.int32, (8, 128), 0) == 0
        here_ref[...] = jnp.where(top, prior_ref[pl.ds(me, 1), :], mxu(jnp.ones((8, devices), BF16), counts, NN))

    def compute(k):
        i = came(k)
        for source in range(chips):
            beside(i, source, 1 - c).wait_recv()
        for x in range(held):
            lane = lax.broadcasted_iota(jnp.int32, (1, 128), 1)
            place = lax.broadcasted_iota(jnp.int32, (slots, 1), 0).astype(F32)
            kept = []
            for j in range(members):
                prior = prior_ref[pl.ds(i * members + j, 1), :]
                prior = jnp.sum(jnp.where(lane == e * held + x, prior, 0.0), axis=1, keepdims=True)
                kept.append((prior + place < capacity).astype(F32))
            kept = jnp.concatenate(kept, axis=0)
            rows = rows_ref[0, x, i].reshape(members * slots, width)
            grads = rows_ref[1, x, i].reshape(members * slots, width)
            pre = mxu(rows, up_ref[x], NN)
            cdf = 0.5 * (1.0 + lax.erf(pre * 0.7071067811865476))
            hidden = (pre * cdf * kept).astype(BF16)
            slope = (cdf + pre * (0.3989422804014327 * jnp.exp(-0.5 * pre * pre))) * kept
            hidden_ref[x, i] = hidden
            parts_ref[0, x, i] = mxu(hidden, down_ref[x], NN).astype(BF16).reshape(members, slots, width)
            d_pre = (mxu(grads, down_ref[x], NT) * slope).astype(BF16)
            dpre_ref[x, i] = d_pre
            parts_ref[1, x, i] = mxu(d_pre, up_ref[x], NT).astype(BF16).reshape(members, slots, width)
        for to in range(chips):
            to_pair(i, to).start()

    def first(k):
        i = came(k)
        for j in range(1, chips + 1):
            to = lax.rem(y + j, chips)
            to_pair(i, to).wait_recv()
            if j < chips:
                for a in range(kinds):
                    for x in range(held):
                        mine = parts_ref[a, x, i, to * 2 + c].astype(F32)
                        pair_ref[i, to, a, x] = (mine + pair_ref[i, to, a, x].astype(F32)).astype(BF16)
                to_row(i, to, y).start()

    def second(k):
        i = came(k)
        for j in range(1, chips):
            source = lax.rem(y + j, chips)
            from_row(i, source).wait_recv()
        for a in range(kinds):
            for x in range(held):
                value = parts_ref[a, x, i, t].astype(F32) + pair_ref[i, y, a, x].astype(F32)
                for j in range(chips - 1):
                    value = value + row_ref[i, j, a, x].astype(F32)
                pair_ref[i, y, a, x] = value.astype(BF16)

        @pl.when(k > 0)
        def _():
            home(i, e).start()

    def slot(n, _):
        @pl.when((n >= 4) & (n < groups + 4))
        def _():
            second(n - 4)

        @pl.when((n >= 3) & (n < groups + 3))
        def _():
            first(n - 3)

        @pl.when(n < groups)
        def _():
            pass_on(n)

        @pl.when(n == 0)
        def _():
            lax.fori_loop(1, devices, spread, 0)
            table_ref[me] = count_ref[...]

        @pl.when((n >= 1) & (n < groups + 1))
        def _():
            hand_over(n - 1)

        @pl.when(n == 2)
        def _():
            ranks()

        @pl.when((n >= 2) & (n < groups + 2))
        def _():
            compute(n - 2)
        return 0

    lax.fori_loop(0, groups + 2, slot, 0)

    def weight_grad(n, x, buffer, which):
        if which == 0:
            left, right, dst = hidden_ref, rows_ref.at[1], gdown_ref
        else:
            left, right, dst = rows_ref.at[0], dpre_ref, gup_ref
        total = mxu(left[x].reshape(-1, width), right[x].reshape(-1, width), TN)
        grad_ref[buffer] = total
        return pltpu.make_async_copy(grad_ref.at[buffer], dst.at[x], grad_sem.at[n])

    copies = []
    plan = [(x, which) for x in range(held) for which in range(2)]
    for n, (x, which) in enumerate(plan):
        if n >= 2:
            copies[n - 2].wait()
        copies.append(weight_grad(n, x, n % 2, which))
        copies[n].start()
        if n < 2:
            slot(groups + 2 + n, 0)
    last = pltpu.make_async_copy(pair_ref.at[e, y], out_ref.at[:, pl.ds(e * held, held)], last_sem)
    last.start()
    for n in range(max(0, len(plan) - 2), len(plan)):
        copies[n].wait()

    def finish(k, _):
        i = lax.rem(e + k, groups)
        home(i, e).wait_send()
        home(i, i).wait_recv()
        far(i, e).wait_send()
        return 0

    lax.fori_loop(1, groups, finish, 0)

    def drain(i, _):
        for source in range(chips):
            beside(i, source, c).wait_send()
            to_pair(i, source).wait_send()
        for j in range(1, chips):
            to = lax.rem(y + j, chips)
            across(i, to, y).wait_send()
            to_row(i, to, y).wait_send()
        return 0

    lax.fori_loop(0, groups, drain, 0)

    def told(k, _):
        d, device = other(k)
        tell(d, device, me).wait_send()
        return 0

    lax.fori_loop(1, devices, told, 0)
    last.wait()


def expert_visit(rows, count, w_up, w_down, groups, members, capacity):
    kinds, experts, slots, width = rows.shape
    held, hidden = w_up.shape[0], w_up.shape[2]
    chips, devices = members // 2, groups * members
    any_space = pl.BlockSpec(memory_space=pl.ANY)
    vmem = pl.BlockSpec(memory_space=pltpu.VMEM)
    dma = pltpu.SemaphoreType.DMA
    block = (kinds, held, slots, width)
    buffer = pltpu.VMEM((kinds, held, groups, members, slots, width), BF16)
    return pl.pallas_call(
        functools.partial(visit_kernel, groups, members, capacity),
        out_shape=(jax.ShapeDtypeStruct(rows.shape, BF16), jax.ShapeDtypeStruct(w_up.shape, F32),
                   jax.ShapeDtypeStruct(w_down.shape, F32), jax.ShapeDtypeStruct((8, 128), F32)),
        in_specs=[any_space, vmem, vmem, vmem],
        out_specs=(any_space, any_space, any_space, vmem),
        scratch_shapes=[buffer, buffer, pltpu.VMEM((held, groups, members * slots, hidden), BF16),
                        pltpu.VMEM((held, groups, members * slots, hidden), BF16),
                        pltpu.VMEM((groups, chips) + block, BF16), pltpu.VMEM((groups, chips - 1) + block, BF16),
                        pltpu.VMEM((devices,) + count.shape, jnp.int32), pltpu.VMEM((2,) + w_up.shape[1:], F32), pltpu.VMEM((devices, 128), F32),
                        dma(()), dma(()), dma((2 * held,)), dma((devices,)), dma((devices,)), dma((groups,)), dma((groups,)),
                        dma((groups, chips)), dma((groups, chips)), dma((groups, chips)), dma((groups, chips)),
                        dma((groups, chips)), dma((groups, chips)), dma((groups, chips)), dma((groups, chips)),
                        dma((groups,)), dma((groups,))],
        compiler_params=pltpu.CompilerParams(collective_id=3, has_side_effects=True, vmem_limit_bytes=60 << 20),
        name="expert_visit",
    )(rows, count, w_up, w_down)


def expert_steps(rows, count, w_up, w_down, groups, members, capacity):
    _, experts, slots, width = rows.shape
    held = w_up.shape[0]
    rows, table = dispatch(rows, count, groups, members)
    everyone = table[:, :, 0, :experts].transpose(1, 0, 2).reshape(groups * members, experts)
    device = jnp.arange(groups * members)
    before = device[None, :] < device[:, None]
    prior = jnp.sum(jnp.where(before[:, :, None], everyone[None], 0), axis=1)
    named = jnp.sum(everyone, axis=0)
    mine = lax.dynamic_slice_in_dim(prior.reshape(groups, members, experts), lax.axis_index("ep") * held, held, 2)
    room = mine.transpose(2, 1, 0)[..., None] + jnp.arange(slots)[None, None, None] < capacity
    room = room.reshape(held, members * groups * slots, 1).astype(F32)
    parts, grad_up, grad_down = expert_block(rows.reshape(2, held, members * groups * slots, width), room, w_up, w_down)
    return collect(parts.reshape(rows.shape), groups, members), grad_up, grad_down, prior, named


def local(tokens, d_out, segment, route, gain_one, w_in, conv_w, conv_b, w_x, w_dt, b_dt, a_log, d_skip, w_out,
          gain_two, w_router, w_up, w_down):
    length, width = tokens.shape
    inner = w_in.shape[1] // 2
    experts = w_router.shape[1]
    groups, members = lax.axis_size("ep"), lax.axis_size("tp")
    slots = 3 * length // (2 * experts)
    capacity = 5 * length * groups * members // (4 * experts)
    rank, states, taps = w_dt.shape[0], a_log.shape[0], conv_w.shape[0]
    used = rank + 2 * states
    labels = (segment.reshape(-1, 128), route.reshape(-1, 128))
    rows = (conv_w, conv_b, b_dt, d_skip, gain_one, gain_two) + labels
    normed, both, wx, wxt, wdt, rates, vec, column, route = front(tokens, rows, w_in, w_x.T, w_dt, a_log)
    gated, *saved, proj, starts = mid_fwd(both, column, vec, wx, wdt, rates, rank)
    after, leaving, count, aux = route_out(gated, w_out, tokens, d_out, column, route, vec, w_router.T, slots)
    leaving = leaving.reshape(2, experts, slots, width)
    if members == 4:
        back, grad_up, grad_down, here = expert_visit(leaving, count, w_up, w_down, groups, members, capacity)
    else:
        back, grad_up, grad_down, prior, named = expert_steps(leaving, count, w_up, w_down, groups, members, capacity)
        this = jnp.arange(groups * members) == lax.axis_index(("ep", "tp"))
        here = jnp.stack([jnp.sum(jnp.where(this[:, None], prior, 0), axis=0), named]).astype(F32)
        here = jnp.pad(here, ((0, 6), (0, 128 - experts)))
    final, d_after, d_mixed, d_gated, g_two, g_router, counts = come_home(
        back.reshape(2, experts * slots, width), after, d_out, aux, column, route, here, vec, w_router.T, w_out, slots,
        capacity,
    )
    d_both, g_vec, g_x, g_dt, g_rates = mid_bwd(
        both, d_gated, saved, proj, starts, column, vec, wxt, wdt, rates, rank
    )
    total, d_tokens = tail_sum(
        normed, d_both, w_in, gated, d_mixed, tokens, d_after, vec, g_two, g_x, g_dt, g_rates, rates, g_vec, g_router, used,
        rank, groups, members,
    )
    total_in, total_out, total_x, total_router, total_dt, total_log, total_taps, total_bias, total_step, total_skip, *gains, up_rows, down_rows, d_tokens = (
        unpack_grads(total, (grad_up.reshape(-1, w_up.shape[2]), grad_down.reshape(-1, width), d_tokens), width, inner, used, experts, (rank, states, taps))
    )
    return (
        final,
        d_tokens,
        counts,
        gains[0],
        total_in,
        total_taps,
        total_bias,
        total_x.T,
        total_dt,
        total_step,
        total_log,
        total_skip,
        total_out,
        gains[1],
        total_router[:, :width].T,
        up_rows.reshape(w_up.shape),
        down_rows.reshape(w_down.shape),
    )


def solution(mesh):
    in_specs = (
        P(("ep", "tp"), None),
        P(("ep", "tp"), None),
        P(("ep", "tp")),
        P(("ep", "tp"), None),
        P(),
        P(),
        P(),
        P(),
        P(),
        P(),
        P(),
        P(),
        P(),
        P(),
        P(),
        P(),
        P("ep", None, "tp"),
        P("ep", "tp", None),
    )
    out_specs = (
        P(("ep", "tp"), None),
        P(("ep", "tp"), None),
        P(),
        P(),
        P(),
        P(),
        P(),
        P(),
        P(),
        P(),
        P(),
        P(),
        P(),
        P(),
        P(),
        P("ep", None, "tp"),
        P("ep", "tp", None),
    )
    return jax.shard_map(local, mesh=mesh, in_specs=in_specs, out_specs=out_specs, check_vma=False)
```
